128 devices in a mesh: angle: 8 (over y, core), tile: 16 (over z, x).
Axes of the slice: x: 4, y: 4, z: 4, core: 2. Of those that a mesh axis runs over, the one named last changes fastest.
Arguments:
- psi: float32 [2, 8, 160, 2048], P(None, 'angle', None, 'tile'), may hold values from -6 to 6
- target: float32 [2, 8, 160, 2048], P(None, 'angle', None, 'tile'), may hold values from -6 to 6
- probe: float32 [2, 128, 128], replicated, may hold values from -4.2 to 4.2
- data: float32 [8, 16, 16, 128, 128], P('angle', 'tile'), may hold values from 0.1 to 10
- pos_z: int32 [8, 16, 16], P('angle', 'tile'), may hold values from 0 to 32
- pos_x: int32 [8, 16, 16], P('angle', 'tile'), may hold values from 0 to 127
- counts: int32 [8, 16], P('angle', 'tile'), may hold values from 1 to 16, as said below
- shears: float32 [8], P('angle'), may hold values from -1 to 1
Outputs:
- psi_new: float32 [2, 8, 160, 2048], P(None, 'angle', None, 'tile')
- probe_new: float32 [2, 128, 128], replicated
- tomo_grad: bfloat16 [2, 160, 256, 2048], P(None, 'tile', 'angle')
The draws below stay inside these ranges and needn't reach their ends.
Inputs may be any that keep to these rules, and one draw needn't show every extreme that they name: counts[a, t] positions of angle a lie in tile t, in slots 0 to counts[a, t] - 1; later slots are unused. Some tile of some angle has exactly 16 in every draw.
All inputs are finite; a program needn't handle non-finite values.
Results may differ from the reference program's by a relative error of at most 0.001.
Values sent between devices are 32-bit elements; how exact they have to be, the bound alone decides.
A program may use at most 192 MiB of HBM per device.

```python
import math
import jax
import jax.numpy as jnp
from jax import lax

PS = 128
TW = 128
CAP = 16
ZWIN = 160
ITERS = 2
ANG = 8
TILES = 16
H = 2048
Y = 256
N_TILE = 16


def draw_counts(key, part):
    first_key, second_key, third_key = jax.random.split(jax.random.fold_in(key, 7103), 3)
    first = jax.random.randint(first_key, (ANG, TILES), 0, CAP)
    second = jax.random.randint(second_key, (ANG, TILES), 0, CAP)
    values = jnp.minimum(first, second) + 1
    chosen = jax.random.randint(third_key, (), 0, ANG * TILES)
    flat_index = jnp.arange(ANG * TILES, dtype=jnp.int32).reshape(ANG, TILES)
    return jnp.where(flat_index == chosen, CAP, values).astype(jnp.int32)


def plant(drawn, stream_key, smallest, high):
    extent = drawn.shape
    place = [jax.random.randint(jax.random.fold_in(stream_key, axis), (), 0, extent[axis]) for axis in range(len(extent))]
    drawn = drawn.at[tuple(place)].set(smallest)
    longest = extent.index(max(extent))
    place[longest] = (place[longest] + 1) % extent[longest]
    return drawn.at[tuple(place)].set(high)


def block_levels(key, extent, cuts, least, largest):
    def one(axis_at, blocks):
        steps = jax.random.uniform(jax.random.fold_in(jax.random.fold_in(key, 6), axis_at), (blocks,), jnp.float32, least / len(cuts), largest / len(cuts))
        return jnp.repeat(jnp.exp(steps), extent[axis_at] // blocks).reshape((-1,) + (1,) * (len(extent) - axis_at - 1))

    level = one(*cuts[0])
    for cut in cuts[1:]:
        level = level * one(*cut)
    return level


def normal_values(own_key, shape, deviation, limit, shards=(), kind=jnp.bfloat16):
    result = deviation * jax.random.normal(own_key, shape, jnp.float32)
    if shards:
        result = result * block_levels(own_key, shape, shards, -0.22, 0.18)
    return jnp.clip(result, -limit, limit).astype(kind)


def setup_inputs(seed: int = 0) -> dict:
    seeds = jax.random.split(jax.random.key(seed), 9)
    psi = normal_values(seeds[0], (2, ANG, ZWIN, H), 1.0, 6.0, ((1, 8), (3, 16)), jnp.float32)
    target = normal_values(seeds[1], (2, ANG, ZWIN, H), 1.0, 6.0, ((1, 8), (3, 16)), jnp.float32)
    probe = normal_values(seeds[2], (2, PS, PS), 0.7, 4.2, (), jnp.float32)
    data = jnp.clip(jnp.exp(math.log(10.0) - 4.6051702 * jax.random.uniform(seeds[3], (ANG, TILES, CAP, PS, PS), jnp.float32) ** block_levels(seeds[3], (ANG, TILES, CAP, PS, PS), ((0, 8), (1, 16)), -0.2, 0.2)), 0.1, 10.0)
    pos_z = plant(jax.random.randint(seeds[4], (ANG, TILES, CAP), 0, ZWIN - PS + 1), jax.random.fold_in(seeds[4], 1), 0, ZWIN - PS).astype(jnp.int32)
    pos_x = plant(jax.random.randint(seeds[5], (ANG, TILES, CAP), 0, TW), jax.random.fold_in(seeds[5], 1), 0, TW - 1).astype(jnp.int32)
    counts = draw_counts(jax.random.fold_in(seeds[8], 71), 0)
    shears = jnp.clip(jax.random.uniform(seeds[7], (ANG,), jnp.float32, -1.0, 1.0) * block_levels(seeds[7], (ANG,), ((0, 8),), -0.4, 0.0), -1.0, 1.0)
    return {"psi": psi, "target": target, "probe": probe, "data": data, "pos_z": pos_z, "pos_x": pos_x, "counts": counts, "shears": shears}


ALPHA = 0.004
RHO = 5.0
PROBE_STEP = 0.02


def reference(psi, target, probe, data, pos_z, pos_x, counts, shears):
    half = PS // 2
    slot_mask = (jnp.arange(CAP, dtype=jnp.int32)[None, None, :] < counts[:, :, None]).astype(jnp.float32)
    tile_start = (jnp.arange(N_TILE, dtype=jnp.int32) * TW)[None, :, None]
    starts_x = (pos_x + tile_start).reshape(ANG, -1).astype(jnp.int32)
    starts_z = pos_z.reshape(ANG, -1).astype(jnp.int32)
    total_count = jnp.sum(counts).astype(jnp.float32)
    data_flat = data.reshape(ANG, -1, PS, PS)
    mask_flat = slot_mask.reshape(ANG, -1)
    field = psi
    probe_now = probe
    for step in range(ITERS):
        padded = jnp.pad(field, ((0, 0), (0, 0), (0, 0), (half, half)))
        probe_cplx = lax.complex(probe_now[0], probe_now[1])

        def one_angle(items):
            plane, data_one, zs_one, xs_one, mask_one = items
            plane_cplx = lax.complex(plane[0], plane[1])

            def cut_window(start_z, start_x):
                return lax.dynamic_slice(plane_cplx, (start_z, start_x), (PS, PS))

            patches = jax.vmap(cut_window)(zs_one, xs_one)
            far = jnp.fft.fft2(probe_cplx * patches, norm="ortho")
            misfit = (jnp.real(far) ** 2 + jnp.imag(far) ** 2 - data_one) * mask_one[:, None, None]
            back = jnp.fft.ifft2(misfit * far, norm="ortho")
            grads = jnp.conj(probe_cplx) * back
            probe_part = jnp.sum(jnp.conj(patches) * back, 0)

            def add_window(total, item):
                piece, start_z, start_x = item
                current = lax.dynamic_slice(total, (start_z, start_x), (PS, PS))
                return lax.dynamic_update_slice(total, current + piece, (start_z, start_x)), None

            total, unused = lax.scan(add_window, jnp.zeros_like(plane_cplx), (grads, zs_one, xs_one))
            return (jnp.stack([jnp.real(total), jnp.imag(total)]),
                    jnp.stack([jnp.real(probe_part), jnp.imag(probe_part)]))

        grads, probe_parts = lax.map(one_angle, (jnp.moveaxis(padded, 1, 0), data_flat, starts_z, starts_x, mask_flat))
        grad_field = jnp.moveaxis(grads, 0, 1)[:, :, :, half:half + H]
        new_field = field - ALPHA * (grad_field + RHO * (field - target))
        probe_now = probe_now - PROBE_STEP * jnp.sum(probe_parts, 0) / total_count
        field = new_field
    gap = target - field
    spectrum = jnp.fft.fft(lax.complex(gap[0], gap[1]), axis=-1)
    freq = jnp.arange(H, dtype=jnp.int32)
    signed = jnp.where(freq < H // 2, freq, freq - H)
    offsets = jnp.arange(Y, dtype=jnp.int32) - Y // 2
    product = (offsets[:, None] * signed[None, :]).astype(jnp.float32)
    theta = (product[None, :, :] * shears[:, None, None]) * (2.0 * math.pi / H)
    table = lax.complex(jnp.cos(theta), jnp.sin(theta))

    def one_slice(spec_row):
        summed = jnp.sum(table * spec_row[:, None, :], 0)
        values = jnp.fft.ifft(summed, axis=-1) / ANG
        return jnp.stack([jnp.real(values), jnp.imag(values)]).astype(jnp.bfloat16)

    tomo = lax.map(one_slice, jnp.moveaxis(spectrum, 1, 0))
    return field, probe_now, jnp.moveaxis(tomo, 0, 1)
```

```python
import functools
import math

import jax
import jax.numpy as jnp
import numpy as np
from jax import lax
from jax.experimental import pallas as pl
from jax.experimental.pallas import tpu as pltpu
from jax.sharding import PartitionSpec as P

ITERS = 2
ALPHA = 0.004
RHO = 5.0
PROBE_STEP = 0.02

ANG = 8
TILES = 16
PS = 128
TW = 128
ROWS = 160
CAP = 16
HALF = 64
WIDE = 256
ZS = ROWS // TILES
YB = 32
H = 2048
CHUNK = 2 * PS // ANG
CROWS = CHUNK + 8

F32 = jnp.float32
BF16 = jnp.bfloat16
MESH = pl.DeviceIdType.MESH
VMEM = pl.BlockSpec(memory_space=pltpu.VMEM)
SMEM = pl.BlockSpec(memory_space=pltpu.SMEM)
VLIMIT = 60 * 1024 * 1024


def dft_block(length, scale):
    index = np.arange(length)
    turns = (index[:, None] * index[None, :]) % length
    angle = -2.0 * math.pi * turns / length
    real, imag = np.cos(angle) * scale, np.sin(angle) * scale
    return np.block([[real, imag], [-imag, real]])


def split_const(matrix):
    high = matrix.astype(BF16)
    low = (matrix - high.astype(np.float64)).astype(BF16)
    return high, low


def right_table(matrix):
    high, low = split_const(matrix)
    return np.concatenate([high, high, low], axis=0)


def left_table(matrix):
    high, low = split_const(matrix)
    return np.concatenate([high, high, low], axis=1)


def turn_table(orient):
    angle = orient * 2.0 * math.pi * np.arange(TILES)[:, None] * np.arange(TW)[None, :] / H
    return np.stack([np.cos(angle), np.sin(angle)]).astype(np.float32)


def split(value):
    high = value.astype(BF16)
    low = (value - high.astype(F32)).astype(BF16)
    return high, low


def dot_right(value, table):
    high, low = split(value)
    return jnp.dot(jnp.concatenate([high, low, high], axis=1), table, preferred_element_type=F32)


def dot_left(table, value):
    high, low = split(value)
    return jnp.dot(table, jnp.concatenate([high, low, high], axis=0), preferred_element_type=F32)


def times(left, right):
    return left[0] * right[0] - left[1] * right[1], left[0] * right[1] + left[1] * right[0]


def four(items, orient):
    (ar, ai), (br, bi), (cr, ci), (dr, di) = items
    sr, si, ur, ui = ar + cr, ai + ci, ar - cr, ai - ci
    pr, pi, qr, qi = br + dr, bi + di, br - dr, bi - di
    first = (sr + pr, si + pi)
    third = (sr - pr, si - pi)
    plus = (ur - qi, ui + qr)
    minus = (ur + qi, ui - qr)
    return [first, plus, third, minus] if orient > 0 else [first, minus, third, plus]


def sixteen(items, orient):
    columns = []
    for fine in range(4):
        partial = four([items[4 * coarse + fine] for coarse in range(4)], orient)
        for order in range(1, 4):
            step = fine * order
            if step:
                angle = orient * 2.0 * math.pi * step / 16
                partial[order] = times(partial[order], (math.cos(angle), math.sin(angle)))
        columns.append(partial)
    result = [None] * 16
    for low in range(4):
        finished = four([columns[fine][low] for fine in range(4)], orient)
        for high in range(4):
            result[low + 4 * high] = finished[high]
    return result


def lanes(shape):
    return lax.broadcasted_iota(jnp.int32, shape, len(shape) - 1)


def sublanes(shape):
    return lax.broadcasted_iota(jnp.int32, shape, len(shape) - 2)


def place():
    return lax.axis_index("angle"), lax.axis_index("tile")


def meet(peers):
    barrier = pltpu.get_barrier_semaphore()
    for peer in peers:
        pl.semaphore_signal(barrier, inc=1, device_id=peer, device_id_type=MESH)
    pl.semaphore_wait(barrier, len(peers))


def send(source, target, sems, slot, peer):
    copy = pltpu.make_async_remote_copy(
        src_ref=source,
        dst_ref=target,
        send_sem=sems.at[0, slot],
        recv_sem=sems.at[1, slot],
        device_id=peer,
        device_id_type=MESH,
    )
    copy.start()
    return copy


def angle_peers(angle, tile):
    return [((angle + step) % ANG, tile) for step in range(1, ANG)]


def tile_peers(angle, tile):
    return [(angle, (tile + step) % TILES) for step in range(1, TILES)]


def neighbours(angle, tile):
    return (angle, (tile + TILES - 1) % TILES), (angle, (tile + 1) % TILES)


def halo_kernel(psi, target, from_left, from_right, pack_left, pack_right, sems):
    angle, tile = place()
    left, right = neighbours(angle, tile)
    low = lanes((ROWS, TW)) < HALF
    for index, source in enumerate((psi, target)):
        real, imag = source[0], source[1]
        pack_left[index] = jnp.where(low, real, pltpu.roll(imag, HALF, 1))
        pack_right[index] = jnp.where(low, pltpu.roll(real, HALF, 1), imag)
    meet([left, right])
    copies = []
    copies.append(send(pack_left, from_right, sems, 0, left))
    copies.append(send(pack_right, from_left, sems, 1, right))
    for copy in copies:
        copy.wait()


def start_edges(grad, from_left, from_right, sems, angle, tile):
    left, right = neighbours(angle, tile)
    return [
        send(grad.at[0], from_right, sems, 0, left),
        send(grad.at[1], from_left, sems, 1, right),
    ]


def start_first(parts, landed, sems, angle, tile):
    return [
        send(parts.at[(angle + step) % ANG], landed.at[step], sems, step, ((angle + step) % ANG, tile))
        for step in range(1, ANG)
    ]


def finish_first(copies, parts, landed, angle):
    for copy in copies:
        copy.wait()
    total = parts[angle]
    for step in range(1, ANG):
        total = total + landed[step]
    return total


def start_second(source, landed, sems, angle, tile):
    return [
        send(source, landed.at[tile], sems, step, (angle, (tile + step) % TILES))
        for step in range(1, TILES)
    ]


def finish_second(copies, source, landed, tile):
    landed[tile] = source[...]
    for copy in copies:
        copy.wait()
    total = landed[0]
    for index in range(1, TILES):
        total = total + landed[index]
    return total


def start_third(source, gathered, sems, angle, tile):
    return [
        send(source, gathered.at[angle], sems, step, ((angle + step) % ANG, tile))
        for step in range(1, ANG)
    ]


def exchange_kernel(
    grad, parts, from_left, from_right, first_out, gathered,
    landed_first, first_sum, landed_second, second_sum, edge_sems, first_sems, second_sems, third_sems,
):
    angle, tile = place()
    meet(angle_peers(angle, tile) + tile_peers(angle, tile))
    first = start_first(parts, landed_first, first_sems, angle, tile)
    edges = start_edges(grad, from_left, from_right, edge_sems, angle, tile)
    first_sum[...] = finish_first(first, parts, landed_first, angle)
    second = start_second(first_sum, landed_second, second_sems, angle, tile)
    first_out[...] = first_sum[pl.ds(CHUNK, 8), :]
    second_sum[...] = finish_second(second, first_sum, landed_second, tile)
    third = start_third(second_sum, gathered, third_sems, angle, tile)
    gathered[angle] = second_sum[...]
    for copy in third + edges:
        copy.wait()


def rims_kernel(grad, parts, from_left, from_right, first_out, landed_first, edge_sems, first_sems):
    angle, tile = place()
    meet(angle_peers(angle, tile) + list(neighbours(angle, tile)))
    edges = start_edges(grad, from_left, from_right, edge_sems, angle, tile)
    first = start_first(parts, landed_first, first_sems, angle, tile)
    first_out[...] = finish_first(first, parts, landed_first, angle)
    for copy in edges:
        copy.wait()


def slabs_kernel(slabs, first_sum, gathered, second_out, landed_second, slab_sems, second_sems):
    angle, tile = place()
    meet(tile_peers(angle, tile))
    copies = []
    for step in range(1, TILES):
        owner = (tile + step) % TILES
        copies.append(send(slabs.at[owner], gathered.at[tile], slab_sems, step, (angle, owner)))
    second = start_second(first_sum, landed_second, second_sems, angle, tile)
    gathered[tile] = slabs[tile]
    second_out[...] = finish_second(second, first_sum, landed_second, tile)
    for copy in copies:
        copy.wait()


def rows_kernel(rows, second_sum, every, gathered, sems, third_sems):
    angle, tile = place()
    chip, core = angle // 2, angle % 2
    up, down, over = (chip + 1) % 4, (chip + 3) % 4, (chip + 2) % 4
    upper, lower, across = 2 * up + core, 2 * down + core, 2 * over + core
    sibling = 2 * chip + 1 - core
    meet(angle_peers(angle, tile))
    to_up = send(rows, every.at[angle], sems, 0, (upper, tile))
    to_down = send(rows, every.at[angle], sems, 1, (lower, tile))
    to_side = send(rows, every.at[angle], sems, 2, (sibling, tile))
    third = start_third(second_sum, gathered, third_sems, angle, tile)
    gathered[angle] = second_sum[...]
    every[angle] = rows[...]
    first_half, last_half = pl.ds(0, ZS // 2), pl.ds(ZS // 2, ZS // 2)
    to_up.wait_recv()
    on_up = send(every.at[lower, first_half], every.at[lower, first_half], sems, 3, (upper, tile))
    side_low = send(every.at[lower], every.at[lower], sems, 4, (sibling, tile))
    to_down.wait_recv()
    on_down = send(every.at[upper, last_half], every.at[upper, last_half], sems, 5, (lower, tile))
    side_up = send(every.at[upper], every.at[upper], sems, 6, (sibling, tile))
    on_up.wait_recv()
    side_first = send(every.at[across, first_half], every.at[across, first_half], sems, 7, (sibling, tile))
    on_down.wait_recv()
    side_last = send(every.at[across, last_half], every.at[across, last_half], sems, 8, (sibling, tile))
    for copy in (to_side, side_low, side_up, side_first, side_last):
        copy.wait()
    for copy in (to_up, to_down, on_up, on_down):
        copy.wait_send()
    for copy in third:
        copy.wait()


def gradients(counts, pos_z, pos_x, ext, probe, data, right_f, left_f, left_b, right_b, grad, parts, probe_acc):
    count = counts[0, 0]
    grad[...] = jnp.zeros_like(grad)
    probe_acc[...] = jnp.zeros_like(probe_acc)

    def pair(index, carry):
        probe_real, probe_imag = probe[0], probe[1]
        rows, windows, spots = [], [], []
        for offset in range(2):
            slot = 2 * index + offset
            start_z, start_x = pos_z[0, 0, slot], pos_x[0, 0, slot]
            back = lax.rem(WIDE - start_x, WIDE)
            here = pl.ds(start_z, PS)
            real, imag = (
                pltpu.roll(jnp.concatenate([ext[0, part, here, :], ext[1, part, here, :]], axis=1), back, 1)[:, :PS]
                for part in range(2)
            )
            windows.append((real, imag))
            spots.append((slot, start_z, start_x))
            wave = times((probe_real, probe_imag), (real, imag))
            rows.append(jnp.concatenate(wave, axis=1))
        half_way = dot_right(jnp.concatenate(rows, axis=0), right_f[...])
        stacked = jnp.concatenate(
            [
                jnp.concatenate([half_way[s * PS : (s + 1) * PS, :PS], half_way[s * PS : (s + 1) * PS, PS:]], axis=0)
                for s in range(2)
            ],
            axis=1,
        )
        far = dot_left(left_f[...], stacked)
        weighted = []
        for s in range(2):
            slot = spots[s][0]
            far_real, far_imag = far[:PS, s * PS : (s + 1) * PS], far[PS:, s * PS : (s + 1) * PS]
            live = jnp.where(slot < count, 1.0, 0.0).astype(F32)
            misfit = (far_real * far_real + far_imag * far_imag - data[slot]) * live
            weighted.append(jnp.concatenate([misfit * far_real, misfit * far_imag], axis=0))
        half_back = dot_left(left_b[...], jnp.concatenate(weighted, axis=1))
        stacked = jnp.concatenate(
            [
                jnp.concatenate([half_back[:PS, s * PS : (s + 1) * PS], half_back[PS:, s * PS : (s + 1) * PS]], axis=1)
                for s in range(2)
            ],
            axis=0,
        )
        chi = dot_right(stacked, right_b[...])
        zeros = jnp.zeros((PS, PS), F32)
        for s in range(2):
            slot, start_z, start_x = spots[s]
            chi_real, chi_imag = chi[s * PS : (s + 1) * PS, :PS], chi[s * PS : (s + 1) * PS, PS:]
            real, imag = windows[s]
            probe_acc[pl.ds(0, PS), :] += real * chi_real + imag * chi_imag
            probe_acc[pl.ds(PS, PS), :] += real * chi_imag - imag * chi_real
            grad_real = probe_real * chi_real + probe_imag * chi_imag
            grad_imag = probe_real * chi_imag - probe_imag * chi_real
            for part, value in ((0, grad_real), (1, grad_imag)):
                moved = pltpu.roll(jnp.concatenate([value, zeros], axis=1), start_x, 1)
                here = pl.ds(start_z, PS)
                grad[0, part, here, :] += moved[:, :TW]
                grad[1, part, here, :] += moved[:, TW:]
        return carry

    lax.fori_loop(0, (count + 1) // 2, pair, 0)
    for chunk in range(ANG):
        parts[chunk, pl.ds(0, CHUNK), :] = probe_acc[pl.ds(chunk * CHUNK, CHUNK), :]


def scalars_rows(counts, shears):
    angle = lax.axis_index("angle")
    row, lane = sublanes((8, TW)), lanes((8, TW))
    count = jnp.where((row == 0) & (lane == 0), counts[0, 0].astype(F32), 0.0)
    return jnp.where((row == 1) & (lane == angle), shears[0], count)


def first_kernel(
    counts, pos_z, pos_x, shears, psi, target, from_left, from_right, probe, data,
    right_f, left_f, left_b, right_b, ext, ext_target, grad, parts, probe_acc,
):
    tile = lax.axis_index("tile")
    low = lanes((ROWS, TW)) < HALF
    for index, (own, wide) in enumerate(((psi, ext), (target, ext_target))):
        before = jnp.where(tile > 0, from_left[index], 0.0)
        after = jnp.where(tile < TILES - 1, from_right[index], 0.0)
        real, imag = pltpu.roll(own[0], HALF, 1), pltpu.roll(own[1], HALF, 1)
        wide[0, 0] = jnp.where(low, before, real)
        wide[0, 1] = jnp.where(low, pltpu.roll(before, HALF, 1), imag)
        wide[1, 0] = jnp.where(low, real, pltpu.roll(after, HALF, 1))
        wide[1, 1] = jnp.where(low, imag, after)
    extra = scalars_rows(counts, shears)
    for chunk in range(ANG):
        parts[chunk, pl.ds(CHUNK, 8), :] = extra
    gradients(counts, pos_z, pos_x, ext, probe, data, right_f, left_f, left_b, right_b, grad, parts, probe_acc)


def second_kernel(
    counts, pos_z, pos_x, ext0, ext_target, grad0, from_left, from_right, probe0, gathered, data,
    right_f, left_f, left_b, right_b, ext, grad, parts, probe, probe_acc,
):
    tile = lax.axis_index("tile")
    low = lanes((ROWS, TW)) < HALF
    inner, outer = tile > 0, tile < TILES - 1
    for part in range(2):
        for side, landed, inside in ((0, from_left, inner), (1, from_right, outer)):
            total = grad0[side, part] + jnp.where(inside, landed[part], 0.0)
            old = ext0[side, part]
            new = old - ALPHA * (total + RHO * (old - ext_target[side, part]))
            keep = jnp.logical_or(inside, jnp.logical_not(low) if side == 0 else low)
            ext[side, part] = jnp.where(keep, new, 0.0)
    number = gathered[0, pl.ds(CHUNK, 1), pl.ds(0, 1)]
    for chunk in range(ANG):
        part, start = divmod(chunk * CHUNK, PS)
        step = PROBE_STEP * gathered[chunk, pl.ds(0, CHUNK), :] / number
        probe[part, pl.ds(start, CHUNK), :] = probe0[part, pl.ds(start, CHUNK), :] - step
        parts[chunk, pl.ds(CHUNK, 8), :] = gathered[chunk, pl.ds(CHUNK, 8), :]
    gradients(counts, pos_z, pos_x, ext, probe, data, right_f, left_f, left_b, right_b, grad, parts, probe_acc)


def update_kernel(ext, target, grad, from_left, from_right, psi_new, slabs):
    tile = lax.axis_index("tile")
    low = lanes((ROWS, TW)) < HALF
    for part in range(2):
        before = jnp.where(tile > 0, from_left[part], 0.0)
        after = jnp.where(tile < TILES - 1, from_right[part], 0.0)
        left = grad[0, part] + before
        right = grad[1, part] + after
        old = jnp.where(low, pltpu.roll(ext[0, part], HALF, 1), pltpu.roll(ext[1, part], HALF, 1))
        total = jnp.where(low, pltpu.roll(left, HALF, 1), pltpu.roll(right, HALF, 1))
        goal = target[part]
        new = old - ALPHA * (total + RHO * (old - goal))
        psi_new[part] = new
        gap = goal - new
        for slab in range(TILES):
            slabs[slab, part] = gap[slab * ZS : (slab + 1) * ZS]


def spectrum_kernel(slabs, turns, right_f, rows, work):
    items = [(slabs[tile, 0], slabs[tile, 1]) for tile in range(TILES)]
    work[...] = jnp.zeros_like(work)
    for order, item in enumerate(sixteen(items, -1)):
        turn = (turns[0, pl.ds(order, 1), :], turns[1, pl.ds(order, 1), :])
        real, imag = times(item, turn)
        work[pl.ds(16 * order, ZS), pl.ds(0, TW)] = real
        work[pl.ds(16 * order, ZS), pl.ds(TW, TW)] = imag
    result = dot_right(work[...], right_f[...])
    for order in range(TILES):
        rows[:, order, :] = result[16 * order : 16 * order + ZS]


def flip8(value):
    row = sublanes(value.shape)
    value = pltpu.roll(value, 4, 0)
    value = jnp.where((row & 2) == 0, pltpu.roll(value, 6, 0), pltpu.roll(value, 2, 0))
    return jnp.where((row & 1) == 0, pltpu.roll(value, 7, 0), pltpu.roll(value, 1, 0))


def image_kernel(
    rows, shear_rows, turns, right_b, probe0, gathered, counted, image, probe_new,
    bases, cosines, sines, turned, spread, middle,
):
    @pl.when(pl.program_id(0) == 0)
    def _():
        number = counted[0, pl.ds(CHUNK, 1), pl.ds(0, 1)]
        for chunk in range(ANG):
            part, start = divmod(chunk * CHUNK, PS)
            step = PROBE_STEP * gathered[chunk, pl.ds(0, CHUNK), :] / number
            probe_new[part, pl.ds(start, CHUNK), :] = probe0[part, pl.ds(start, CHUNK), :] - step
        frequency = sublanes((TILES, TW)) + TILES * lanes((TILES, TW))
        signed = jnp.where(frequency < H // 2, frequency, frequency - H).astype(F32)
        centre = (YB * lax.axis_index("angle") - ANG * YB // 2).astype(F32) + (YB - 1) / 2.0
        row = sublanes((8, TW))

        for angle in range(ANG):
            turn = signed * (1.0 / H) * shear_rows[pl.ds(1, 1), pl.ds(angle, 1)]
            whole = centre * turn
            whole = 2.0 * math.pi * (whole - jnp.round(whole))
            half = math.pi * turn
            bases[angle, 0], bases[angle, 1] = jnp.cos(whole), jnp.sin(whole)
            power = (jnp.cos(half), jnp.sin(half))
            for level in range(5):
                bases[angle, 2 + 2 * level], bases[angle, 3 + 2 * level] = power
                power = times(power, power)

        def fill(angle, carry):
            for order in range(TILES):
                line = [
                    tuple(
                        jnp.broadcast_to(bases[angle, 2 + 2 * level + part, pl.ds(order, 1), :], (8, TW))
                        for part in range(2)
                    )
                    for level in range(5)
                ]
                now = line[0]
                for level in range(3):
                    ahead = times(now, line[1 + level])
                    chosen = (row & (1 << level)) != 0
                    now = tuple(jnp.where(chosen, new, old) for new, old in zip(ahead, now))
                later = times(now, line[4])
                cosines[angle, order, pl.ds(0, 8), :], sines[angle, order, pl.ds(0, 8), :] = now
                cosines[angle, order, pl.ds(8, 8), :], sines[angle, order, pl.ds(8, 8), :] = later
            return carry

        lax.fori_loop(0, ANG, fill, 0)

    for angle in range(ANG):
        value = (rows[angle, 0, :, pl.ds(0, TW)], rows[angle, 0, :, pl.ds(TW, TW)])
        turned[angle, 0], turned[angle, 1] = times(value, (bases[angle, 0], bases[angle, 1]))

    for order in range(TILES):
        sums = None
        for angle in range(ANG):
            real = jnp.broadcast_to(turned[angle, 0, pl.ds(order, 1), :], (16, TW))
            imag = jnp.broadcast_to(turned[angle, 1, pl.ds(order, 1), :], (16, TW))
            cosine, sine = cosines[angle, order], sines[angle, order]
            terms = (real * cosine, imag * sine, real * sine, imag * cosine)
            sums = terms if sums is None else tuple(s + t for s, t in zip(sums, terms))
        rc, isn, rs, ic = sums
        above = (rc - isn, rs + ic)
        below = (rc + isn, ic - rs)
        for part in range(2):
            back = jnp.concatenate([flip8(below[part][8:]), flip8(below[part][:8])], axis=0)
            value = jnp.concatenate([back, above[part]], axis=0)
            high, low = split(value)
            here = pl.ds(order * YB, YB)
            spread[here, pl.ds(part * TW, TW)] = high
            spread[here, pl.ds((2 + part) * TW, TW)] = low
            spread[here, pl.ds((4 + part) * TW, TW)] = high

    middle[...] = jnp.dot(spread[...], right_b[...], preferred_element_type=F32)

    def finish(group, carry):
        items = []
        for order in range(TILES):
            here = pl.ds(pl.multiple_of(order * YB + 16 * group, 16), 16)
            value = (middle[here, pl.ds(0, TW)], middle[here, pl.ds(TW, TW)])
            turn = (turns[0, pl.ds(order, 1), :], turns[1, pl.ds(order, 1), :])
            items.append(times(value, turn))
        for tile, item in enumerate(sixteen(items, 1)):
            for part in range(2):
                image[part, 0, pl.ds(pl.multiple_of(16 * group, 16), 16), pl.ds(tile * TW, TW)] = item[part].astype(BF16)
        return carry

    lax.fori_loop(0, YB // 16, finish, 0)


def arr(*shape):
    return jax.ShapeDtypeStruct(shape, F32)


def dma(*shape):
    return pltpu.SemaphoreType.DMA(shape)


def remote(kernel, outs, scratch, ident):
    return pl.pallas_call(
        kernel,
        out_shape=outs,
        in_specs=[VMEM, VMEM],
        out_specs=[VMEM] * len(outs),
        scratch_shapes=scratch,
        compiler_params=pltpu.CompilerParams(collective_id=ident, has_side_effects=True, vmem_limit_bytes=VLIMIT),
    )


def local(kernel, outs, specs, scratch):
    return pl.pallas_call(
        kernel,
        out_shape=outs,
        in_specs=specs,
        out_specs=[VMEM] * len(outs),
        scratch_shapes=scratch,
        compiler_params=pltpu.CompilerParams(vmem_limit_bytes=VLIMIT),
    )


def image_call(rows, shear_rows, turns, table, probe, gathered, counted):
    full = lambda *shape: pl.BlockSpec(shape, lambda z: (0,) * len(shape))
    return pl.pallas_call(
        image_kernel,
        grid=(ZS,),
        out_shape=[jax.ShapeDtypeStruct((2, ZS, YB, H), BF16), arr(2, PS, PS)],
        in_specs=[
            pl.BlockSpec((ANG, 1, TILES, WIDE), lambda z: (0, z, 0, 0)),
            full(8, TW),
            full(2, TILES, TW),
            full(3 * WIDE, WIDE),
            full(2, PS, PS),
            full(ANG, CROWS, TW),
            full(ANG, CROWS, TW),
        ],
        out_specs=[pl.BlockSpec((2, 1, YB, H), lambda z: (0, z, 0, 0)), full(2, PS, PS)],
        scratch_shapes=[
            pltpu.VMEM((ANG, 12, TILES, TW), F32),
            pltpu.VMEM((ANG, TILES, 16, TW), F32),
            pltpu.VMEM((ANG, TILES, 16, TW), F32),
            pltpu.VMEM((ANG, 2, TILES, TW), F32),
            pltpu.VMEM((TILES * YB, 3 * WIDE), BF16),
            pltpu.VMEM((TILES * YB, WIDE), F32),
        ],
        compiler_params=pltpu.CompilerParams(vmem_limit_bytes=VLIMIT),
    )(rows, shear_rows, turns, table, probe, gathered, counted)


def shards(psi, target, probe, data, pos_z, pos_x, counts, shears):
    psi, target = psi.reshape(2, ROWS, TW), target.reshape(2, ROWS, TW)
    data = data.reshape(CAP, PS, PS)
    unit = dft_block(PS, 1.0 / math.sqrt(PS))
    tables = [
        jnp.asarray(t)
        for t in (right_table(unit), left_table(unit.T), left_table(unit), right_table(unit.T))
    ]
    wide, edge = arr(2, 2, ROWS, TW), arr(2, ROWS, TW)
    small, chunks = arr(8, TW), arr(ANG, CROWS, TW)
    one = lambda *shape: pltpu.VMEM(shape, F32)
    accumulate = [one(2 * PS, PS)]

    from_left, from_right = remote(
        halo_kernel, [edge, edge], [one(2, ROWS, TW), one(2, ROWS, TW), dma(2, 2)], 0
    )(psi, target)
    ext, ext_target, grad, parts = local(
        first_kernel, [wide, wide, wide, chunks], [SMEM] * 4 + [VMEM] * 10, accumulate
    )(counts, pos_z, pos_x, shears, psi, target, from_left, from_right, probe, data, *tables)
    from_left, from_right, shear_rows, counted = remote(
        exchange_kernel,
        [edge, edge, small, chunks],
        [
            one(ANG, CROWS, TW), one(CROWS, TW), one(TILES, CROWS, TW), one(CROWS, TW),
            dma(2, 2), dma(2, ANG), dma(2, TILES), dma(2, ANG),
        ],
        1,
    )(grad, parts)
    ext, grad, parts, probe = local(
        second_kernel, [wide, wide, chunks, arr(2, PS, PS)], [SMEM] * 3 + [VMEM] * 12, accumulate
    )(counts, pos_z, pos_x, ext, ext_target, grad, from_left, from_right, probe, counted, data, *tables)
    from_left, from_right, first_sum = remote(
        rims_kernel,
        [edge, edge, arr(CROWS, TW)],
        [one(ANG, CROWS, TW), dma(2, 2), dma(2, ANG)],
        2,
    )(grad, parts)
    psi_new, slabs = local(update_kernel, [edge, arr(TILES, 2, ZS, TW)], [VMEM] * 5, [])(
        ext, target, grad, from_left, from_right
    )
    slabs, second_sum = remote(
        slabs_kernel,
        [arr(TILES, 2, ZS, TW), arr(CROWS, TW)],
        [one(TILES, CROWS, TW), dma(2, TILES), dma(2, TILES)],
        3,
    )(slabs, first_sum)
    (rows,) = local(spectrum_kernel, [arr(ZS, TILES, WIDE)], [VMEM] * 3, [one(WIDE, WIDE)])(
        slabs, jnp.asarray(turn_table(-1)), jnp.asarray(right_table(dft_block(TW, 1.0)))
    )
    every, gathered = remote(
        rows_kernel, [arr(ANG, ZS, TILES, WIDE), chunks], [dma(2, 9), dma(2, ANG)], 4
    )(rows, second_sum)
    inverse = dft_block(TW, 1.0 / (H * ANG)).T
    image, probe_new = image_call(
        every, shear_rows, jnp.asarray(turn_table(1)), jnp.asarray(right_table(inverse)), probe, gathered, counted
    )
    return psi_new.reshape(2, 1, ROWS, TW), probe_new, image


def solution(mesh):
    in_specs = (
        P(None, "angle", None, "tile"),
        P(None, "angle", None, "tile"),
        P(),
        P("angle", "tile", None, None, None),
        P("angle", "tile", None),
        P("angle", "tile", None),
        P("angle", "tile"),
        P("angle"),
    )
    out_specs = (P(None, "angle", None, "tile"), P(), P(None, "tile", "angle", None))
    return jax.shard_map(shards, mesh=mesh, in_specs=in_specs, out_specs=out_specs, check_vma=False)
```

```python
import functools
import math

import jax
import jax.numpy as jnp
import numpy as np
from jax import lax
from jax.experimental import pallas as pl
from jax.experimental.pallas import tpu as pltpu
from jax.sharding import PartitionSpec as P

ITERS = 2
ALPHA = 0.004
RHO = 5.0
PROBE_STEP = 0.02

ANG = 8
TILES = 16
PS = 128
TW = 128
ROWS = 160
CAP = 16
HALF = 64
WIDE = 256
ZS = ROWS // TILES
YB = 32
H = 2048
CHUNK = 2 * PS // ANG
GROUP = 4

F32 = jnp.float32
BF16 = jnp.bfloat16
MESH = pl.DeviceIdType.MESH
VMEM = pl.BlockSpec(memory_space=pltpu.VMEM)
SMEM = pl.BlockSpec(memory_space=pltpu.SMEM)
HBM = pl.BlockSpec(memory_space=pltpu.HBM)
VLIMIT = 20 * 1024 * 1024


def dft_block(length, scale):
    index = np.arange(length)
    turns = (index[:, None] * index[None, :]) % length
    angle = -2.0 * math.pi * turns / length
    real, imag = np.cos(angle) * scale, np.sin(angle) * scale
    return np.block([[real, imag], [-imag, real]])


def split_const(matrix):
    high = matrix.astype(BF16)
    low = (matrix - high.astype(np.float64)).astype(BF16)
    return high, low


def right_table(matrix):
    high, low = split_const(matrix)
    return np.concatenate([high, high, low], axis=0)


def left_table(matrix):
    high, low = split_const(matrix)
    return np.concatenate([high, high, low], axis=1)


def turn_table(orient):
    angle = orient * 2.0 * math.pi * np.arange(TILES)[:, None] * np.arange(TW)[None, :] / H
    return np.stack([np.cos(angle), np.sin(angle)]).astype(np.float32)


def split(value):
    high = value.astype(BF16)
    low = (value - high.astype(F32)).astype(BF16)
    return high, low


def dot_right(value, table):
    high, low = split(value)
    return jnp.dot(jnp.concatenate([high, low, high], axis=1), table, preferred_element_type=F32)


def dot_left(table, value):
    high, low = split(value)
    return jnp.dot(table, jnp.concatenate([high, low, high], axis=0), preferred_element_type=F32)


def times(left, right):
    return left[0] * right[0] - left[1] * right[1], left[0] * right[1] + left[1] * right[0]


def four(items, orient):
    (ar, ai), (br, bi), (cr, ci), (dr, di) = items
    sr, si, ur, ui = ar + cr, ai + ci, ar - cr, ai - ci
    pr, pi, qr, qi = br + dr, bi + di, br - dr, bi - di
    first = (sr + pr, si + pi)
    third = (sr - pr, si - pi)
    plus = (ur - qi, ui + qr)
    minus = (ur + qi, ui - qr)
    return [first, plus, third, minus] if orient > 0 else [first, minus, third, plus]


def sixteen(items, orient):
    columns = []
    for fine in range(4):
        partial = four([items[4 * coarse + fine] for coarse in range(4)], orient)
        for order in range(1, 4):
            step = fine * order
            if step:
                angle = orient * 2.0 * math.pi * step / 16
                partial[order] = times(partial[order], (math.cos(angle), math.sin(angle)))
        columns.append(partial)
    result = [None] * 16
    for low in range(4):
        finished = four([columns[fine][low] for fine in range(4)], orient)
        for high in range(4):
            result[low + 4 * high] = finished[high]
    return result


def lanes(shape):
    return lax.broadcasted_iota(jnp.int32, shape, len(shape) - 1)


def sublanes(shape):
    return lax.broadcasted_iota(jnp.int32, shape, len(shape) - 2)


def place():
    return lax.axis_index("angle"), lax.axis_index("tile")


def meet(peers):
    barrier = pltpu.get_barrier_semaphore()
    for peer in peers:
        pl.semaphore_signal(barrier, inc=1, device_id=peer, device_id_type=MESH)
    pl.semaphore_wait(barrier, len(peers))


def send(source, target, sems, slot, peer):
    copy = pltpu.make_async_remote_copy(
        src_ref=source,
        dst_ref=target,
        send_sem=sems.at[0, slot],
        recv_sem=sems.at[1, slot],
        device_id=peer,
        device_id_type=MESH,
    )
    copy.start()
    return copy


def angle_peers(angle, tile):
    return [((angle + step) % ANG, tile) for step in range(1, ANG)]


def tile_peers(angle, tile):
    return [(angle, (tile + step) % TILES) for step in range(1, TILES)]


def neighbours(angle, tile):
    return (angle, (tile + TILES - 1) % TILES), (angle, (tile + 1) % TILES)


def start_edges(packs, from_left, from_right, sems, angle, tile):
    left, right = neighbours(angle, tile)
    return [
        send(packs.at[0], from_right, sems, 0, left),
        send(packs.at[1], from_left, sems, 1, right),
    ]


def start_first(parts, landed, sems, angle, tile):
    return [
        send(parts.at[(angle + step) % ANG], landed.at[step], sems, step, ((angle + step) % ANG, tile))
        for step in range(1, ANG)
    ]


def finish_first(copies, parts, landed, angle):
    for copy in copies:
        copy.wait()
    total = parts[angle]
    for step in range(1, ANG):
        total = total + landed[step]
    return total


def start_second(source, landed, sems, angle, tile):
    return [
        send(source, landed.at[tile], sems, step, (angle, (tile + step) % TILES))
        for step in range(1, TILES)
    ]


def finish_second(copies, source, landed, tile):
    landed[tile] = source[...]
    for copy in copies:
        copy.wait()
    total = landed[0]
    for index in range(1, TILES):
        total = total + landed[index]
    return total


def start_third(source, gathered, sems, angle, tile):
    return [
        send(source, gathered.at[angle], sems, step, ((angle + step) % ANG, tile))
        for step in range(1, ANG)
    ]


def packed_sides(real, imag):
    low = lanes((ROWS, TW)) < HALF
    return (
        jnp.where(low, real, pltpu.roll(imag, HALF, 1)),
        jnp.where(low, pltpu.roll(real, HALF, 1), imag),
    )


def widened(real, imag, before, after, tile):
    low = lanes((ROWS, TW)) < HALF
    before = jnp.where(tile > 0, before, 0.0)
    after = jnp.where(tile < TILES - 1, after, 0.0)
    real, imag = pltpu.roll(real, HALF, 1), pltpu.roll(imag, HALF, 1)
    return (
        (jnp.where(low, before, real), jnp.where(low, pltpu.roll(before, HALF, 1), imag)),
        (jnp.where(low, real, pltpu.roll(after, HALF, 1)), jnp.where(low, imag, after)),
    )


def halo_kernel(
    counts, shears, psi, target, probe, data, *refs,
):
    tables, refs = refs[:4], refs[4:]
    ext, own_target, packs, info, probe_here, data_here, *refs = refs
    tables_here, refs = refs[:4], refs[4:]
    own, sides, from_left, from_right, block, landed, edge_sems, info_sems, local_sems = refs
    angle, tile = place()
    fetches = [
        pltpu.make_async_copy(source, here, local_sems.at[index])
        for index, (source, here) in enumerate(
            zip((psi, target, probe, data) + tables, (own, own_target, probe_here, data_here) + tuple(tables_here))
        )
    ]
    for fetch in fetches:
        fetch.start()
    row, lane = sublanes((8, TW)), lanes((8, TW))
    count = jnp.where((row == 0) & (lane == 0), counts[0, 0].astype(F32), 0.0)
    block[...] = jnp.where((row == 1) & (lane == angle), shears[0], count)
    fetches[0].wait()
    for side, value in enumerate(packed_sides(own[0], own[1])):
        sides[side] = value
    meet(angle_peers(angle, tile) + list(neighbours(angle, tile)))
    edges = start_edges(sides, from_left, from_right, edge_sems, angle, tile)
    infos = [
        send(block, landed.at[step], info_sems, step, ((angle + step) % ANG, tile)) for step in range(1, ANG)
    ]
    fetches[1].wait()
    for side, value in enumerate(packed_sides(own_target[0], own_target[1])):
        packs[side] = value
    for fetch in fetches[2:]:
        fetch.wait()
    for copy in edges:
        copy.wait()
    for side, pair in enumerate(widened(own[0], own[1], from_left[...], from_right[...], tile)):
        for part in range(2):
            ext[side, part] = pair[part]
    for copy in infos:
        copy.wait()
    total = block[...]
    for step in range(1, ANG):
        total = total + landed[step]
    info[...] = total


def exchange_kernel(
    grad, parts, packs, info, ext0, own_target, probe0, ext, probe, info_all,
    from_left, from_right, goal_left, goal_right, landed_first, first_sum, landed_second, second_sum, gathered, landed_info,
    edge_sems, goal_sems, first_sems, second_sems, third_sems, info_sems,
):
    angle, tile = place()
    meet(angle_peers(angle, tile) + tile_peers(angle, tile))
    first = start_first(parts, landed_first, first_sems, angle, tile)
    edges = start_edges(grad, from_left, from_right, edge_sems, angle, tile)
    infos = start_second(info, landed_info, info_sems, angle, tile)
    goals = start_edges(packs, goal_left, goal_right, goal_sems, angle, tile)
    first_sum[...] = finish_first(first, parts, landed_first, angle)
    second = start_second(first_sum, landed_second, second_sems, angle, tile)
    for copy in edges + goals:
        copy.wait()
    low = lanes((ROWS, TW)) < HALF
    inner, outer = tile > 0, tile < TILES - 1
    goal = widened(own_target[0], own_target[1], goal_left[...], goal_right[...], tile)
    for side, landed, inside in ((0, from_left, inner), (1, from_right, outer)):
        for part in range(2):
            total = grad[side, part] + jnp.where(inside, landed[part], 0.0)
            old = ext0[side, part]
            new = old - ALPHA * (total + RHO * (old - goal[side][part]))
            keep = jnp.logical_or(inside, jnp.logical_not(low) if side == 0 else low)
            ext[side, part] = jnp.where(keep, new, 0.0)
    info_all[...] = finish_second(infos, info, landed_info, tile)
    second_sum[...] = finish_second(second, first_sum, landed_second, tile)
    third = start_third(second_sum, gathered, third_sems, angle, tile)
    gathered[angle] = second_sum[...]
    number = info_all[pl.ds(0, 1), pl.ds(0, 1)]
    for copy in third:
        copy.wait()
    for chunk in range(ANG):
        part, start = divmod(chunk * CHUNK, PS)
        here = pl.ds(start, CHUNK)
        probe[part, here, :] = probe0[part, here, :] - PROBE_STEP * gathered[chunk] / number


def tail_kernel(
    ext, own_target, grad, rims, parts, info, turns, right_f,
    psi_new, every, gathered, bases, cosines, sines,
    from_left, from_right, landed_first, first_sum, landed_second, second_sum, slabs, slabs_here, work, rows,
    edge_sems, first_sems, second_sems, third_sems, slab_sems, row_sems,
):
    angle, tile = place()
    meet(angle_peers(angle, tile) + tile_peers(angle, tile))
    edges = start_edges(rims, from_left, from_right, edge_sems, angle, tile)
    first = start_first(parts, landed_first, first_sems, angle, tile)
    low = lanes((ROWS, TW)) < HALF
    inner, outer = tile > 0, tile < TILES - 1
    for part in range(2):
        old, total = (
            jnp.where(low, pltpu.roll(wide[0, part], HALF, 1), pltpu.roll(wide[1, part], HALF, 1))
            for wide in (ext, grad)
        )
        psi_new[part] = old - ALPHA * (total + RHO * (old - own_target[part]))
    for copy in edges:
        copy.wait()
    for part in range(2):
        before = jnp.where(inner, from_left[...], 0.0)
        after = jnp.where(outer, from_right[...], 0.0)
        if part == 0:
            extra = jnp.where(low, before, pltpu.roll(after, HALF, 1))
        else:
            extra = jnp.where(low, pltpu.roll(before, HALF, 1), after)
        new = psi_new[part] - ALPHA * extra
        psi_new[part] = new
        gap = own_target[part] - new
        for slab in range(TILES):
            slabs[slab, part] = gap[slab * ZS : (slab + 1) * ZS]
    copies = []
    for step in range(1, TILES):
        owner = (tile + step) % TILES
        copies.append(send(slabs.at[owner], slabs_here.at[tile], slab_sems, step, (angle, owner)))
    slabs_here[tile] = slabs[tile]
    first_sum[...] = finish_first(first, parts, landed_first, angle)
    second = start_second(first_sum, landed_second, second_sems, angle, tile)
    for copy in copies:
        copy.wait()

    items = [(slabs_here[index, 0], slabs_here[index, 1]) for index in range(TILES)]
    work[...] = jnp.zeros_like(work)
    for order, item in enumerate(sixteen(items, -1)):
        turn = (turns[0, pl.ds(order, 1), :], turns[1, pl.ds(order, 1), :])
        real, imag = times(item, turn)
        work[pl.ds(16 * order, ZS), pl.ds(0, TW)] = real
        work[pl.ds(16 * order, ZS), pl.ds(TW, TW)] = imag
    result = dot_right(work[...], right_f[...])
    for order in range(TILES):
        rows[:, order, :] = result[16 * order : 16 * order + ZS]

    chip, core = angle // 2, angle % 2
    up, down, over = (chip + 1) % 4, (chip + 3) % 4, (chip + 2) % 4
    upper, lower, across = 2 * up + core, 2 * down + core, 2 * over + core
    above, below, beside = (upper, tile), (lower, tile), (2 * chip + 1 - core, tile)
    one, two = pl.ds(0, ZS // 2), pl.ds(ZS // 2, ZS // 2)
    up_one = send(rows.at[one], every.at[angle, one], row_sems, 0, above)
    down_two = send(rows.at[two], every.at[angle, two], row_sems, 1, below)
    up_two = send(rows.at[two], every.at[angle, two], row_sems, 2, above)
    down_one = send(rows.at[one], every.at[angle, one], row_sems, 3, below)
    side = send(rows, every.at[angle], row_sems, 4, beside)
    every[angle] = rows[...]
    second_sum[...] = finish_second(second, first_sum, landed_second, tile)
    third = start_third(second_sum, gathered, third_sems, angle, tile)
    gathered[angle] = second_sum[...]
    phase_tables(info, bases, cosines, sines, angle)

    def pass_on(part, slot, peer):
        return send(every.at[part[0], part[1]], every.at[part[0], part[1]], row_sems, slot, peer)

    up_one.wait_recv()
    far_up = pass_on((lower, one), 5, above)
    side_a = pass_on((lower, one), 6, beside)
    down_two.wait_recv()
    far_down = pass_on((upper, two), 7, below)
    side_b = pass_on((upper, two), 8, beside)
    up_two.wait_recv()
    side_c = pass_on((lower, two), 9, beside)
    down_one.wait_recv()
    side_d = pass_on((upper, one), 10, beside)
    far_up.wait_recv()
    side_e = pass_on((across, one), 11, beside)
    far_down.wait_recv()
    side_f = pass_on((across, two), 12, beside)
    for copy in (side, side_a, side_b, side_c, side_d, side_e, side_f) + tuple(third):
        copy.wait()
    for copy in (up_one, down_two, up_two, down_one, far_up, far_down):
        copy.wait_send()


def gradient_kernel(
    counts, pos_z, pos_x, ext, probe, data, right_f, left_f, left_b, right_b, grad, parts, rims, probe_acc,
):
    count = counts[0, 0]
    grad[...] = jnp.zeros_like(grad)
    probe_acc[...] = jnp.zeros_like(probe_acc)
    lane = lanes((PS, TW))

    def sheet(values, axis):
        return jnp.concatenate(values, axis=axis)

    def group(index, carry):
        probe_real, probe_imag = probe[0], probe[1]
        rows, windows, spots = [], [], []
        for offset in range(GROUP):
            slot = GROUP * index + offset
            start_z, start_x = pos_z[0, 0, slot], pos_x[0, 0, slot]
            back = lax.rem(TW - start_x, TW)
            here = pl.ds(start_z, PS)
            real, imag = (
                pltpu.roll(jnp.where(lane >= start_x, ext[0, part, here, :], ext[1, part, here, :]), back, 1)
                for part in range(2)
            )
            windows.append((real, imag))
            spots.append((slot, start_z, start_x))
            rows.append(sheet(times((probe_real, probe_imag), (real, imag)), 1))
        turned = dot_right(sheet(rows, 0), right_f[...])
        turned = [turned[s * PS : (s + 1) * PS] for s in range(GROUP)]
        far = dot_left(left_f[...], sheet([sheet([v[:, :PS], v[:, PS:]], 0) for v in turned], 1))
        weighted = []
        for s in range(GROUP):
            slot = spots[s][0]
            far_real, far_imag = far[:PS, s * PS : (s + 1) * PS], far[PS:, s * PS : (s + 1) * PS]
            live = jnp.where(slot < count, 1.0, 0.0).astype(F32)
            misfit = (far_real * far_real + far_imag * far_imag - data[slot]) * live
            weighted.append(sheet([misfit * far_real, misfit * far_imag], 0))
        turned = dot_left(left_b[...], sheet(weighted, 1))
        turned = [turned[:, s * PS : (s + 1) * PS] for s in range(GROUP)]
        chi = dot_right(sheet([sheet([v[:PS], v[PS:]], 1) for v in turned], 0), right_b[...])
        for s in range(GROUP):
            slot, start_z, start_x = spots[s]
            here = pl.ds(start_z, PS)
            chi_real, chi_imag = chi[s * PS : (s + 1) * PS, :PS], chi[s * PS : (s + 1) * PS, PS:]
            real, imag = windows[s]
            probe_acc[pl.ds(0, PS), :] += real * chi_real + imag * chi_imag
            probe_acc[pl.ds(PS, PS), :] += real * chi_imag - imag * chi_real
            grad_real = probe_real * chi_real + probe_imag * chi_imag
            grad_imag = probe_real * chi_imag - probe_imag * chi_real
            for part, value in ((0, grad_real), (1, grad_imag)):
                moved = pltpu.roll(value, start_x, 1)
                grad[0, part, here, :] += jnp.where(lane >= start_x, moved, 0.0)
                grad[1, part, here, :] += jnp.where(lane < start_x, moved, 0.0)
        return carry

    lax.fori_loop(0, (count + GROUP - 1) // GROUP, group, 0)
    for chunk in range(ANG):
        parts[chunk] = probe_acc[pl.ds(chunk * CHUNK, CHUNK), :]
    low = lanes((ROWS, TW)) < HALF
    rims[0] = jnp.where(low, grad[0, 0], pltpu.roll(grad[0, 1], HALF, 1))
    rims[1] = jnp.where(low, pltpu.roll(grad[1, 0], HALF, 1), grad[1, 1])


def phase_tables(info, bases, cosines, sines, here):
    frequency = sublanes((TILES, TW)) + TILES * lanes((TILES, TW))
    signed = jnp.where(frequency < H // 2, frequency, frequency - H).astype(F32)
    centre = (YB * here - ANG * YB // 2).astype(F32) + (YB - 1) / 2.0
    row = sublanes((8, TW))
    for angle in range(ANG):
        turn = signed * (1.0 / H) * info[pl.ds(1, 1), pl.ds(angle, 1)]
        whole = centre * turn
        whole = 2.0 * math.pi * (whole - jnp.round(whole))
        half = math.pi * turn
        bases[angle, 0], bases[angle, 1] = jnp.cos(whole), jnp.sin(whole)
        power = (jnp.cos(half), jnp.sin(half))
        for level in range(5):
            bases[angle, 2 + 2 * level], bases[angle, 3 + 2 * level] = power
            power = times(power, power)

    def fill(angle, carry):
        for order in range(TILES):
            line = [
                tuple(
                    jnp.broadcast_to(bases[angle, 2 + 2 * level + part, pl.ds(order, 1), :], (8, TW))
                    for part in range(2)
                )
                for level in range(5)
            ]
            now = line[0]
            for level in range(3):
                ahead = times(now, line[1 + level])
                chosen = (row & (1 << level)) != 0
                now = tuple(jnp.where(chosen, new, old) for new, old in zip(ahead, now))
            later = times(now, line[4])
            cosines[angle, order, pl.ds(0, 8), :], sines[angle, order, pl.ds(0, 8), :] = now
            cosines[angle, order, pl.ds(8, 8), :], sines[angle, order, pl.ds(8, 8), :] = later
        return carry

    lax.fori_loop(0, ANG, fill, 0)


def flip8(value):
    row = sublanes(value.shape)
    value = pltpu.roll(value, 4, 0)
    value = jnp.where((row & 2) == 0, pltpu.roll(value, 6, 0), pltpu.roll(value, 2, 0))
    return jnp.where((row & 1) == 0, pltpu.roll(value, 7, 0), pltpu.roll(value, 1, 0))


def image_kernel(
    rows, bases, cosines, sines, turns, right_b, probe0, gathered, info, psi,
    image, probe_new, psi_new, turned, spread, middle, ready, sems,
):
    number = info[pl.ds(0, 1), pl.ds(0, 1)]
    for chunk in range(ANG):
        part, start = divmod(chunk * CHUNK, PS)
        here = pl.ds(start, CHUNK)
        probe_new[part, here, :] = probe0[part, here, :] - PROBE_STEP * gathered[chunk] / number
    psi_new[...] = psi[...]

    def shear(z):
        for angle in range(ANG):
            value = (rows[angle, z, :, pl.ds(0, TW)], rows[angle, z, :, pl.ds(TW, TW)])
            turned[angle, 0], turned[angle, 1] = times(value, (bases[angle, 0], bases[angle, 1]))
        for order in range(TILES):
            sums = None
            for angle in range(ANG):
                real = jnp.broadcast_to(turned[angle, 0, pl.ds(order, 1), :], (16, TW))
                imag = jnp.broadcast_to(turned[angle, 1, pl.ds(order, 1), :], (16, TW))
                cosine, sine = cosines[angle, order], sines[angle, order]
                terms = (real * cosine, imag * sine, real * sine, imag * cosine)
                sums = terms if sums is None else tuple(s + t for s, t in zip(sums, terms))
            rc, isn, rs, ic = sums
            above = (rc - isn, rs + ic)
            below = (rc + isn, ic - rs)
            for part in range(2):
                back = jnp.concatenate([flip8(below[part][8:]), flip8(below[part][:8])], axis=0)
                value = jnp.concatenate([back, above[part]], axis=0)
                high, low = split(value)
                here = pl.ds(order * YB, YB)
                spread[here, pl.ds(part * TW, TW)] = high
                spread[here, pl.ds((2 + part) * TW, TW)] = low
                spread[here, pl.ds((4 + part) * TW, TW)] = high

    def finish(slot):
        middle[...] = jnp.dot(spread[...], right_b[...], preferred_element_type=F32)
        for group in range(YB // 16):
            items = []
            for order in range(TILES):
                here = pl.ds(order * YB + 16 * group, 16)
                value = (middle[here, pl.ds(0, TW)], middle[here, pl.ds(TW, TW)])
                turn = (turns[0, pl.ds(order, 1), :], turns[1, pl.ds(order, 1), :])
                items.append(times(value, turn))
            for tile, item in enumerate(sixteen(items, 1)):
                for part in range(2):
                    ready[slot, part, pl.ds(16 * group, 16), pl.ds(tile * TW, TW)] = item[part].astype(BF16)

    def put(slot, z):
        return [
            pltpu.make_async_copy(ready.at[slot, part], image.at[part, z], sems.at[slot, part]) for part in range(2)
        ]

    def step(pair, carry):
        for slot in range(2):
            z = 2 * pair + slot
            shear(z)

            @pl.when(pair > 0)
            def _():
                for copy in put(slot, z - 2):
                    copy.wait()

            finish(slot)
            for copy in put(slot, z):
                copy.start()
        return carry

    lax.fori_loop(0, ZS // 2, step, 0)
    for slot in range(2):
        for copy in put(slot, ZS - 2 + slot):
            copy.wait()


def arr(*shape):
    return jax.ShapeDtypeStruct(shape, F32)


def dma(*shape):
    return pltpu.SemaphoreType.DMA(shape)


def call(kernel, outs, specs, out_specs, scratch, ident=None):
    extra = {} if ident is None else {"collective_id": ident, "has_side_effects": True}
    return pl.pallas_call(
        kernel,
        out_shape=outs,
        in_specs=specs,
        out_specs=out_specs,
        scratch_shapes=scratch,
        compiler_params=pltpu.CompilerParams(vmem_limit_bytes=VLIMIT, **extra),
    )


def shards(psi, target, probe, data, pos_z, pos_x, counts, shears):
    psi, target = psi.reshape(2, ROWS, TW), target.reshape(2, ROWS, TW)
    data = data.reshape(CAP, PS, PS)
    unit = dft_block(PS, 1.0 / math.sqrt(PS))
    tables = [
        jnp.asarray(t)
        for t in (right_table(unit), left_table(unit.T), left_table(unit), right_table(unit.T))
    ]
    wide, edge, small = arr(2, 2, ROWS, TW), arr(2, ROWS, TW), arr(8, TW)
    chunks, square = arr(ANG, CHUNK, TW), arr(2, PS, PS)
    table_shapes = [jax.ShapeDtypeStruct(t.shape, t.dtype) for t in tables]
    one = lambda *shape: pltpu.VMEM(shape, F32)

    outs = [wide, edge, edge, small, square, arr(CAP, PS, PS)] + table_shapes
    ext, goal, packs, info, probe, data, *tables = call(
        halo_kernel,
        outs,
        [SMEM] * 2 + [HBM] * 8,
        [VMEM] * len(outs),
        [
            one(2, ROWS, TW), one(2, ROWS, TW), one(ROWS, TW), one(ROWS, TW), one(8, TW), one(ANG, 8, TW),
            dma(2, 2), dma(2, ANG), dma(8),
        ],
        0,
    )(counts, shears, *(pltpu.with_memory_space_constraint(x, pltpu.HBM) for x in (psi, target, probe, data, *tables)))

    def gradient(ext, probe):
        return call(
            gradient_kernel, [wide, chunks, edge], [SMEM] * 3 + [VMEM] * 7, [VMEM] * 3, [one(2 * PS, PS)]
        )(counts, pos_z, pos_x, ext, probe, data, *tables)

    grad, parts, rims = gradient(ext, probe)
    ext, probe, info_all = call(
        exchange_kernel,
        [wide, square, small],
        [VMEM] * 7,
        [VMEM] * 3,
        [
            one(2, ROWS, TW), one(2, ROWS, TW), one(ROWS, TW), one(ROWS, TW),
            one(ANG, CHUNK, TW), one(CHUNK, TW), one(TILES, CHUNK, TW), one(CHUNK, TW), one(ANG, CHUNK, TW), one(TILES, 8, TW),
            dma(2, 2), dma(2, 2), dma(2, ANG), dma(2, TILES), dma(2, ANG), dma(2, TILES),
        ],
        1,
    )(grad, parts, packs, info, ext, goal, probe)
    grad, parts, rims = gradient(ext, probe)
    every, phases = arr(ANG, ZS, TILES, WIDE), arr(ANG, TILES, 16, TW)
    psi_new, every, gathered, bases, cosines, sines = call(
        tail_kernel,
        [edge, every, chunks, arr(ANG, 12, TILES, TW), phases, phases],
        [VMEM] * 8,
        [VMEM] * 6,
        [
            one(ROWS, TW), one(ROWS, TW),
            one(ANG, CHUNK, TW), one(CHUNK, TW), one(TILES, CHUNK, TW), one(CHUNK, TW),
            one(TILES, 2, ZS, TW), one(TILES, 2, ZS, TW), one(WIDE, WIDE), one(ZS, TILES, WIDE),
            dma(2, 2), dma(2, ANG), dma(2, TILES), dma(2, ANG), dma(2, TILES), dma(2, 13),
        ],
        2,
    )(ext, goal, grad, rims, parts, info, jnp.asarray(turn_table(-1)), jnp.asarray(right_table(dft_block(TW, 1.0))))
    inverse = dft_block(TW, 1.0 / (H * ANG)).T
    image, probe_new, psi_new = call(
        image_kernel,
        [jax.ShapeDtypeStruct((2, ZS, YB, H), BF16), square, edge],
        [VMEM] * 10,
        [HBM, VMEM, VMEM],
        [
            one(ANG, 2, TILES, TW),
            pltpu.VMEM((TILES * YB, 3 * WIDE), BF16),
            one(TILES * YB, WIDE),
            pltpu.VMEM((2, 2, YB, H), BF16),
            dma(2, 2),
        ],
    )(
        every, bases, cosines, sines, jnp.asarray(turn_table(1)), jnp.asarray(right_table(inverse)),
        probe, gathered, info_all, psi_new,
    )
    return psi_new.reshape(2, 1, ROWS, TW), probe_new, image


def solution(mesh):
    in_specs = (
        P(None, "angle", None, "tile"),
        P(None, "angle", None, "tile"),
        P(),
        P("angle", "tile", None, None, None),
        P("angle", "tile", None),
        P("angle", "tile", None),
        P("angle", "tile"),
        P("angle"),
    )
    out_specs = (P(None, "angle", None, "tile"), P(), P(None, "tile", "angle", None))
    return jax.shard_map(shards, mesh=mesh, in_specs=in_specs, out_specs=out_specs, check_vma=False)
```

```python
import functools
import math

import jax
import jax.numpy as jnp
import numpy as np
from jax import lax
from jax.experimental import pallas as pl
from jax.experimental.pallas import tpu as pltpu
from jax.sharding import PartitionSpec as P

ITERS = 2
ALPHA = 0.004
RHO = 5.0
PROBE_STEP = 0.02

ANG = 8
TILES = 16
PS = 128
TW = 128
ROWS = 160
CAP = 16
HALF = 64
WIDE = 256
ZS = ROWS // TILES
YB = 32
H = 2048
CHUNK = 2 * PS // ANG
GROUP = 8

F32 = jnp.float32
BF16 = jnp.bfloat16
MESH = pl.DeviceIdType.MESH
VMEM = pl.BlockSpec(memory_space=pltpu.VMEM)
SMEM = pl.BlockSpec(memory_space=pltpu.SMEM)
HBM = pl.BlockSpec(memory_space=pltpu.HBM)
VLIMIT = 20 * 1024 * 1024


def dft_block(length, scale):
    index = np.arange(length)
    turns = (index[:, None] * index[None, :]) % length
    angle = -2.0 * math.pi * turns / length
    real, imag = np.cos(angle) * scale, np.sin(angle) * scale
    return np.block([[real, imag], [-imag, real]])


def split_const(matrix):
    high = matrix.astype(BF16)
    low = (matrix - high.astype(np.float64)).astype(BF16)
    return high, low


def right_table(matrix):
    high, low = split_const(matrix)
    return np.concatenate([high, high, low], axis=0)


def left_table(matrix):
    high, low = split_const(matrix)
    return np.concatenate([high, high, low], axis=1)


def turn_table(orient):
    angle = orient * 2.0 * math.pi * np.arange(TILES)[:, None] * np.arange(TW)[None, :] / H
    return np.stack([np.cos(angle), np.sin(angle)]).astype(np.float32)


def split(value):
    high = value.astype(BF16)
    low = (value - high.astype(F32)).astype(BF16)
    return high, low


def dot_right(value, table):
    high, low = split(value)
    return jnp.dot(jnp.concatenate([high, low, high], axis=1), table, preferred_element_type=F32)


def dot_left(table, value):
    high, low = split(value)
    return jnp.dot(table, jnp.concatenate([high, low, high], axis=0), preferred_element_type=F32)


def times(left, right):
    return left[0] * right[0] - left[1] * right[1], left[0] * right[1] + left[1] * right[0]


def four(items, orient):
    (ar, ai), (br, bi), (cr, ci), (dr, di) = items
    sr, si, ur, ui = ar + cr, ai + ci, ar - cr, ai - ci
    pr, pi, qr, qi = br + dr, bi + di, br - dr, bi - di
    first = (sr + pr, si + pi)
    third = (sr - pr, si - pi)
    plus = (ur - qi, ui + qr)
    minus = (ur + qi, ui - qr)
    return [first, plus, third, minus] if orient > 0 else [first, minus, third, plus]


def turn_by(value, step, orient):
    real, imag = value
    if orient < 0:
        real, imag = imag, real
    if step == 4:
        real, imag = -imag, real
    elif step == 2:
        real, imag = (real - imag) * math.sqrt(0.5), (real + imag) * math.sqrt(0.5)
    elif step == 6:
        real, imag = (real + imag) * -math.sqrt(0.5), (real - imag) * math.sqrt(0.5)
    else:
        angle = 2.0 * math.pi * step / 16
        real, imag = times((real, imag), (math.cos(angle), math.sin(angle)))
    return (imag, real) if orient < 0 else (real, imag)


def sixteen(items, orient):
    columns = []
    for fine in range(4):
        partial = four([items[4 * coarse + fine] for coarse in range(4)], orient)
        for order in range(1, 4):
            step = fine * order
            if step:
                partial[order] = turn_by(partial[order], step, orient)
        columns.append(partial)
    result = [None] * 16
    for low in range(4):
        finished = four([columns[fine][low] for fine in range(4)], orient)
        for high in range(4):
            result[low + 4 * high] = finished[high]
    return result


def lanes(shape):
    return lax.broadcasted_iota(jnp.int32, shape, len(shape) - 1)


def sublanes(shape):
    return lax.broadcasted_iota(jnp.int32, shape, len(shape) - 2)


def place():
    return lax.axis_index("angle"), lax.axis_index("tile")


def meet(peers):
    barrier = pltpu.get_barrier_semaphore()
    for peer in peers:
        pl.semaphore_signal(barrier, inc=1, device_id=peer, device_id_type=MESH)
    pl.semaphore_wait(barrier, len(peers))


def send(source, target, sems, slot, peer):
    copy = pltpu.make_async_remote_copy(
        src_ref=source,
        dst_ref=target,
        send_sem=sems.at[0, slot],
        recv_sem=sems.at[1, slot],
        device_id=peer,
        device_id_type=MESH,
    )
    copy.start()
    return copy


def angle_peers(angle, tile):
    return [((angle + step) % ANG, tile) for step in range(1, ANG)]


def tile_peers(angle, tile):
    return [(angle, (tile + step) % TILES) for step in range(1, TILES)]


def neighbours(angle, tile):
    return (angle, (tile + TILES - 1) % TILES), (angle, (tile + 1) % TILES)


def start_edges(packs, from_left, from_right, sems, angle, tile):
    def copy(side, landing, peer):
        return pltpu.make_async_remote_copy(
            src_ref=packs.at[side],
            dst_ref=landing,
            send_sem=sems.at[0, side],
            recv_sem=sems.at[1, side],
            device_id=peer,
            device_id_type=MESH,
        )

    left, right = neighbours(angle, tile)
    to_left, to_right = copy(0, from_right, left), copy(1, from_left, right)

    @pl.when(tile > 0)
    def _():
        to_left.start()

    @pl.when(tile < TILES - 1)
    def _():
        to_right.start()

    return to_left, to_right


def finish_edges(copies, tile):
    to_left, to_right = copies

    @pl.when(tile > 0)
    def _():
        to_left.wait_send()
        to_right.wait_recv()

    @pl.when(tile < TILES - 1)
    def _():
        to_right.wait_send()
        to_left.wait_recv()


def clear_edges(from_left, from_right, tile):
    @pl.when(tile == 0)
    def _():
        from_left[...] = jnp.zeros_like(from_left)

    @pl.when(tile == TILES - 1)
    def _():
        from_right[...] = jnp.zeros_like(from_right)


def start_first(parts, landed, sems, angle, tile):
    return [
        send(parts.at[(angle + step) % ANG], landed.at[step], sems, step, ((angle + step) % ANG, tile))
        for step in range(1, ANG)
    ]


def finish_first(copies, parts, landed, angle):
    for copy in copies:
        copy.wait()
    total = parts[angle]
    for step in range(1, ANG):
        total = total + landed[step]
    return total


def start_second(source, landed, sems, angle, tile):
    return [
        send(source, landed.at[tile], sems, step, (angle, (tile + step) % TILES))
        for step in range(1, TILES)
    ]


def finish_second(copies, source, landed, tile):
    landed[tile] = source[...]
    for copy in copies:
        copy.wait()
    total = landed[0]
    for index in range(1, TILES):
        total = total + landed[index]
    return total


def start_third(source, gathered, sems, angle, tile):
    return [
        send(source, gathered.at[angle], sems, step, ((angle + step) % ANG, tile))
        for step in range(1, ANG)
    ]


def packed_sides(real, imag):
    low = lanes((ROWS, TW)) < HALF
    return (
        jnp.where(low, real, pltpu.roll(imag, HALF, 1)),
        jnp.where(low, pltpu.roll(real, HALF, 1), imag),
    )


def widened(real, imag, before, after):
    low = lanes((ROWS, TW)) < HALF
    real, imag = pltpu.roll(real, HALF, 1), pltpu.roll(imag, HALF, 1)
    return (
        (jnp.where(low, before, real), jnp.where(low, pltpu.roll(before, HALF, 1), imag)),
        (jnp.where(low, real, pltpu.roll(after, HALF, 1)), jnp.where(low, imag, after)),
    )


def halo_kernel(
    counts, shears, psi, target, probe, data, *refs,
):
    tables, refs = refs[:4], refs[4:]
    ext, own_target, packs, info, probe_here, data_here, *refs = refs
    tables_here, refs = refs[:4], refs[4:]
    own, sides, from_left, from_right, block, landed, edge_sems, info_sems, local_sems = refs
    angle, tile = place()
    fetches = [
        pltpu.make_async_copy(source, here, local_sems.at[index])
        for index, (source, here) in enumerate(
            zip((psi, target, probe, data) + tables, (own, own_target, probe_here, data_here) + tuple(tables_here))
        )
    ]
    for fetch in fetches:
        fetch.start()
    row, lane = sublanes((8, TW)), lanes((8, TW))
    count = jnp.where((row == 0) & (lane == 0), counts[0, 0].astype(F32), 0.0)
    block[...] = jnp.where((row == 1) & (lane == angle), shears[0], count)
    fetches[0].wait()
    for side, value in enumerate(packed_sides(own[0], own[1])):
        sides[side] = value
    clear_edges(from_left, from_right, tile)
    meet(angle_peers(angle, tile) + list(neighbours(angle, tile)))
    edges = start_edges(sides, from_left, from_right, edge_sems, angle, tile)
    infos = [
        send(block, landed.at[step], info_sems, step, ((angle + step) % ANG, tile)) for step in range(1, ANG)
    ]
    fetches[1].wait()
    for side, value in enumerate(packed_sides(own_target[0], own_target[1])):
        packs[side] = value
    for fetch in fetches[2:]:
        fetch.wait()
    finish_edges(edges, tile)
    for side, pair in enumerate(widened(own[0], own[1], from_left[...], from_right[...])):
        for part in range(2):
            ext[side, part] = pair[part]
    for copy in infos:
        copy.wait()
    total = block[...]
    for step in range(1, ANG):
        total = total + landed[step]
    info[...] = total


def exchange_kernel(
    grad, parts, packs, info, ext0, own_target, probe0, ext, probe, info_all,
    from_left, from_right, goal_left, goal_right, landed_first, first_sum, landed_second, second_sum, gathered, landed_info,
    edge_sems, goal_sems, first_sems, second_sems, third_sems, info_sems,
):
    angle, tile = place()
    clear_edges(from_left, from_right, tile)
    clear_edges(goal_left, goal_right, tile)
    meet(angle_peers(angle, tile) + tile_peers(angle, tile))
    first = start_first(parts, landed_first, first_sems, angle, tile)
    edges = start_edges(grad, from_left, from_right, edge_sems, angle, tile)
    infos = start_second(info, landed_info, info_sems, angle, tile)
    goals = start_edges(packs, goal_left, goal_right, goal_sems, angle, tile)
    first_sum[...] = finish_first(first, parts, landed_first, angle)
    second = start_second(first_sum, landed_second, second_sems, angle, tile)
    finish_edges(edges, tile)
    finish_edges(goals, tile)
    low = lanes((ROWS, TW)) < HALF
    inner, outer = tile > 0, tile < TILES - 1
    goal = widened(own_target[0], own_target[1], goal_left[...], goal_right[...])
    for side, landed, inside in ((0, from_left, inner), (1, from_right, outer)):
        for part in range(2):
            total = grad[side, part] + landed[part]
            old = ext0[side, part]
            new = old - ALPHA * (total + RHO * (old - goal[side][part]))
            keep = jnp.logical_or(inside, jnp.logical_not(low) if side == 0 else low)
            ext[side, part] = jnp.where(keep, new, 0.0)
    info_all[...] = finish_second(infos, info, landed_info, tile)
    second_sum[...] = finish_second(second, first_sum, landed_second, tile)
    third = start_third(second_sum, gathered, third_sems, angle, tile)
    gathered[angle] = second_sum[...]
    number = info_all[pl.ds(0, 1), pl.ds(0, 1)]
    for copy in third:
        copy.wait()
    for chunk in range(ANG):
        part, start = divmod(chunk * CHUNK, PS)
        here = pl.ds(start, CHUNK)
        probe[part, here, :] = probe0[part, here, :] - PROBE_STEP * gathered[chunk] / number


def tail_kernel(
    ext, own_target, grad, rims, parts, info, turns, right_f,
    psi_new, every, gathered, bases, cosines, sines,
    from_left, from_right, landed_first, first_sum, landed_second, second_sum, slabs, slabs_here, work, rows,
    edge_sems, first_sems, second_sems, third_sems, slab_sems, row_sems,
):
    angle, tile = place()
    clear_edges(from_left, from_right, tile)
    low = lanes((ROWS, TW)) < HALF
    for part in range(2):
        old, total = (
            jnp.where(low, pltpu.roll(wide[0, part], HALF, 1), pltpu.roll(wide[1, part], HALF, 1))
            for wide in (ext, grad)
        )
        new = old - ALPHA * (total + RHO * (old - own_target[part]))
        psi_new[part] = new
        for source, first_row in ((own_target[part] - new, part * ZS), (rims[part], (2 + part) * ZS)):
            for slab in range(TILES):
                slabs[slab, pl.ds(first_row, ZS), :] = source[slab * ZS : (slab + 1) * ZS]
    meet(angle_peers(angle, tile) + tile_peers(angle, tile))
    copies = []
    for step in range(1, TILES):
        owner = (tile + step) % TILES
        copies.append(send(slabs.at[owner], slabs_here.at[tile], slab_sems, step, (angle, owner)))
    first = start_first(parts, landed_first, first_sems, angle, tile)
    edges = start_edges(rims, from_left, from_right, edge_sems, angle, tile)
    slabs_here[tile] = slabs[tile]
    work[...] = jnp.zeros_like(work)
    first_sum[...] = finish_first(first, parts, landed_first, angle)
    second = start_second(first_sum, landed_second, second_sems, angle, tile)
    for copy in copies:
        copy.wait()

    low = lanes((ZS, TW)) < HALF
    zero = jnp.zeros((ZS, TW), F32)
    items = []
    for index in range(TILES):
        before = slabs_here[index - 1, pl.ds(3 * ZS, ZS), :] if index else zero
        after = slabs_here[index + 1, pl.ds(2 * ZS, ZS), :] if index < TILES - 1 else zero
        real = jnp.where(low, before, pltpu.roll(after, HALF, 1))
        imag = jnp.where(low, pltpu.roll(before, HALF, 1), after)
        items.append(
            (
                slabs_here[index, pl.ds(0, ZS), :] + ALPHA * real,
                slabs_here[index, pl.ds(ZS, ZS), :] + ALPHA * imag,
            )
        )
    for order, item in enumerate(sixteen(items, -1)):
        turn = (turns[0, pl.ds(order, 1), :], turns[1, pl.ds(order, 1), :])
        real, imag = times(item, turn)
        work[pl.ds(16 * order, ZS), pl.ds(0, TW)] = real
        work[pl.ds(16 * order, ZS), pl.ds(TW, TW)] = imag
    result = dot_right(work[...], right_f[...])
    for order in range(TILES):
        rows[:, order, :] = result[16 * order : 16 * order + ZS]

    chip, core = angle // 2, angle % 2
    up, down, over = (chip + 1) % 4, (chip + 3) % 4, (chip + 2) % 4
    upper, lower, across = 2 * up + core, 2 * down + core, 2 * over + core
    above, below, beside = (upper, tile), (lower, tile), (2 * chip + 1 - core, tile)
    one, two = pl.ds(0, ZS // 2), pl.ds(ZS // 2, ZS // 2)
    up_one = send(rows.at[one], every.at[angle, one], row_sems, 0, above)
    down_two = send(rows.at[two], every.at[angle, two], row_sems, 1, below)
    up_two = send(rows.at[two], every.at[angle, two], row_sems, 2, above)
    down_one = send(rows.at[one], every.at[angle, one], row_sems, 3, below)
    side = send(rows, every.at[angle], row_sems, 4, beside)
    every[angle] = rows[...]
    second_sum[...] = finish_second(second, first_sum, landed_second, tile)
    third = start_third(second_sum, gathered, third_sems, angle, tile)
    gathered[angle] = second_sum[...]
    finish_edges(edges, tile)
    for part in range(2):
        before, after = from_left[...], from_right[...]
        low = lanes((ROWS, TW)) < HALF
        if part == 0:
            extra = jnp.where(low, before, pltpu.roll(after, HALF, 1))
        else:
            extra = jnp.where(low, pltpu.roll(before, HALF, 1), after)
        psi_new[part] = psi_new[part] - ALPHA * extra
    phase_tables(info, bases, cosines, sines, angle)

    def pass_on(part, slot, peer):
        return send(every.at[part[0], part[1]], every.at[part[0], part[1]], row_sems, slot, peer)

    up_one.wait_recv()
    far_up = pass_on((lower, one), 5, above)
    side_a = pass_on((lower, one), 6, beside)
    down_two.wait_recv()
    far_down = pass_on((upper, two), 7, below)
    side_b = pass_on((upper, two), 8, beside)
    up_two.wait_recv()
    side_c = pass_on((lower, two), 9, beside)
    down_one.wait_recv()
    side_d = pass_on((upper, one), 10, beside)
    far_up.wait_recv()
    side_e = pass_on((across, one), 11, beside)
    far_down.wait_recv()
    side_f = pass_on((across, two), 12, beside)
    for copy in (side, side_a, side_b, side_c, side_d, side_e, side_f) + tuple(third):
        copy.wait()
    for copy in (up_one, down_two, up_two, down_one, far_up, far_down):
        copy.wait_send()


def gradient_kernel(
    counts, pos_z, pos_x, ext, probe, data, right_f, left_f, left_b, right_b, grad, parts, rims, probe_acc,
):
    count = counts[0, 0]
    grad[...] = jnp.zeros_like(grad)
    probe_acc[...] = jnp.zeros_like(probe_acc)
    lane = lanes((PS, TW))

    def sheet(values, axis):
        return jnp.concatenate(values, axis=axis)

    def group(index, carry):
        probe_real, probe_imag = probe[0], probe[1]
        rows, windows, spots = [], [], []
        for offset in range(GROUP):
            slot = GROUP * index + offset
            start_z, start_x = pos_z[0, 0, slot], pos_x[0, 0, slot]
            back = lax.rem(TW - start_x, TW)
            here = pl.ds(start_z, PS)
            real, imag = (
                pltpu.roll(jnp.where(lane >= start_x, ext[0, part, here, :], ext[1, part, here, :]), back, 1)
                for part in range(2)
            )
            windows.append((real, imag))
            spots.append((slot, start_z, start_x))
            rows.append(sheet(times((probe_real, probe_imag), (real, imag)), 1))
        pairs = range(0, GROUP, 2)
        sides = (slice(0, PS), slice(PS, 2 * PS))
        turned = [dot_right(sheet(rows[p : p + 2], 0), right_f[...]) for p in pairs]
        turned = [sheet([sheet([v[k, :PS], v[k, PS:]], 0) for k in sides], 1) for v in turned]
        far = [dot_left(left_f[...], v) for v in turned]
        weighted = []
        for s in range(GROUP):
            slot = spots[s][0]
            far_real, far_imag = (far[s // 2][k, sides[s % 2]] for k in sides)
            live = jnp.where(slot < count, 1.0, 0.0).astype(F32)
            misfit = (far_real * far_real + far_imag * far_imag - data[slot]) * live
            weighted.append(sheet([misfit * far_real, misfit * far_imag], 0))
        turned = [dot_left(left_b[...], sheet(weighted[p : p + 2], 1)) for p in pairs]
        turned = [sheet([sheet([v[:PS, k], v[PS:, k]], 1) for k in sides], 0) for v in turned]
        chi = [dot_right(v, right_b[...]) for v in turned]
        for s in range(GROUP):
            slot, start_z, start_x = spots[s]
            here = pl.ds(start_z, PS)
            chi_real, chi_imag = (chi[s // 2][sides[s % 2], k] for k in sides)
            real, imag = windows[s]
            probe_acc[pl.ds(0, PS), :] += real * chi_real + imag * chi_imag
            probe_acc[pl.ds(PS, PS), :] += real * chi_imag - imag * chi_real
            grad_real = probe_real * chi_real + probe_imag * chi_imag
            grad_imag = probe_real * chi_imag - probe_imag * chi_real
            for part, value in ((0, grad_real), (1, grad_imag)):
                moved = pltpu.roll(value, start_x, 1)
                grad[0, part, here, :] += jnp.where(lane >= start_x, moved, 0.0)
                grad[1, part, here, :] += jnp.where(lane < start_x, moved, 0.0)
        return carry

    lax.fori_loop(0, (count + GROUP - 1) // GROUP, group, 0)
    for chunk in range(ANG):
        parts[chunk] = probe_acc[pl.ds(chunk * CHUNK, CHUNK), :]
    low = lanes((ROWS, TW)) < HALF
    rims[0] = jnp.where(low, grad[0, 0], pltpu.roll(grad[0, 1], HALF, 1))
    rims[1] = jnp.where(low, pltpu.roll(grad[1, 0], HALF, 1), grad[1, 1])


def phase_tables(info, bases, cosines, sines, here):
    frequency = sublanes((TILES, TW)) + TILES * lanes((TILES, TW))
    signed = jnp.where(frequency < H // 2, frequency, frequency - H).astype(F32)
    centre = (YB * here - ANG * YB // 2).astype(F32) + (YB - 1) / 2.0
    row = sublanes((8, TW))
    for angle in range(ANG):
        turn = signed * (1.0 / H) * info[pl.ds(1, 1), pl.ds(angle, 1)]
        whole = centre * turn
        whole = 2.0 * math.pi * (whole - jnp.round(whole))
        half = math.pi * turn
        bases[angle, 0], bases[angle, 1] = jnp.cos(whole), jnp.sin(whole)
        power = (jnp.cos(half), jnp.sin(half))
        for level in range(5):
            bases[angle, 2 + 2 * level], bases[angle, 3 + 2 * level] = power
            power = times(power, power)

    def fill(angle, carry):
        for order in range(TILES):
            line = [
                tuple(
                    jnp.broadcast_to(bases[angle, 2 + 2 * level + part, pl.ds(order, 1), :], (8, TW))
                    for part in range(2)
                )
                for level in range(5)
            ]
            now = line[0]
            for level in range(3):
                ahead = times(now, line[1 + level])
                chosen = (row & (1 << level)) != 0
                now = tuple(jnp.where(chosen, new, old) for new, old in zip(ahead, now))
            later = times(now, line[4])
            cosines[angle, order, pl.ds(0, 8), :], sines[angle, order, pl.ds(0, 8), :] = now
            cosines[angle, order, pl.ds(8, 8), :], sines[angle, order, pl.ds(8, 8), :] = later
        return carry

    lax.fori_loop(0, ANG, fill, 0)


def flip8(value):
    row = sublanes(value.shape)
    value = pltpu.roll(value, 4, 0)
    value = jnp.where((row & 2) == 0, pltpu.roll(value, 6, 0), pltpu.roll(value, 2, 0))
    return jnp.where((row & 1) == 0, pltpu.roll(value, 7, 0), pltpu.roll(value, 1, 0))


def image_kernel(
    rows, bases, cosines, sines, turns, right_b, probe0, gathered, info, psi,
    image, probe_new, psi_new, turned_a, turned_b, spread_a, spread_b, middle_a, middle_b, ready, sems,
):
    number = info[pl.ds(0, 1), pl.ds(0, 1)]
    for chunk in range(ANG):
        part, start = divmod(chunk * CHUNK, PS)
        here = pl.ds(start, CHUNK)
        probe_new[part, here, :] = probe0[part, here, :] - PROBE_STEP * gathered[chunk] / number
    psi_new[...] = psi[...]

    def shear(z, turned, spread):
        for angle in range(ANG):
            value = (rows[angle, z, :, pl.ds(0, TW)], rows[angle, z, :, pl.ds(TW, TW)])
            turned[angle, 0], turned[angle, 1] = times(value, (bases[angle, 0], bases[angle, 1]))
        for order in range(TILES):
            sums = None
            for angle in range(ANG):
                real = jnp.broadcast_to(turned[angle, 0, pl.ds(order, 1), :], (16, TW))
                imag = jnp.broadcast_to(turned[angle, 1, pl.ds(order, 1), :], (16, TW))
                cosine, sine = cosines[angle, order], sines[angle, order]
                terms = (real * cosine, imag * sine, real * sine, imag * cosine)
                sums = terms if sums is None else tuple(s + t for s, t in zip(sums, terms))
            rc, isn, rs, ic = sums
            above = (rc - isn, rs + ic)
            below = (rc + isn, ic - rs)
            for part in range(2):
                back = jnp.concatenate([flip8(below[part][8:]), flip8(below[part][:8])], axis=0)
                value = jnp.concatenate([back, above[part]], axis=0)
                high, low = split(value)
                here = pl.ds(order * YB, YB)
                spread[here, pl.ds(part * TW, TW)] = high
                spread[here, pl.ds((2 + part) * TW, TW)] = low
                spread[here, pl.ds((4 + part) * TW, TW)] = high

    def finish(slot, spread, middle):
        middle[...] = jnp.dot(spread[...], right_b[...], preferred_element_type=F32)
        for group in range(YB // 16):
            items = []
            for order in range(TILES):
                here = pl.ds(order * YB + 16 * group, 16)
                value = (middle[here, pl.ds(0, TW)], middle[here, pl.ds(TW, TW)])
                turn = (turns[0, pl.ds(order, 1), :], turns[1, pl.ds(order, 1), :])
                items.append(times(value, turn))
            for tile, item in enumerate(sixteen(items, 1)):
                for part in range(2):
                    ready[slot, part, pl.ds(16 * group, 16), pl.ds(tile * TW, TW)] = item[part].astype(BF16)

    def put(slot, z):
        return [
            pltpu.make_async_copy(ready.at[slot, part], image.at[part, z], sems.at[slot, part]) for part in range(2)
        ]

    def step(pair, carry):
        base = 2 * lax.rem(pair, 2)

        @pl.when(pair > 1)
        def _():
            for odd in range(2):
                for copy in put(base + odd, 2 * pair - 4 + odd):
                    copy.wait()

        shear(2 * pair + 1, turned_b, spread_b)
        finish(base, spread_a, middle_a)
        shear(2 * pair + 2, turned_a, spread_a)
        finish(base + 1, spread_b, middle_b)
        for odd in range(2):
            for copy in put(base + odd, 2 * pair + odd):
                copy.start()
        return carry

    shear(0, turned_a, spread_a)
    lax.fori_loop(0, ZS // 2 - 1, step, 0)
    for odd in range(2):
        for copy in put(odd, ZS - 6 + odd):
            copy.wait()
    shear(ZS - 1, turned_b, spread_b)
    finish(0, spread_a, middle_a)
    for copy in put(0, ZS - 2):
        copy.start()
    finish(1, spread_b, middle_b)
    for copy in put(1, ZS - 1):
        copy.start()
    for slot, z in ((2, ZS - 4), (3, ZS - 3), (0, ZS - 2), (1, ZS - 1)):
        for copy in put(slot, z):
            copy.wait()


def arr(*shape):
    return jax.ShapeDtypeStruct(shape, F32)


def dma(*shape):
    return pltpu.SemaphoreType.DMA(shape)


def call(kernel, outs, specs, out_specs, scratch, ident=None):
    extra = {} if ident is None else {"collective_id": ident, "has_side_effects": True}
    return pl.pallas_call(
        kernel,
        out_shape=outs,
        in_specs=specs,
        out_specs=out_specs,
        scratch_shapes=scratch,
        compiler_params=pltpu.CompilerParams(vmem_limit_bytes=VLIMIT, **extra),
    )


def shards(psi, target, probe, data, pos_z, pos_x, counts, shears):
    psi, target = psi.reshape(2, ROWS, TW), target.reshape(2, ROWS, TW)
    data = data.reshape(CAP, PS, PS)
    unit = dft_block(PS, 1.0 / math.sqrt(PS))
    tables = [
        jnp.asarray(t)
        for t in (right_table(unit), left_table(unit.T), left_table(unit), right_table(unit.T))
    ]
    wide, edge, small = arr(2, 2, ROWS, TW), arr(2, ROWS, TW), arr(8, TW)
    chunks, square = arr(ANG, CHUNK, TW), arr(2, PS, PS)
    table_shapes = [jax.ShapeDtypeStruct(t.shape, t.dtype) for t in tables]
    one = lambda *shape: pltpu.VMEM(shape, F32)

    outs = [wide, edge, edge, small, square, arr(CAP, PS, PS)] + table_shapes
    ext, goal, packs, info, probe, data, *tables = call(
        halo_kernel,
        outs,
        [SMEM] * 2 + [HBM] * 8,
        [VMEM] * len(outs),
        [
            one(2, ROWS, TW), one(2, ROWS, TW), one(ROWS, TW), one(ROWS, TW), one(8, TW), one(ANG, 8, TW),
            dma(2, 2), dma(2, ANG), dma(8),
        ],
        0,
    )(counts, shears, *(pltpu.with_memory_space_constraint(x, pltpu.HBM) for x in (psi, target, probe, data, *tables)))

    def gradient(ext, probe):
        return call(
            gradient_kernel, [wide, chunks, edge], [SMEM] * 3 + [VMEM] * 7, [VMEM] * 3, [one(2 * PS, PS)]
        )(counts, pos_z, pos_x, ext, probe, data, *tables)

    grad, parts, rims = gradient(ext, probe)
    ext, probe, info_all = call(
        exchange_kernel,
        [wide, square, small],
        [VMEM] * 7,
        [VMEM] * 3,
        [
            one(2, ROWS, TW), one(2, ROWS, TW), one(ROWS, TW), one(ROWS, TW),
            one(ANG, CHUNK, TW), one(CHUNK, TW), one(TILES, CHUNK, TW), one(CHUNK, TW), one(ANG, CHUNK, TW), one(TILES, 8, TW),
            dma(2, 2), dma(2, 2), dma(2, ANG), dma(2, TILES), dma(2, ANG), dma(2, TILES),
        ],
        1,
    )(grad, parts, packs, info, ext, goal, probe)
    grad, parts, rims = gradient(ext, probe)
    every, phases = arr(ANG, ZS, TILES, WIDE), arr(ANG, TILES, 16, TW)
    psi_new, every, gathered, bases, cosines, sines = call(
        tail_kernel,
        [edge, every, chunks, arr(ANG, 12, TILES, TW), phases, phases],
        [VMEM] * 8,
        [VMEM] * 6,
        [
            one(ROWS, TW), one(ROWS, TW),
            one(ANG, CHUNK, TW), one(CHUNK, TW), one(TILES, CHUNK, TW), one(CHUNK, TW),
            one(TILES, 4 * ZS, TW), one(TILES, 4 * ZS, TW), one(WIDE, WIDE), one(ZS, TILES, WIDE),
            dma(2, 2), dma(2, ANG), dma(2, TILES), dma(2, ANG), dma(2, TILES), dma(2, 13),
        ],
        2,
    )(ext, goal, grad, rims, parts, info, jnp.asarray(turn_table(-1)), jnp.asarray(right_table(dft_block(TW, 1.0))))
    inverse = dft_block(TW, 1.0 / (H * ANG)).T
    image, probe_new, psi_new = call(
        image_kernel,
        [jax.ShapeDtypeStruct((2, ZS, YB, H), BF16), square, edge],
        [VMEM] * 10,
        [HBM, VMEM, VMEM],
        [
            one(ANG, 2, TILES, TW),
            one(ANG, 2, TILES, TW),
            pltpu.VMEM((TILES * YB, 3 * WIDE), BF16),
            pltpu.VMEM((TILES * YB, 3 * WIDE), BF16),
            one(TILES * YB, WIDE),
            one(TILES * YB, WIDE),
            pltpu.VMEM((4, 2, YB, H), BF16),
            dma(4, 2),
        ],
    )(
        every, bases, cosines, sines, jnp.asarray(turn_table(1)), jnp.asarray(right_table(inverse)),
        probe, gathered, info_all, psi_new,
    )
    return psi_new.reshape(2, 1, ROWS, TW), probe_new, image


def solution(mesh):
    in_specs = (
        P(None, "angle", None, "tile"),
        P(None, "angle", None, "tile"),
        P(),
        P("angle", "tile", None, None, None),
        P("angle", "tile", None),
        P("angle", "tile", None),
        P("angle", "tile"),
        P("angle"),
    )
    out_specs = (P(None, "angle", None, "tile"), P(), P(None, "tile", "angle", None))
    return jax.shard_map(shards, mesh=mesh, in_specs=in_specs, out_specs=out_specs, check_vma=False)
```

```python
import functools
import math

import jax
import jax.numpy as jnp
import numpy as np
from jax import lax
from jax.experimental import pallas as pl
from jax.experimental.pallas import tpu as pltpu
from jax.sharding import PartitionSpec as P

ITERS = 2
ALPHA = 0.004
RHO = 5.0
PROBE_STEP = 0.02

ANG = 8
TILES = 16
PS = 128
TW = 128
ROWS = 160
CAP = 16
HALF = 64
WIDE = 256
ZS = ROWS // TILES
YB = 32
H = 2048
CHUNK = 2 * PS // ANG
GROUP = 8
FIRST = 4

F32 = jnp.float32
BF16 = jnp.bfloat16
MESH = pl.DeviceIdType.MESH
VMEM = pl.BlockSpec(memory_space=pltpu.VMEM)
SMEM = pl.BlockSpec(memory_space=pltpu.SMEM)
HBM = pl.BlockSpec(memory_space=pltpu.HBM)
VLIMIT = 20 * 1024 * 1024


def dft_block(length, scale):
    index = np.arange(length)
    turns = (index[:, None] * index[None, :]) % length
    angle = -2.0 * math.pi * turns / length
    real, imag = np.cos(angle) * scale, np.sin(angle) * scale
    return np.block([[real, imag], [-imag, real]])


def split_const(matrix):
    high = matrix.astype(BF16)
    low = (matrix - high.astype(np.float64)).astype(BF16)
    return high, low


def right_table(matrix):
    high, low = split_const(matrix)
    return np.concatenate([high, high, low], axis=0)


def left_table(matrix):
    high, low = split_const(matrix)
    return np.concatenate([high, high, low], axis=1)


def turn_table(orient):
    angle = orient * 2.0 * math.pi * np.arange(TILES)[:, None] * np.arange(TW)[None, :] / H
    return np.stack([np.cos(angle), np.sin(angle)]).astype(np.float32)


def split(value):
    high = value.astype(BF16)
    low = (value - high.astype(F32)).astype(BF16)
    return high, low


def dot_right(value, table):
    high, low = split(value)
    return jnp.dot(jnp.concatenate([high, low, high], axis=1), table, preferred_element_type=F32)


def dot_left(table, value):
    high, low = split(value)
    return jnp.dot(table, jnp.concatenate([high, low, high], axis=0), preferred_element_type=F32)


def times(left, right):
    return left[0] * right[0] - left[1] * right[1], left[0] * right[1] + left[1] * right[0]


def four(items, orient):
    (ar, ai), (br, bi), (cr, ci), (dr, di) = items
    sr, si, ur, ui = ar + cr, ai + ci, ar - cr, ai - ci
    pr, pi, qr, qi = br + dr, bi + di, br - dr, bi - di
    first = (sr + pr, si + pi)
    third = (sr - pr, si - pi)
    plus = (ur - qi, ui + qr)
    minus = (ur + qi, ui - qr)
    return [first, plus, third, minus] if orient > 0 else [first, minus, third, plus]


def turn_by(value, step, orient):
    real, imag = value
    if orient < 0:
        real, imag = imag, real
    if step == 4:
        real, imag = -imag, real
    elif step == 2:
        real, imag = (real - imag) * math.sqrt(0.5), (real + imag) * math.sqrt(0.5)
    elif step == 6:
        real, imag = (real + imag) * -math.sqrt(0.5), (real - imag) * math.sqrt(0.5)
    else:
        angle = 2.0 * math.pi * step / 16
        real, imag = times((real, imag), (math.cos(angle), math.sin(angle)))
    return (imag, real) if orient < 0 else (real, imag)


def sixteen(items, orient):
    columns = []
    for fine in range(4):
        partial = four([items[4 * coarse + fine] for coarse in range(4)], orient)
        for order in range(1, 4):
            step = fine * order
            if step:
                partial[order] = turn_by(partial[order], step, orient)
        columns.append(partial)
    result = [None] * 16
    for low in range(4):
        finished = four([columns[fine][low] for fine in range(4)], orient)
        for high in range(4):
            result[low + 4 * high] = finished[high]
    return result


def lanes(shape):
    return lax.broadcasted_iota(jnp.int32, shape, len(shape) - 1)


def sublanes(shape):
    return lax.broadcasted_iota(jnp.int32, shape, len(shape) - 2)


def place():
    return lax.axis_index("angle"), lax.axis_index("tile")


def meet(peers):
    barrier = pltpu.get_barrier_semaphore()
    for peer in peers:
        pl.semaphore_signal(barrier, inc=1, device_id=peer, device_id_type=MESH)
    pl.semaphore_wait(barrier, len(peers))


def send(source, target, sems, slot, peer):
    copy = pltpu.make_async_remote_copy(
        src_ref=source,
        dst_ref=target,
        send_sem=sems.at[0, slot],
        recv_sem=sems.at[1, slot],
        device_id=peer,
        device_id_type=MESH,
    )
    copy.start()
    return copy


def meet_line(angle, tile):
    barrier = pltpu.get_barrier_semaphore()
    sides = ((tile > 0, tile - 1), (tile < TILES - 1, tile + 1))
    for inside, peer in sides:

        @pl.when(inside)
        def _():
            pl.semaphore_signal(barrier, inc=1, device_id=(angle, peer), device_id_type=MESH)

    inner = jnp.logical_and(tile > 0, tile < TILES - 1)

    @pl.when(inner)
    def _():
        pl.semaphore_wait(barrier, 2)

    @pl.when(jnp.logical_not(inner))
    def _():
        pl.semaphore_wait(barrier, 1)


def angle_peers(angle, tile):
    return [((angle + step) % ANG, tile) for step in range(1, ANG)]


FARTHEST = sorted(range(1, TILES), key=lambda s: -(min(s // 4, 4 - s // 4) + min(s % 4, 4 - s % 4)))


def shifted(tile, step):
    return (tile // 4 + step // 4) % 4 * 4 + (tile % 4 + step % 4) % 4


def tile_peers(angle, tile):
    return [(angle, shifted(tile, step)) for step in FARTHEST]


def neighbours(angle, tile):
    return (angle, (tile + TILES - 1) % TILES), (angle, (tile + 1) % TILES)


def start_edges(packs, from_left, from_right, sems, angle, tile):
    def copy(side, landing, peer):
        return pltpu.make_async_remote_copy(
            src_ref=packs.at[side],
            dst_ref=landing,
            send_sem=sems.at[0, side],
            recv_sem=sems.at[1, side],
            device_id=peer,
            device_id_type=MESH,
        )

    left, right = neighbours(angle, tile)
    to_left, to_right = copy(0, from_right, left), copy(1, from_left, right)

    @pl.when(tile > 0)
    def _():
        to_left.start()

    @pl.when(tile < TILES - 1)
    def _():
        to_right.start()

    return to_left, to_right


def finish_edges(copies, tile):
    to_left, to_right = copies

    @pl.when(tile > 0)
    def _():
        to_left.wait_send()
        to_right.wait_recv()

    @pl.when(tile < TILES - 1)
    def _():
        to_right.wait_send()
        to_left.wait_recv()


def clear_edges(from_left, from_right, tile):
    @pl.when(tile == 0)
    def _():
        from_left[...] = jnp.zeros_like(from_left)

    @pl.when(tile == TILES - 1)
    def _():
        from_right[...] = jnp.zeros_like(from_right)


def start_first(parts, landed, sems, angle, tile):
    return [
        send(parts.at[(angle + step) % ANG], landed.at[step], sems, step, ((angle + step) % ANG, tile))
        for step in range(1, ANG)
    ]


def finish_first(copies, parts, landed, angle):
    for copy in copies:
        copy.wait()
    total = parts[angle]
    for step in range(1, ANG):
        total = total + landed[step]
    return total


def start_second(source, landed, sems, angle, tile):
    return [
        send(source, landed.at[tile], sems, step, (angle, shifted(tile, step)))
        for step in FARTHEST
    ]


def finish_second(copies, source, landed, tile):
    landed[tile] = source[...]
    for copy in copies:
        copy.wait()
    total = landed[0]
    for index in range(1, TILES):
        total = total + landed[index]
    return total


def start_third(source, gathered, sems, angle, tile):
    return [
        send(source, gathered.at[angle], sems, step, ((angle + step) % ANG, tile))
        for step in range(1, ANG)
    ]


def packed_sides(real, imag):
    low = lanes((ROWS, TW)) < HALF
    return (
        jnp.where(low, real, pltpu.roll(imag, HALF, 1)),
        jnp.where(low, pltpu.roll(real, HALF, 1), imag),
    )


def widened(real, imag, before, after):
    low = lanes((ROWS, TW)) < HALF
    real, imag = pltpu.roll(real, HALF, 1), pltpu.roll(imag, HALF, 1)
    return (
        (jnp.where(low, before, real), jnp.where(low, pltpu.roll(before, HALF, 1), imag)),
        (jnp.where(low, real, pltpu.roll(after, HALF, 1)), jnp.where(low, imag, after)),
    )


def halo_kernel(
    counts, shears, psi, target, probe, data, *refs,
):
    tables, refs = refs[:4], refs[4:]
    ext, own_target, packs, info, probe_here, data_here, *refs = refs
    tables_here, refs = refs[:4], refs[4:]
    own, sides, from_left, from_right, edge_sems, local_sems = refs
    angle, tile = place()
    fetches = [
        pltpu.make_async_copy(source, here, local_sems.at[index])
        for index, (source, here) in enumerate(
            zip((psi, target, probe, data) + tables, (own, own_target, probe_here, data_here) + tuple(tables_here))
        )
    ]
    for fetch in fetches:
        fetch.start()
    row, lane = sublanes((8, TW)), lanes((8, TW))
    count = jnp.where((row == 0) & (lane == 0), counts[0, 0].astype(F32), 0.0)
    info[...] = jnp.where((row == 1) & (lane == angle), shears[0], count)
    fetches[0].wait()
    for side, value in enumerate(packed_sides(own[0], own[1])):
        sides[side] = value
    clear_edges(from_left, from_right, tile)
    meet_line(angle, tile)
    edges = start_edges(sides, from_left, from_right, edge_sems, angle, tile)
    fetches[1].wait()
    for side, value in enumerate(packed_sides(own_target[0], own_target[1])):
        packs[side] = value
    for fetch in fetches[2:]:
        fetch.wait()
    finish_edges(edges, tile)
    for side, pair in enumerate(widened(own[0], own[1], from_left[...], from_right[...])):
        for part in range(2):
            ext[side, part] = pair[part]


def exchange_kernel(
    grad, parts, packs, info, ext0, own_target, probe0, ext, probe, info_some, info_all,
    from_left, from_right, goal_left, goal_right, landed_first, first_sum, landed_second, second_sum, gathered, landed_some, landed_info,
    edge_sems, goal_sems, first_sems, second_sems, third_sems, some_sems, info_sems,
):
    angle, tile = place()
    clear_edges(from_left, from_right, tile)
    clear_edges(goal_left, goal_right, tile)
    meet(angle_peers(angle, tile) + tile_peers(angle, tile))
    first = start_first(parts, landed_first, first_sems, angle, tile)
    edges = start_edges(grad, from_left, from_right, edge_sems, angle, tile)
    some = [
        send(info, landed_some.at[step], some_sems, step, ((angle + step) % ANG, tile)) for step in range(1, ANG)
    ]
    first_sum[...] = finish_first(first, parts, landed_first, angle)
    second = start_second(first_sum, landed_second, second_sems, angle, tile)
    for copy in some:
        copy.wait()
    total = info[...]
    for step in range(1, ANG):
        total = total + landed_some[step]
    info_some[...] = total
    infos = start_second(info_some, landed_info, info_sems, angle, tile)
    goals = start_edges(packs, goal_left, goal_right, goal_sems, angle, tile)
    second_sum[...] = finish_second(second, first_sum, landed_second, tile)
    third = start_third(second_sum, gathered, third_sems, angle, tile)
    finish_edges(edges, tile)
    finish_edges(goals, tile)
    low = lanes((ROWS, TW)) < HALF
    inner, outer = tile > 0, tile < TILES - 1
    goal = widened(own_target[0], own_target[1], goal_left[...], goal_right[...])
    for side, landed, inside in ((0, from_left, inner), (1, from_right, outer)):
        for part in range(2):
            total = grad[side, part] + landed[part]
            old = ext0[side, part]
            new = old - ALPHA * (total + RHO * (old - goal[side][part]))
            keep = jnp.logical_or(inside, jnp.logical_not(low) if side == 0 else low)
            ext[side, part] = jnp.where(keep, new, 0.0)
    gathered[angle] = second_sum[...]
    info_all[...] = finish_second(infos, info_some, landed_info, tile)
    number = info_all[pl.ds(0, 1), pl.ds(0, 1)]
    for copy in third:
        copy.wait()
    for chunk in range(ANG):
        part, start = divmod(chunk * CHUNK, PS)
        here = pl.ds(start, CHUNK)
        probe[part, here, :] = probe0[part, here, :] - PROBE_STEP * gathered[chunk] / number


def tail_kernel(
    ext, own_target, grad, rims, parts, info, turns, right_f,
    psi_new, every, gathered, bases, cosines, sines,
    from_left, from_right, landed_first, first_sum, landed_second, second_sum,
    slabs_one, slabs_two, here_one, here_two, work_one, work_two, rows,
    edge_sems, first_sems, second_sems, third_sems, one_sems, two_sems, row_sems,
):
    angle, tile = place()
    clear_edges(from_left, from_right, tile)
    low = lanes((ROWS, TW)) < HALF
    for part in range(2):
        old, total = (
            jnp.where(low, pltpu.roll(wide[0, part], HALF, 1), pltpu.roll(wide[1, part], HALF, 1))
            for wide in (ext, grad)
        )
        new = old - ALPHA * (total + RHO * (old - own_target[part]))
        psi_new[part] = new
        for source, place_at in ((own_target[part] - new, part), (rims[part], 2 + part)):
            for slab in range(TILES):
                for slabs, first, count in ((slabs_one, 0, FIRST), (slabs_two, FIRST, ZS - FIRST)):
                    start = slab * ZS + first
                    slabs[slab, pl.ds(place_at * count, count), :] = source[start : start + count]
    meet(tile_peers(angle, tile) + angle_peers(angle, tile))
    halves = []
    for slabs, landed, sems in ((slabs_one, here_one, one_sems), (slabs_two, here_two, two_sems)):
        copies = []
        for step in FARTHEST:
            owner = shifted(tile, step)
            copies.append(send(slabs.at[owner], landed.at[tile], sems, step, (angle, owner)))
        halves.append(copies)
    first = start_first(parts, landed_first, first_sems, angle, tile)
    for slabs, landed in ((slabs_one, here_one), (slabs_two, here_two)):
        landed[tile] = slabs[tile]
    work_one[...] = jnp.zeros_like(work_one)
    work_two[...] = jnp.zeros_like(work_two)
    first_sum[...] = finish_first(first, parts, landed_first, angle)
    second = start_second(first_sum, landed_second, second_sems, angle, tile)

    def spectrum(copies, landed, work, start, count):
        for copy in copies:
            copy.wait()
        low = lanes((count, TW)) < HALF
        zero = jnp.zeros((count, TW), F32)
        items = []
        for index in range(TILES):
            before = landed[index - 1, pl.ds(3 * count, count), :] if index else zero
            after = landed[index + 1, pl.ds(2 * count, count), :] if index < TILES - 1 else zero
            real = jnp.where(low, before, pltpu.roll(after, HALF, 1))
            imag = jnp.where(low, pltpu.roll(before, HALF, 1), after)
            items.append(
                (
                    landed[index, pl.ds(0, count), :] + ALPHA * real,
                    landed[index, pl.ds(count, count), :] + ALPHA * imag,
                )
            )
        for order, item in enumerate(sixteen(items, -1)):
            turn = (turns[0, pl.ds(order, 1), :], turns[1, pl.ds(order, 1), :])
            real, imag = times(item, turn)
            work[pl.ds(8 * order, count), pl.ds(0, TW)] = real
            work[pl.ds(8 * order, count), pl.ds(TW, TW)] = imag
        result = dot_right(work[...], right_f[...])
        for order in range(TILES):
            rows[pl.ds(start, count), order, :] = result[8 * order : 8 * order + count]

    chip, core = angle // 2, angle % 2
    up, down, over = (chip + 1) % 4, (chip + 3) % 4, (chip + 2) % 4
    upper, lower, across = 2 * up + core, 2 * down + core, 2 * over + core
    above, below, beside = (upper, tile), (lower, tile), (2 * chip + 1 - core, tile)
    one, two = pl.ds(0, FIRST), pl.ds(FIRST, ZS - FIRST)
    spectrum(halves[0], here_one, work_one, 0, FIRST)

    def spread(part, slot):
        peers = ((across, 0), (upper, 1), (lower, 2))
        return [
            send(rows.at[part], every.at[angle, part], row_sems, slot + index, (peer, tile)) for peer, index in peers
        ]

    sent_one = spread(one, 0)
    spectrum(halves[1], here_two, work_two, FIRST, ZS - FIRST)
    sent_two = spread(two, 3)
    side = send(rows, every.at[angle], row_sems, 12, beside)
    edges = start_edges(rims, from_left, from_right, edge_sems, angle, tile)
    every[angle] = rows[...]
    second_sum[...] = finish_second(second, first_sum, landed_second, tile)
    third = [
        send(second_sum, gathered.at[angle], third_sems, slot, (peer, tile))
        for slot, peer in enumerate((across, upper, lower))
    ]
    handed = [side, send(second_sum, gathered.at[angle], third_sems, 3, beside)]
    gathered[angle] = second_sum[...]
    phase_tables(info, bases, cosines, sines, angle)

    def hand(copies, target, sems, slot):
        for index, source in ((1, lower), (2, upper), (0, across)):
            copies[index].wait()
            landed = target(source)
            handed.append(send(landed, landed, sems, slot + index, beside))

    hand(sent_one, lambda source: every.at[source, one], row_sems, 6)
    hand(third, lambda source: gathered.at[source], third_sems, 4)
    finish_edges(edges, tile)
    for part in range(2):
        before, after = from_left[...], from_right[...]
        low = lanes((ROWS, TW)) < HALF
        if part == 0:
            extra = jnp.where(low, before, pltpu.roll(after, HALF, 1))
        else:
            extra = jnp.where(low, pltpu.roll(before, HALF, 1), after)
        psi_new[part] = psi_new[part] - ALPHA * extra
    hand(sent_two, lambda source: every.at[source, two], row_sems, 9)
    for copy in handed:
        copy.wait()


def gradient_kernel(
    counts, pos_z, pos_x, ext, probe, data, right_f, left_f, left_b, right_b, grad, parts, rims, probe_acc,
):
    count = counts[0, 0]
    grad[...] = jnp.zeros_like(grad)
    probe_acc[...] = jnp.zeros_like(probe_acc)
    lane = lanes((PS, TW))

    def sheet(values, axis):
        return jnp.concatenate(values, axis=axis)

    def group(index, carry):
        probe_real, probe_imag = probe[0], probe[1]
        rows, windows, spots = [], [], []
        for offset in range(GROUP):
            slot = GROUP * index + offset
            start_z, start_x = pos_z[0, 0, slot], pos_x[0, 0, slot]
            back = lax.rem(TW - start_x, TW)
            here = pl.ds(start_z, PS)
            real, imag = (
                pltpu.roll(jnp.where(lane >= start_x, ext[0, part, here, :], ext[1, part, here, :]), back, 1)
                for part in range(2)
            )
            windows.append((real, imag))
            spots.append((slot, start_z, start_x))
            rows.append(sheet(times((probe_real, probe_imag), (real, imag)), 1))
        pairs = range(0, GROUP, 2)
        sides = (slice(0, PS), slice(PS, 2 * PS))
        turned = [dot_right(sheet(rows[p : p + 2], 0), right_f[...]) for p in pairs]
        turned = [sheet([sheet([v[k, :PS], v[k, PS:]], 0) for k in sides], 1) for v in turned]
        far = [dot_left(left_f[...], v) for v in turned]
        weighted = []
        for s in range(GROUP):
            slot = spots[s][0]
            far_real, far_imag = (far[s // 2][k, sides[s % 2]] for k in sides)
            live = jnp.where(slot < count, 1.0, 0.0).astype(F32)
            misfit = (far_real * far_real + far_imag * far_imag - data[slot]) * live
            weighted.append(sheet([misfit * far_real, misfit * far_imag], 0))
        turned = [dot_left(left_b[...], sheet(weighted[p : p + 2], 1)) for p in pairs]
        turned = [sheet([sheet([v[:PS, k], v[PS:, k]], 1) for k in sides], 0) for v in turned]
        chi = [dot_right(v, right_b[...]) for v in turned]
        for s in range(GROUP):
            slot, start_z, start_x = spots[s]
            here = pl.ds(start_z, PS)
            chi_real, chi_imag = (chi[s // 2][sides[s % 2], k] for k in sides)
            real, imag = windows[s]
            probe_acc[pl.ds(0, PS), :] += real * chi_real + imag * chi_imag
            probe_acc[pl.ds(PS, PS), :] += real * chi_imag - imag * chi_real
            grad_real = probe_real * chi_real + probe_imag * chi_imag
            grad_imag = probe_real * chi_imag - probe_imag * chi_real
            for part, value in ((0, grad_real), (1, grad_imag)):
                moved = pltpu.roll(value, start_x, 1)
                grad[0, part, here, :] += jnp.where(lane >= start_x, moved, 0.0)
                grad[1, part, here, :] += jnp.where(lane < start_x, moved, 0.0)
        return carry

    lax.fori_loop(0, (count + GROUP - 1) // GROUP, group, 0)
    for chunk in range(ANG):
        parts[chunk] = probe_acc[pl.ds(chunk * CHUNK, CHUNK), :]
    low = lanes((ROWS, TW)) < HALF
    rims[0] = jnp.where(low, grad[0, 0], pltpu.roll(grad[0, 1], HALF, 1))
    rims[1] = jnp.where(low, pltpu.roll(grad[1, 0], HALF, 1), grad[1, 1])


def phase_tables(info, bases, cosines, sines, here):
    frequency = sublanes((TILES, TW)) + TILES * lanes((TILES, TW))
    signed = jnp.where(frequency < H // 2, frequency, frequency - H).astype(F32)
    centre = (YB * here - ANG * YB // 2).astype(F32) + (YB - 1) / 2.0
    row = sublanes((8, TW))
    for angle in range(ANG):
        turn = signed * (1.0 / H) * info[pl.ds(1, 1), pl.ds(angle, 1)]
        whole = centre * turn
        whole = 2.0 * math.pi * (whole - jnp.round(whole))
        half = math.pi * turn
        bases[angle, 0], bases[angle, 1] = jnp.cos(whole), jnp.sin(whole)
        power = (jnp.cos(half), jnp.sin(half))
        for level in range(5):
            bases[angle, 2 + 2 * level], bases[angle, 3 + 2 * level] = power
            power = times(power, power)

    def fill(angle, carry):
        for order in range(TILES):
            line = [
                tuple(
                    jnp.broadcast_to(bases[angle, 2 + 2 * level + part, pl.ds(order, 1), :], (8, TW))
                    for part in range(2)
                )
                for level in range(5)
            ]
            now = line[0]
            for level in range(3):
                ahead = times(now, line[1 + level])
                chosen = (row & (1 << level)) != 0
                now = tuple(jnp.where(chosen, new, old) for new, old in zip(ahead, now))
            later = times(now, line[4])
            cosines[angle, order, pl.ds(0, 8), :], sines[angle, order, pl.ds(0, 8), :] = now
            cosines[angle, order, pl.ds(8, 8), :], sines[angle, order, pl.ds(8, 8), :] = later
        return carry

    lax.fori_loop(0, ANG, fill, 0)


def flip8(value):
    row = sublanes(value.shape)
    value = pltpu.roll(value, 4, 0)
    value = jnp.where((row & 2) == 0, pltpu.roll(value, 6, 0), pltpu.roll(value, 2, 0))
    return jnp.where((row & 1) == 0, pltpu.roll(value, 7, 0), pltpu.roll(value, 1, 0))


def image_kernel(
    rows, bases, cosines, sines, turns, right_b, probe0, gathered, info, psi,
    image, probe_new, psi_new, turned_a, turned_b, spread_a, spread_b, middle_a, middle_b, ready, sems,
):
    number = info[pl.ds(0, 1), pl.ds(0, 1)]
    for chunk in range(ANG):
        part, start = divmod(chunk * CHUNK, PS)
        here = pl.ds(start, CHUNK)
        probe_new[part, here, :] = probe0[part, here, :] - PROBE_STEP * gathered[chunk] / number
    psi_new[...] = psi[...]

    def shear(z, turned, spread):
        for angle in range(ANG):
            value = (rows[angle, z, :, pl.ds(0, TW)], rows[angle, z, :, pl.ds(TW, TW)])
            turned[angle, 0], turned[angle, 1] = times(value, (bases[angle, 0], bases[angle, 1]))
        for order in range(TILES):
            sums = None
            for angle in range(ANG):
                real = jnp.broadcast_to(turned[angle, 0, pl.ds(order, 1), :], (16, TW))
                imag = jnp.broadcast_to(turned[angle, 1, pl.ds(order, 1), :], (16, TW))
                cosine, sine = cosines[angle, order], sines[angle, order]
                terms = (real * cosine, imag * sine, real * sine, imag * cosine)
                sums = terms if sums is None else tuple(s + t for s, t in zip(sums, terms))
            rc, isn, rs, ic = sums
            above = (rc - isn, rs + ic)
            below = (rc + isn, ic - rs)
            for part in range(2):
                back = jnp.concatenate([flip8(below[part][8:]), flip8(below[part][:8])], axis=0)
                value = jnp.concatenate([back, above[part]], axis=0)
                high, low = split(value)
                here = pl.ds(order * YB, YB)
                spread[here, pl.ds(part * TW, TW)] = high
                spread[here, pl.ds((2 + part) * TW, TW)] = low
                spread[here, pl.ds((4 + part) * TW, TW)] = high

    def finish(slot, spread, middle):
        middle[...] = jnp.dot(spread[...], right_b[...], preferred_element_type=F32)
        for group in range(YB // 16):
            items = []
            for order in range(TILES):
                here = pl.ds(order * YB + 16 * group, 16)
                value = (middle[here, pl.ds(0, TW)], middle[here, pl.ds(TW, TW)])
                turn = (turns[0, pl.ds(order, 1), :], turns[1, pl.ds(order, 1), :])
                items.append(times(value, turn))
            for tile, item in enumerate(sixteen(items, 1)):
                for part in range(2):
                    ready[slot, part, pl.ds(16 * group, 16), pl.ds(tile * TW, TW)] = item[part].astype(BF16)

    def put(slot, z):
        return [
            pltpu.make_async_copy(ready.at[slot, part], image.at[part, z], sems.at[slot, part]) for part in range(2)
        ]

    def step(pair, carry):
        base = 2 * lax.rem(pair, 2)

        @pl.when(pair > 1)
        def _():
            for odd in range(2):
                for copy in put(base + odd, 2 * pair - 4 + odd):
                    copy.wait()

        shear(2 * pair + 1, turned_b, spread_b)
        finish(base, spread_a, middle_a)
        shear(2 * pair + 2, turned_a, spread_a)
        finish(base + 1, spread_b, middle_b)
        for odd in range(2):
            for copy in put(base + odd, 2 * pair + odd):
                copy.start()
        return carry

    shear(0, turned_a, spread_a)
    lax.fori_loop(0, ZS // 2 - 1, step, 0)
    for odd in range(2):
        for copy in put(odd, ZS - 6 + odd):
            copy.wait()
    shear(ZS - 1, turned_b, spread_b)
    finish(0, spread_a, middle_a)
    for copy in put(0, ZS - 2):
        copy.start()
    finish(1, spread_b, middle_b)
    for copy in put(1, ZS - 1):
        copy.start()
    for slot, z in ((2, ZS - 4), (3, ZS - 3), (0, ZS - 2), (1, ZS - 1)):
        for copy in put(slot, z):
            copy.wait()


def arr(*shape):
    return jax.ShapeDtypeStruct(shape, F32)


def dma(*shape):
    return pltpu.SemaphoreType.DMA(shape)


def call(kernel, outs, specs, out_specs, scratch, ident=None):
    extra = {} if ident is None else {"collective_id": ident, "has_side_effects": True}
    return pl.pallas_call(
        kernel,
        out_shape=outs,
        in_specs=specs,
        out_specs=out_specs,
        scratch_shapes=scratch,
        compiler_params=pltpu.CompilerParams(vmem_limit_bytes=VLIMIT, **extra),
    )


def shards(psi, target, probe, data, pos_z, pos_x, counts, shears):
    psi, target = psi.reshape(2, ROWS, TW), target.reshape(2, ROWS, TW)
    data = data.reshape(CAP, PS, PS)
    unit = dft_block(PS, 1.0 / math.sqrt(PS))
    tables = [
        jnp.asarray(t)
        for t in (right_table(unit), left_table(unit.T), left_table(unit), right_table(unit.T))
    ]
    wide, edge, small = arr(2, 2, ROWS, TW), arr(2, ROWS, TW), arr(8, TW)
    chunks, square = arr(ANG, CHUNK, TW), arr(2, PS, PS)
    table_shapes = [jax.ShapeDtypeStruct(t.shape, t.dtype) for t in tables]
    one = lambda *shape: pltpu.VMEM(shape, F32)

    outs = [wide, edge, edge, small, square, arr(CAP, PS, PS)] + table_shapes
    ext, goal, packs, info, probe, data, *tables = call(
        halo_kernel,
        outs,
        [SMEM] * 2 + [HBM] * 8,
        [VMEM] * len(outs),
        [
            one(2, ROWS, TW), one(2, ROWS, TW), one(ROWS, TW), one(ROWS, TW),
            dma(2, 2), dma(8),
        ],
        0,
    )(counts, shears, *(pltpu.with_memory_space_constraint(x, pltpu.HBM) for x in (psi, target, probe, data, *tables)))

    def gradient(ext, probe):
        return call(
            gradient_kernel, [wide, chunks, edge], [SMEM] * 3 + [VMEM] * 7, [VMEM] * 3, [one(2 * PS, PS)]
        )(counts, pos_z, pos_x, ext, probe, data, *tables)

    grad, parts, rims = gradient(ext, probe)
    ext, probe, info, info_all = call(
        exchange_kernel,
        [wide, square, small, small],
        [VMEM] * 7,
        [VMEM] * 4,
        [
            one(2, ROWS, TW), one(2, ROWS, TW), one(ROWS, TW), one(ROWS, TW),
            one(ANG, CHUNK, TW), one(CHUNK, TW), one(TILES, CHUNK, TW), one(CHUNK, TW), one(ANG, CHUNK, TW), one(ANG, 8, TW), one(TILES, 8, TW),
            dma(2, 2), dma(2, 2), dma(2, ANG), dma(2, TILES), dma(2, ANG), dma(2, ANG), dma(2, TILES),
        ],
        1,
    )(grad, parts, packs, info, ext, goal, probe)
    grad, parts, rims = gradient(ext, probe)
    every, phases = arr(ANG, ZS, TILES, WIDE), arr(ANG, TILES, 16, TW)
    psi_new, every, gathered, bases, cosines, sines = call(
        tail_kernel,
        [edge, every, chunks, arr(ANG, 12, TILES, TW), phases, phases],
        [VMEM] * 8,
        [VMEM] * 6,
        [
            one(ROWS, TW), one(ROWS, TW),
            one(ANG, CHUNK, TW), one(CHUNK, TW), one(TILES, CHUNK, TW), one(CHUNK, TW),
            one(TILES, 4 * FIRST, TW), one(TILES, 4 * (ZS - FIRST), TW),
            one(TILES, 4 * FIRST, TW), one(TILES, 4 * (ZS - FIRST), TW),
            one(PS, WIDE), one(PS, WIDE), one(ZS, TILES, WIDE),
            dma(2, 2), dma(2, ANG), dma(2, TILES), dma(2, ANG), dma(2, TILES), dma(2, TILES), dma(2, 13),
        ],
        2,
    )(ext, goal, grad, rims, parts, info, jnp.asarray(turn_table(-1)), jnp.asarray(right_table(dft_block(TW, 1.0))))
    inverse = dft_block(TW, 1.0 / (H * ANG)).T
    image, probe_new, psi_new = call(
        image_kernel,
        [jax.ShapeDtypeStruct((2, ZS, YB, H), BF16), square, edge],
        [VMEM] * 10,
        [HBM, VMEM, VMEM],
        [
            one(ANG, 2, TILES, TW),
            one(ANG, 2, TILES, TW),
            pltpu.VMEM((TILES * YB, 3 * WIDE), BF16),
            pltpu.VMEM((TILES * YB, 3 * WIDE), BF16),
            one(TILES * YB, WIDE),
            one(TILES * YB, WIDE),
            pltpu.VMEM((4, 2, YB, H), BF16),
            dma(4, 2),
        ],
    )(
        every, bases, cosines, sines, jnp.asarray(turn_table(1)), jnp.asarray(right_table(inverse)),
        probe, gathered, info_all, psi_new,
    )
    return psi_new.reshape(2, 1, ROWS, TW), probe_new, image


def solution(mesh):
    in_specs = (
        P(None, "angle", None, "tile"),
        P(None, "angle", None, "tile"),
        P(),
        P("angle", "tile", None, None, None),
        P("angle", "tile", None),
        P("angle", "tile", None),
        P("angle", "tile"),
        P("angle"),
    )
    out_specs = (P(None, "angle", None, "tile"), P(), P(None, "tile", "angle", None))
    return jax.shard_map(shards, mesh=mesh, in_specs=in_specs, out_specs=out_specs, check_vma=False)
```

```python
import functools
import math

import jax
import jax.numpy as jnp
import numpy as np
from jax import lax
from jax.experimental import pallas as pl
from jax.experimental.pallas import tpu as pltpu
from jax.sharding import PartitionSpec as P

ITERS = 2
ALPHA = 0.004
RHO = 5.0
PROBE_STEP = 0.02

ANG = 8
TILES = 16
PS = 128
TW = 128
ROWS = 160
CAP = 16
HALF = 64
WIDE = 256
ZS = ROWS // TILES
YB = 32
H = 2048
CHUNK = 2 * PS // ANG
GROUP = 8
FIRST = 4

F32 = jnp.float32
BF16 = jnp.bfloat16
MESH = pl.DeviceIdType.MESH
VMEM = pl.BlockSpec(memory_space=pltpu.VMEM)
SMEM = pl.BlockSpec(memory_space=pltpu.SMEM)
HBM = pl.BlockSpec(memory_space=pltpu.HBM)
VLIMIT = 20 * 1024 * 1024


def dft_block(length, scale):
    index = np.arange(length)
    turns = (index[:, None] * index[None, :]) % length
    angle = -2.0 * math.pi * turns / length
    real, imag = np.cos(angle) * scale, np.sin(angle) * scale
    return np.block([[real, imag], [-imag, real]])


def split_const(matrix):
    high = matrix.astype(BF16)
    low = (matrix - high.astype(np.float64)).astype(BF16)
    return high, low


def right_table(matrix):
    high, low = split_const(matrix)
    return np.concatenate([high, high, low], axis=0)


def left_table(matrix):
    high, low = split_const(matrix)
    return np.concatenate([high, high, low], axis=1)


def turn_table(orient):
    angle = orient * 2.0 * math.pi * np.arange(TILES)[:, None] * np.arange(TW)[None, :] / H
    return np.stack([np.cos(angle), np.sin(angle)]).astype(np.float32)


def split(value):
    high = value.astype(BF16)
    low = (value - high.astype(F32)).astype(BF16)
    return high, low


def dot_right(value, table):
    high, low = split(value)
    return jnp.dot(jnp.concatenate([high, low, high], axis=1), table, preferred_element_type=F32)


def dot_left(table, value):
    high, low = split(value)
    return jnp.dot(table, jnp.concatenate([high, low, high], axis=0), preferred_element_type=F32)


def times(left, right):
    return left[0] * right[0] - left[1] * right[1], left[0] * right[1] + left[1] * right[0]


def four(items, orient):
    (ar, ai), (br, bi), (cr, ci), (dr, di) = items
    sr, si, ur, ui = ar + cr, ai + ci, ar - cr, ai - ci
    pr, pi, qr, qi = br + dr, bi + di, br - dr, bi - di
    first = (sr + pr, si + pi)
    third = (sr - pr, si - pi)
    plus = (ur - qi, ui + qr)
    minus = (ur + qi, ui - qr)
    return [first, plus, third, minus] if orient > 0 else [first, minus, third, plus]


def turn_by(value, step, orient):
    real, imag = value
    if orient < 0:
        real, imag = imag, real
    if step == 4:
        real, imag = -imag, real
    elif step == 2:
        real, imag = (real - imag) * math.sqrt(0.5), (real + imag) * math.sqrt(0.5)
    elif step == 6:
        real, imag = (real + imag) * -math.sqrt(0.5), (real - imag) * math.sqrt(0.5)
    else:
        angle = 2.0 * math.pi * step / 16
        real, imag = times((real, imag), (math.cos(angle), math.sin(angle)))
    return (imag, real) if orient < 0 else (real, imag)


def sixteen(items, orient):
    columns = []
    for fine in range(4):
        partial = four([items[4 * coarse + fine] for coarse in range(4)], orient)
        for order in range(1, 4):
            step = fine * order
            if step:
                partial[order] = turn_by(partial[order], step, orient)
        columns.append(partial)
    result = [None] * 16
    for low in range(4):
        finished = four([columns[fine][low] for fine in range(4)], orient)
        for high in range(4):
            result[low + 4 * high] = finished[high]
    return result


def lanes(shape):
    return lax.broadcasted_iota(jnp.int32, shape, len(shape) - 1)


def sublanes(shape):
    return lax.broadcasted_iota(jnp.int32, shape, len(shape) - 2)


def place():
    return lax.axis_index("angle"), lax.axis_index("tile")


def greet(peers):
    barrier = pltpu.get_barrier_semaphore()
    for peer in peers:
        pl.semaphore_signal(barrier, inc=1, device_id=peer, device_id_type=MESH)
    return lambda: pl.semaphore_wait(barrier, len(peers))


def send(source, target, sems, slot, peer):
    copy = pltpu.make_async_remote_copy(
        src_ref=source,
        dst_ref=target,
        send_sem=sems.at[0, slot],
        recv_sem=sems.at[1, slot],
        device_id=peer,
        device_id_type=MESH,
    )
    copy.start()
    return copy


def greet_line(angle, tile):
    barrier = pltpu.get_barrier_semaphore()
    sides = ((tile > 0, tile - 1), (tile < TILES - 1, tile + 1))
    for inside, peer in sides:

        @pl.when(inside)
        def _():
            pl.semaphore_signal(barrier, inc=1, device_id=(angle, peer), device_id_type=MESH)

    inner = jnp.logical_and(tile > 0, tile < TILES - 1)

    def wait():
        @pl.when(inner)
        def _():
            pl.semaphore_wait(barrier, 2)

        @pl.when(jnp.logical_not(inner))
        def _():
            pl.semaphore_wait(barrier, 1)

    return wait


def angle_peers(angle, tile):
    return [((angle + step) % ANG, tile) for step in range(1, ANG)]


FARTHEST = sorted(range(1, TILES), key=lambda s: -(min(s // 4, 4 - s // 4) + min(s % 4, 4 - s % 4)))


def shifted(tile, step):
    return (tile // 4 + step // 4) % 4 * 4 + (tile % 4 + step % 4) % 4


def tile_peers(angle, tile):
    return [(angle, shifted(tile, step)) for step in FARTHEST]


def neighbours(angle, tile):
    return (angle, (tile + TILES - 1) % TILES), (angle, (tile + 1) % TILES)


def start_edges(packs, from_left, from_right, sems, angle, tile):
    def copy(side, landing, peer):
        return pltpu.make_async_remote_copy(
            src_ref=packs.at[side],
            dst_ref=landing,
            send_sem=sems.at[0, side],
            recv_sem=sems.at[1, side],
            device_id=peer,
            device_id_type=MESH,
        )

    left, right = neighbours(angle, tile)
    to_left, to_right = copy(0, from_right, left), copy(1, from_left, right)

    @pl.when(tile > 0)
    def _():
        to_left.start()

    @pl.when(tile < TILES - 1)
    def _():
        to_right.start()

    return to_left, to_right


def finish_edges(copies, tile):
    to_left, to_right = copies

    @pl.when(tile > 0)
    def _():
        to_left.wait_send()
        to_right.wait_recv()

    @pl.when(tile < TILES - 1)
    def _():
        to_right.wait_send()
        to_left.wait_recv()


def clear_edges(from_left, from_right, tile):
    @pl.when(tile == 0)
    def _():
        from_left[...] = jnp.zeros_like(from_left)

    @pl.when(tile == TILES - 1)
    def _():
        from_right[...] = jnp.zeros_like(from_right)


def start_first(parts, landed, sems, angle, tile):
    return [
        send(parts.at[(angle + step) % ANG], landed.at[step], sems, step, ((angle + step) % ANG, tile))
        for step in range(1, ANG)
    ]


def finish_first(copies, parts, landed, angle):
    for copy in copies:
        copy.wait()
    total = parts[angle]
    for step in range(1, ANG):
        total = total + landed[step]
    return total


def start_second(source, landed, sems, angle, tile):
    return [
        send(source, landed.at[tile], sems, step, (angle, shifted(tile, step)))
        for step in FARTHEST
    ]


def finish_second(copies, source, landed, tile):
    landed[tile] = source[...]
    for copy in copies:
        copy.wait()
    total = landed[0]
    for index in range(1, TILES):
        total = total + landed[index]
    return total


def start_third(source, gathered, sems, angle, tile):
    return [
        send(source, gathered.at[angle], sems, step, ((angle + step) % ANG, tile))
        for step in range(1, ANG)
    ]


def packed_sides(real, imag):
    low = lanes((ROWS, TW)) < HALF
    return (
        jnp.where(low, real, pltpu.roll(imag, HALF, 1)),
        jnp.where(low, pltpu.roll(real, HALF, 1), imag),
    )


def widened(real, imag, before, after):
    low = lanes((ROWS, TW)) < HALF
    real, imag = pltpu.roll(real, HALF, 1), pltpu.roll(imag, HALF, 1)
    return (
        (jnp.where(low, before, real), jnp.where(low, pltpu.roll(before, HALF, 1), imag)),
        (jnp.where(low, real, pltpu.roll(after, HALF, 1)), jnp.where(low, imag, after)),
    )


def halo_kernel(
    counts, shears, psi, target, probe, data, *refs,
):
    tables, refs = refs[:4], refs[4:]
    ext, own_target, packs, info, probe_here, data_here, *refs = refs
    tables_here, refs = refs[:4], refs[4:]
    own, sides, from_left, from_right, edge_sems, local_sems = refs
    angle, tile = place()
    fetches = [
        pltpu.make_async_copy(source, here, local_sems.at[index])
        for index, (source, here) in enumerate(
            zip((psi, target, probe, data) + tables, (own, own_target, probe_here, data_here) + tuple(tables_here))
        )
    ]
    for fetch in fetches:
        fetch.start()
    clear_edges(from_left, from_right, tile)
    met = greet_line(angle, tile)
    row, lane = sublanes((8, TW)), lanes((8, TW))
    count = jnp.where((row == 0) & (lane == 0), counts[0, 0].astype(F32), 0.0)
    info[...] = jnp.where((row == 1) & (lane == angle), shears[0], count)
    fetches[0].wait()
    for side, value in enumerate(packed_sides(own[0], own[1])):
        sides[side] = value
    met()
    edges = start_edges(sides, from_left, from_right, edge_sems, angle, tile)
    fetches[1].wait()
    for side, value in enumerate(packed_sides(own_target[0], own_target[1])):
        packs[side] = value
    for fetch in fetches[2:]:
        fetch.wait()
    finish_edges(edges, tile)
    for side, pair in enumerate(widened(own[0], own[1], from_left[...], from_right[...])):
        for part in range(2):
            ext[side, part] = pair[part]


def exchange_kernel(
    grad, parts, packs, info, ext0, own_target, probe0, ext, probe, info_some, info_all,
    from_left, from_right, goal_left, goal_right, landed_first, first_sum, landed_second, second_sum, gathered, landed_some, landed_info,
    edge_sems, goal_sems, first_sems, second_sems, third_sems, some_sems, info_sems,
):
    angle, tile = place()
    clear_edges(from_left, from_right, tile)
    clear_edges(goal_left, goal_right, tile)
    greet(tile_peers(angle, tile) + angle_peers(angle, tile))()
    first = start_first(parts, landed_first, first_sems, angle, tile)
    edges = start_edges(grad, from_left, from_right, edge_sems, angle, tile)
    some = [
        send(info, landed_some.at[step], some_sems, step, ((angle + step) % ANG, tile)) for step in range(1, ANG)
    ]
    first_sum[...] = finish_first(first, parts, landed_first, angle)
    second = start_second(first_sum, landed_second, second_sems, angle, tile)
    for copy in some:
        copy.wait()
    total = info[...]
    for step in range(1, ANG):
        total = total + landed_some[step]
    info_some[...] = total
    infos = start_second(info_some, landed_info, info_sems, angle, tile)
    goals = start_edges(packs, goal_left, goal_right, goal_sems, angle, tile)
    second_sum[...] = finish_second(second, first_sum, landed_second, tile)
    third = start_third(second_sum, gathered, third_sems, angle, tile)
    finish_edges(edges, tile)
    finish_edges(goals, tile)
    low = lanes((ROWS, TW)) < HALF
    inner, outer = tile > 0, tile < TILES - 1
    goal = widened(own_target[0], own_target[1], goal_left[...], goal_right[...])
    for side, landed, inside in ((0, from_left, inner), (1, from_right, outer)):
        for part in range(2):
            total = grad[side, part] + landed[part]
            old = ext0[side, part]
            new = old - ALPHA * (total + RHO * (old - goal[side][part]))
            keep = jnp.logical_or(inside, jnp.logical_not(low) if side == 0 else low)
            ext[side, part] = jnp.where(keep, new, 0.0)
    gathered[angle] = second_sum[...]
    info_all[...] = finish_second(infos, info_some, landed_info, tile)
    number = info_all[pl.ds(0, 1), pl.ds(0, 1)]
    for copy in third:
        copy.wait()
    for chunk in range(ANG):
        part, start = divmod(chunk * CHUNK, PS)
        here = pl.ds(start, CHUNK)
        probe[part, here, :] = probe0[part, here, :] - PROBE_STEP * gathered[chunk] / number


def tail_kernel(
    ext, own_target, grad, rims, parts, info, turns, right_f,
    psi_new, every, gathered, bases, cosines, sines,
    from_left, from_right, landed_first, first_sum, landed_second, second_sum,
    slabs_one, slabs_two, here_one, here_two, work_one, work_two, rows,
    edge_sems, first_sems, second_sems, third_sems, one_sems, two_sems, row_sems,
):
    angle, tile = place()
    clear_edges(from_left, from_right, tile)
    met = greet(tile_peers(angle, tile) + angle_peers(angle, tile))
    low = lanes((ROWS, TW)) < HALF
    for part in range(2):
        old, total = (
            jnp.where(low, pltpu.roll(wide[0, part], HALF, 1), pltpu.roll(wide[1, part], HALF, 1))
            for wide in (ext, grad)
        )
        new = old - ALPHA * (total + RHO * (old - own_target[part]))
        psi_new[part] = new
        for source, place_at in ((own_target[part] - new, part), (rims[part], 2 + part)):
            for slab in range(TILES):
                for slabs, first, count in ((slabs_one, 0, FIRST), (slabs_two, FIRST, ZS - FIRST)):
                    start = slab * ZS + first
                    slabs[slab, pl.ds(place_at * count, count), :] = source[start : start + count]
    work_one[...] = jnp.zeros_like(work_one)
    work_two[...] = jnp.zeros_like(work_two)
    met()
    halves = []
    for slabs, landed, sems in ((slabs_one, here_one, one_sems), (slabs_two, here_two, two_sems)):
        copies = []
        for step in FARTHEST:
            owner = shifted(tile, step)
            copies.append(send(slabs.at[owner], landed.at[tile], sems, step, (angle, owner)))
        halves.append(copies)
    first = start_first(parts, landed_first, first_sems, angle, tile)
    for slabs, landed in ((slabs_one, here_one), (slabs_two, here_two)):
        landed[tile] = slabs[tile]
    first_sum[...] = finish_first(first, parts, landed_first, angle)
    second = start_second(first_sum, landed_second, second_sems, angle, tile)

    def spectrum(copies, landed, work, start, count):
        for copy in copies:
            copy.wait()
        low = lanes((count, TW)) < HALF
        zero = jnp.zeros((count, TW), F32)
        items = []
        for index in range(TILES):
            before = landed[index - 1, pl.ds(3 * count, count), :] if index else zero
            after = landed[index + 1, pl.ds(2 * count, count), :] if index < TILES - 1 else zero
            real = jnp.where(low, before, pltpu.roll(after, HALF, 1))
            imag = jnp.where(low, pltpu.roll(before, HALF, 1), after)
            items.append(
                (
                    landed[index, pl.ds(0, count), :] + ALPHA * real,
                    landed[index, pl.ds(count, count), :] + ALPHA * imag,
                )
            )
        for order, item in enumerate(sixteen(items, -1)):
            turn = (turns[0, pl.ds(order, 1), :], turns[1, pl.ds(order, 1), :])
            real, imag = times(item, turn)
            work[pl.ds(8 * order, count), pl.ds(0, TW)] = real
            work[pl.ds(8 * order, count), pl.ds(TW, TW)] = imag
        result = dot_right(work[...], right_f[...])
        for order in range(TILES):
            rows[pl.ds(start, count), order, :] = result[8 * order : 8 * order + count]

    chip, core = angle // 2, angle % 2
    up, down, over = (chip + 1) % 4, (chip + 3) % 4, (chip + 2) % 4
    upper, lower, across = 2 * up + core, 2 * down + core, 2 * over + core
    above, below, beside = (upper, tile), (lower, tile), (2 * chip + 1 - core, tile)
    one, two = pl.ds(0, FIRST), pl.ds(FIRST, ZS - FIRST)
    spectrum(halves[0], here_one, work_one, 0, FIRST)

    def spread(part, slot):
        peers = ((across, 0), (upper, 1), (lower, 2))
        return [
            send(rows.at[part], every.at[angle, part], row_sems, slot + index, (peer, tile)) for peer, index in peers
        ]

    sent_one = spread(one, 0)
    spectrum(halves[1], here_two, work_two, FIRST, ZS - FIRST)
    sent_two = spread(two, 3)
    side = send(rows, every.at[angle], row_sems, 12, beside)
    edges = start_edges(rims, from_left, from_right, edge_sems, angle, tile)
    every[angle] = rows[...]
    second_sum[...] = finish_second(second, first_sum, landed_second, tile)
    third = [
        send(second_sum, gathered.at[angle], third_sems, slot, (peer, tile))
        for slot, peer in enumerate((across, upper, lower))
    ]
    handed = [side, send(second_sum, gathered.at[angle], third_sems, 3, beside)]
    gathered[angle] = second_sum[...]
    phase_tables(info, bases, cosines, sines, angle)

    def hand(copies, target, sems, slot):
        for index, source in ((1, lower), (2, upper), (0, across)):
            copies[index].wait()
            landed = target(source)
            handed.append(send(landed, landed, sems, slot + index, beside))

    hand(sent_one, lambda source: every.at[source, one], row_sems, 6)
    hand(third, lambda source: gathered.at[source], third_sems, 4)
    finish_edges(edges, tile)
    for part in range(2):
        before, after = from_left[...], from_right[...]
        low = lanes((ROWS, TW)) < HALF
        if part == 0:
            extra = jnp.where(low, before, pltpu.roll(after, HALF, 1))
        else:
            extra = jnp.where(low, pltpu.roll(before, HALF, 1), after)
        psi_new[part] = psi_new[part] - ALPHA * extra
    hand(sent_two, lambda source: every.at[source, two], row_sems, 9)
    for copy in handed:
        copy.wait()


def gradient_kernel(
    counts, pos_z, pos_x, ext, probe, data, right_f, left_f, left_b, right_b, grad, parts, rims, probe_acc,
):
    count = counts[0, 0]
    grad[...] = jnp.zeros_like(grad)
    probe_acc[...] = jnp.zeros_like(probe_acc)
    lane = lanes((PS, TW))

    def sheet(values, axis):
        return jnp.concatenate(values, axis=axis)

    def group(index, carry):
        probe_real, probe_imag = probe[0], probe[1]
        rows, windows, spots = [], [], []
        for offset in range(GROUP):
            slot = GROUP * index + offset
            start_z, start_x = pos_z[0, 0, slot], pos_x[0, 0, slot]
            back = lax.rem(TW - start_x, TW)
            here = pl.ds(start_z, PS)
            real, imag = (
                pltpu.roll(jnp.where(lane >= start_x, ext[0, part, here, :], ext[1, part, here, :]), back, 1)
                for part in range(2)
            )
            windows.append((real, imag))
            spots.append((slot, start_z, start_x))
            rows.append(sheet(times((probe_real, probe_imag), (real, imag)), 1))
        pairs = range(0, GROUP, 2)
        sides = (slice(0, PS), slice(PS, 2 * PS))
        turned = [dot_right(sheet(rows[p : p + 4], 0), right_f[...]) for p in range(0, GROUP, 4)]
        turned = [v[k] for v in turned for k in (slice(0, 2 * PS), slice(2 * PS, 4 * PS))]
        turned = [sheet([sheet([v[k, :PS], v[k, PS:]], 0) for k in sides], 1) for v in turned]
        far = [dot_left(left_f[...], v) for v in turned]
        weighted = []
        for s in range(GROUP):
            slot = spots[s][0]
            far_real, far_imag = (far[s // 2][k, sides[s % 2]] for k in sides)
            live = jnp.where(slot < count, 1.0, 0.0).astype(F32)
            misfit = (far_real * far_real + far_imag * far_imag - data[slot]) * live
            weighted.append(sheet([misfit * far_real, misfit * far_imag], 0))
        turned = [dot_left(left_b[...], sheet(weighted[p : p + 2], 1)) for p in pairs]
        turned = [sheet([sheet([v[:PS, k], v[PS:, k]], 1) for k in sides], 0) for v in turned]
        chi = [dot_right(sheet(turned[p : p + 2], 0), right_b[...]) for p in range(0, GROUP // 2, 2)]
        chi = [v[k] for v in chi for k in (slice(0, 2 * PS), slice(2 * PS, 4 * PS))]
        for s in range(GROUP):
            slot, start_z, start_x = spots[s]
            here = pl.ds(start_z, PS)
            chi_real, chi_imag = (chi[s // 2][sides[s % 2], k] for k in sides)
            real, imag = windows[s]
            probe_acc[pl.ds(0, PS), :] += real * chi_real + imag * chi_imag
            probe_acc[pl.ds(PS, PS), :] += real * chi_imag - imag * chi_real
            grad_real = probe_real * chi_real + probe_imag * chi_imag
            grad_imag = probe_real * chi_imag - probe_imag * chi_real
            for part, value in ((0, grad_real), (1, grad_imag)):
                moved = pltpu.roll(value, start_x, 1)
                grad[0, part, here, :] += jnp.where(lane >= start_x, moved, 0.0)
                grad[1, part, here, :] += jnp.where(lane < start_x, moved, 0.0)
        return carry

    lax.fori_loop(0, (count + GROUP - 1) // GROUP, group, 0)
    for chunk in range(ANG):
        parts[chunk] = probe_acc[pl.ds(chunk * CHUNK, CHUNK), :]
    low = lanes((ROWS, TW)) < HALF
    rims[0] = jnp.where(low, grad[0, 0], pltpu.roll(grad[0, 1], HALF, 1))
    rims[1] = jnp.where(low, pltpu.roll(grad[1, 0], HALF, 1), grad[1, 1])


def phase_tables(info, bases, cosines, sines, here):
    frequency = sublanes((TILES, TW)) + TILES * lanes((TILES, TW))
    signed = jnp.where(frequency < H // 2, frequency, frequency - H).astype(F32)
    centre = (YB * here - ANG * YB // 2).astype(F32) + (YB - 1) / 2.0
    row = sublanes((8, TW))
    for angle in range(ANG):
        turn = signed * (1.0 / H) * info[pl.ds(1, 1), pl.ds(angle, 1)]
        whole = centre * turn
        whole = 2.0 * math.pi * (whole - jnp.round(whole))
        half = math.pi * turn
        bases[angle, 0], bases[angle, 1] = jnp.cos(whole), jnp.sin(whole)
        power = (jnp.cos(half), jnp.sin(half))
        for level in range(5):
            bases[angle, 2 + 2 * level], bases[angle, 3 + 2 * level] = power
            power = times(power, power)

    def fill(angle, carry):
        for order in range(TILES):
            line = [
                tuple(
                    jnp.broadcast_to(bases[angle, 2 + 2 * level + part, pl.ds(order, 1), :], (8, TW))
                    for part in range(2)
                )
                for level in range(5)
            ]
            now = line[0]
            for level in range(3):
                ahead = times(now, line[1 + level])
                chosen = (row & (1 << level)) != 0
                now = tuple(jnp.where(chosen, new, old) for new, old in zip(ahead, now))
            later = times(now, line[4])
            cosines[angle, order, pl.ds(0, 8), :], sines[angle, order, pl.ds(0, 8), :] = now
            cosines[angle, order, pl.ds(8, 8), :], sines[angle, order, pl.ds(8, 8), :] = later
        return carry

    lax.fori_loop(0, ANG, fill, 0)


def flip8(value):
    row = sublanes(value.shape)
    value = pltpu.roll(value, 4, 0)
    value = jnp.where((row & 2) == 0, pltpu.roll(value, 6, 0), pltpu.roll(value, 2, 0))
    return jnp.where((row & 1) == 0, pltpu.roll(value, 7, 0), pltpu.roll(value, 1, 0))


def image_kernel(
    rows, bases, cosines, sines, turns, right_b, probe0, gathered, info, psi,
    image, probe_new, psi_new, turned_a, turned_b, spread_a, spread_b, middle_a, middle_b, ready, sems,
):
    number = info[pl.ds(0, 1), pl.ds(0, 1)]
    for chunk in range(ANG):
        part, start = divmod(chunk * CHUNK, PS)
        here = pl.ds(start, CHUNK)
        probe_new[part, here, :] = probe0[part, here, :] - PROBE_STEP * gathered[chunk] / number
    psi_new[...] = psi[...]

    def shear(z, turned, spread):
        for angle in range(ANG):
            value = (rows[angle, z, :, pl.ds(0, TW)], rows[angle, z, :, pl.ds(TW, TW)])
            turned[angle, 0], turned[angle, 1] = times(value, (bases[angle, 0], bases[angle, 1]))
        for order in range(TILES):
            sums = None
            for angle in range(ANG):
                real = jnp.broadcast_to(turned[angle, 0, pl.ds(order, 1), :], (16, TW))
                imag = jnp.broadcast_to(turned[angle, 1, pl.ds(order, 1), :], (16, TW))
                cosine, sine = cosines[angle, order], sines[angle, order]
                terms = (real * cosine, imag * sine, real * sine, imag * cosine)
                sums = terms if sums is None else tuple(s + t for s, t in zip(sums, terms))
            rc, isn, rs, ic = sums
            above = (rc - isn, rs + ic)
            below = (rc + isn, ic - rs)
            for part in range(2):
                back = jnp.concatenate([flip8(below[part][8:]), flip8(below[part][:8])], axis=0)
                value = jnp.concatenate([back, above[part]], axis=0)
                high, low = split(value)
                here = pl.ds(order * YB, YB)
                spread[here, pl.ds(part * TW, TW)] = high
                spread[here, pl.ds((2 + part) * TW, TW)] = low
                spread[here, pl.ds((4 + part) * TW, TW)] = high

    def finish(slot, spread, middle):
        middle[...] = jnp.dot(spread[...], right_b[...], preferred_element_type=F32)
        for group in range(YB // 16):
            items = []
            for order in range(TILES):
                here = pl.ds(order * YB + 16 * group, 16)
                value = (middle[here, pl.ds(0, TW)], middle[here, pl.ds(TW, TW)])
                turn = (turns[0, pl.ds(order, 1), :], turns[1, pl.ds(order, 1), :])
                items.append(times(value, turn))
            for tile, item in enumerate(sixteen(items, 1)):
                for part in range(2):
                    ready[slot, part, pl.ds(16 * group, 16), pl.ds(tile * TW, TW)] = item[part].astype(BF16)

    def put(slot, z):
        return [
            pltpu.make_async_copy(ready.at[slot, part], image.at[part, z], sems.at[slot, part]) for part in range(2)
        ]

    def step(pair, carry):
        base = 2 * lax.rem(pair, 2)

        @pl.when(pair > 1)
        def _():
            for odd in range(2):
                for copy in put(base + odd, 2 * pair - 4 + odd):
                    copy.wait()

        shear(2 * pair + 1, turned_b, spread_b)
        finish(base, spread_a, middle_a)
        shear(2 * pair + 2, turned_a, spread_a)
        finish(base + 1, spread_b, middle_b)
        for odd in range(2):
            for copy in put(base + odd, 2 * pair + odd):
                copy.start()
        return carry

    shear(0, turned_a, spread_a)
    lax.fori_loop(0, ZS // 2 - 1, step, 0)
    for odd in range(2):
        for copy in put(odd, ZS - 6 + odd):
            copy.wait()
    shear(ZS - 1, turned_b, spread_b)
    finish(0, spread_a, middle_a)
    for copy in put(0, ZS - 2):
        copy.start()
    finish(1, spread_b, middle_b)
    for copy in put(1, ZS - 1):
        copy.start()
    for slot, z in ((2, ZS - 4), (3, ZS - 3), (0, ZS - 2), (1, ZS - 1)):
        for copy in put(slot, z):
            copy.wait()


def arr(*shape):
    return jax.ShapeDtypeStruct(shape, F32)


def dma(*shape):
    return pltpu.SemaphoreType.DMA(shape)


def call(kernel, outs, specs, out_specs, scratch, ident=None):
    extra = {} if ident is None else {"collective_id": ident, "has_side_effects": True}
    return pl.pallas_call(
        kernel,
        out_shape=outs,
        in_specs=specs,
        out_specs=out_specs,
        scratch_shapes=scratch,
        compiler_params=pltpu.CompilerParams(vmem_limit_bytes=VLIMIT, **extra),
    )


def shards(psi, target, probe, data, pos_z, pos_x, counts, shears):
    psi, target = psi.reshape(2, ROWS, TW), target.reshape(2, ROWS, TW)
    data = data.reshape(CAP, PS, PS)
    unit = dft_block(PS, 1.0 / math.sqrt(PS))
    tables = [
        jnp.asarray(t)
        for t in (right_table(unit), left_table(unit.T), left_table(unit), right_table(unit.T))
    ]
    wide, edge, small = arr(2, 2, ROWS, TW), arr(2, ROWS, TW), arr(8, TW)
    chunks, square = arr(ANG, CHUNK, TW), arr(2, PS, PS)
    table_shapes = [jax.ShapeDtypeStruct(t.shape, t.dtype) for t in tables]
    one = lambda *shape: pltpu.VMEM(shape, F32)

    outs = [wide, edge, edge, small, square, arr(CAP, PS, PS)] + table_shapes
    ext, goal, packs, info, probe, data, *tables = call(
        halo_kernel,
        outs,
        [SMEM] * 2 + [HBM] * 8,
        [VMEM] * len(outs),
        [
            one(2, ROWS, TW), one(2, ROWS, TW), one(ROWS, TW), one(ROWS, TW),
            dma(2, 2), dma(8),
        ],
        0,
    )(counts, shears, *(pltpu.with_memory_space_constraint(x, pltpu.HBM) for x in (psi, target, probe, data, *tables)))

    def gradient(ext, probe):
        return call(
            gradient_kernel, [wide, chunks, edge], [SMEM] * 3 + [VMEM] * 7, [VMEM] * 3, [one(2 * PS, PS)]
        )(counts, pos_z, pos_x, ext, probe, data, *tables)

    grad, parts, rims = gradient(ext, probe)
    ext, probe, info, info_all = call(
        exchange_kernel,
        [wide, square, small, small],
        [VMEM] * 7,
        [VMEM] * 4,
        [
            one(2, ROWS, TW), one(2, ROWS, TW), one(ROWS, TW), one(ROWS, TW),
            one(ANG, CHUNK, TW), one(CHUNK, TW), one(TILES, CHUNK, TW), one(CHUNK, TW), one(ANG, CHUNK, TW), one(ANG, 8, TW), one(TILES, 8, TW),
            dma(2, 2), dma(2, 2), dma(2, ANG), dma(2, TILES), dma(2, ANG), dma(2, ANG), dma(2, TILES),
        ],
        1,
    )(grad, parts, packs, info, ext, goal, probe)
    grad, parts, rims = gradient(ext, probe)
    every, phases = arr(ANG, ZS, TILES, WIDE), arr(ANG, TILES, 16, TW)
    psi_new, every, gathered, bases, cosines, sines = call(
        tail_kernel,
        [edge, every, chunks, arr(ANG, 12, TILES, TW), phases, phases],
        [VMEM] * 8,
        [VMEM] * 6,
        [
            one(ROWS, TW), one(ROWS, TW),
            one(ANG, CHUNK, TW), one(CHUNK, TW), one(TILES, CHUNK, TW), one(CHUNK, TW),
            one(TILES, 4 * FIRST, TW), one(TILES, 4 * (ZS - FIRST), TW),
            one(TILES, 4 * FIRST, TW), one(TILES, 4 * (ZS - FIRST), TW),
            one(PS, WIDE), one(PS, WIDE), one(ZS, TILES, WIDE),
            dma(2, 2), dma(2, ANG), dma(2, TILES), dma(2, ANG), dma(2, TILES), dma(2, TILES), dma(2, 13),
        ],
        2,
    )(ext, goal, grad, rims, parts, info, jnp.asarray(turn_table(-1)), jnp.asarray(right_table(dft_block(TW, 1.0))))
    inverse = dft_block(TW, 1.0 / (H * ANG)).T
    image, probe_new, psi_new = call(
        image_kernel,
        [jax.ShapeDtypeStruct((2, ZS, YB, H), BF16), square, edge],
        [VMEM] * 10,
        [HBM, VMEM, VMEM],
        [
            one(ANG, 2, TILES, TW),
            one(ANG, 2, TILES, TW),
            pltpu.VMEM((TILES * YB, 3 * WIDE), BF16),
            pltpu.VMEM((TILES * YB, 3 * WIDE), BF16),
            one(TILES * YB, WIDE),
            one(TILES * YB, WIDE),
            pltpu.VMEM((4, 2, YB, H), BF16),
            dma(4, 2),
        ],
    )(
        every, bases, cosines, sines, jnp.asarray(turn_table(1)), jnp.asarray(right_table(inverse)),
        probe, gathered, info_all, psi_new,
    )
    return psi_new.reshape(2, 1, ROWS, TW), probe_new, image


def solution(mesh):
    in_specs = (
        P(None, "angle", None, "tile"),
        P(None, "angle", None, "tile"),
        P(),
        P("angle", "tile", None, None, None),
        P("angle", "tile", None),
        P("angle", "tile", None),
        P("angle", "tile"),
        P("angle"),
    )
    out_specs = (P(None, "angle", None, "tile"), P(), P(None, "tile", "angle", None))
    return jax.shard_map(shards, mesh=mesh, in_specs=in_specs, out_specs=out_specs, check_vma=False)
```

```python
import functools
import math

import jax
import jax.numpy as jnp
import numpy as np
from jax import lax
from jax.experimental import pallas as pl
from jax.experimental.pallas import tpu as pltpu
from jax.sharding import PartitionSpec as P

ITERS = 2
ALPHA = 0.004
RHO = 5.0
PROBE_STEP = 0.02

ANG = 8
TILES = 16
PS = 128
TW = 128
ROWS = 160
CAP = 16
HALF = 64
WIDE = 256
ZS = ROWS // TILES
YB = 32
H = 2048
CHUNK = 2 * PS // ANG
GROUP = 8
FIRST = 4

F32 = jnp.float32
BF16 = jnp.bfloat16
MESH = pl.DeviceIdType.MESH
VMEM = pl.BlockSpec(memory_space=pltpu.VMEM)
SMEM = pl.BlockSpec(memory_space=pltpu.SMEM)
HBM = pl.BlockSpec(memory_space=pltpu.HBM)
VLIMIT = 20 * 1024 * 1024


def dft_block(length, scale):
    index = np.arange(length)
    turns = (index[:, None] * index[None, :]) % length
    angle = -2.0 * math.pi * turns / length
    real, imag = np.cos(angle) * scale, np.sin(angle) * scale
    return np.block([[real, imag], [-imag, real]])


def split_const(matrix):
    high = matrix.astype(BF16)
    low = (matrix - high.astype(np.float64)).astype(BF16)
    return high, low


def right_table(matrix):
    high, low = split_const(matrix)
    return np.concatenate([high, high, low], axis=0)


def left_table(matrix):
    high, low = split_const(matrix)
    return np.concatenate([high, high, low], axis=1)


def turn_table(orient):
    angle = orient * 2.0 * math.pi * np.arange(TILES)[:, None] * np.arange(TW)[None, :] / H
    return np.stack([np.cos(angle), np.sin(angle)]).astype(np.float32)


def split(value):
    high = value.astype(BF16)
    low = (value - high.astype(F32)).astype(BF16)
    return high, low


def dot_right(value, table):
    high, low = split(value)
    return jnp.dot(jnp.concatenate([high, low, high], axis=1), table, preferred_element_type=F32)


def dot_left(table, value):
    high, low = split(value)
    return jnp.dot(table, jnp.concatenate([high, low, high], axis=0), preferred_element_type=F32)


def times(left, right):
    return left[0] * right[0] - left[1] * right[1], left[0] * right[1] + left[1] * right[0]


def four(items, orient):
    (ar, ai), (br, bi), (cr, ci), (dr, di) = items
    sr, si, ur, ui = ar + cr, ai + ci, ar - cr, ai - ci
    pr, pi, qr, qi = br + dr, bi + di, br - dr, bi - di
    first = (sr + pr, si + pi)
    third = (sr - pr, si - pi)
    plus = (ur - qi, ui + qr)
    minus = (ur + qi, ui - qr)
    return [first, plus, third, minus] if orient > 0 else [first, minus, third, plus]


def turn_by(value, step, orient):
    real, imag = value
    if orient < 0:
        real, imag = imag, real
    if step == 4:
        real, imag = -imag, real
    elif step == 2:
        real, imag = (real - imag) * math.sqrt(0.5), (real + imag) * math.sqrt(0.5)
    elif step == 6:
        real, imag = (real + imag) * -math.sqrt(0.5), (real - imag) * math.sqrt(0.5)
    else:
        angle = 2.0 * math.pi * step / 16
        real, imag = times((real, imag), (math.cos(angle), math.sin(angle)))
    return (imag, real) if orient < 0 else (real, imag)


def sixteen(items, orient):
    columns = []
    for fine in range(4):
        partial = four([items[4 * coarse + fine] for coarse in range(4)], orient)
        for order in range(1, 4):
            step = fine * order
            if step:
                partial[order] = turn_by(partial[order], step, orient)
        columns.append(partial)
    result = [None] * 16
    for low in range(4):
        finished = four([columns[fine][low] for fine in range(4)], orient)
        for high in range(4):
            result[low + 4 * high] = finished[high]
    return result


def lanes(shape):
    return lax.broadcasted_iota(jnp.int32, shape, len(shape) - 1)


def sublanes(shape):
    return lax.broadcasted_iota(jnp.int32, shape, len(shape) - 2)


def place():
    return lax.axis_index("angle"), lax.axis_index("tile")


def greet(peers):
    barrier = pltpu.get_barrier_semaphore()
    for peer in peers:
        pl.semaphore_signal(barrier, inc=1, device_id=peer, device_id_type=MESH)
    return lambda: pl.semaphore_wait(barrier, len(peers))


def send(source, target, sems, slot, peer):
    copy = pltpu.make_async_remote_copy(
        src_ref=source,
        dst_ref=target,
        send_sem=sems.at[0, slot],
        recv_sem=sems.at[1, slot],
        device_id=peer,
        device_id_type=MESH,
    )
    copy.start()
    return copy


def greet_line(angle, tile):
    barrier = pltpu.get_barrier_semaphore()
    sides = ((tile > 0, tile - 1), (tile < TILES - 1, tile + 1))
    for inside, peer in sides:

        @pl.when(inside)
        def _():
            pl.semaphore_signal(barrier, inc=1, device_id=(angle, peer), device_id_type=MESH)

    inner = jnp.logical_and(tile > 0, tile < TILES - 1)

    def wait():
        @pl.when(inner)
        def _():
            pl.semaphore_wait(barrier, 2)

        @pl.when(jnp.logical_not(inner))
        def _():
            pl.semaphore_wait(barrier, 1)

    return wait


OPPOSITE = (4, 3, 5, 2, 6, 1, 7)


def angle_peers(angle, tile):
    return [((angle + step) % ANG, tile) for step in OPPOSITE]


FARTHEST = sorted(range(1, TILES), key=lambda s: -(min(s // 4, 4 - s // 4) + min(s % 4, 4 - s % 4)))


def shifted(tile, step):
    return (tile // 4 + step // 4) % 4 * 4 + (tile % 4 + step % 4) % 4


def tile_peers(angle, tile):
    return [(angle, shifted(tile, step)) for step in FARTHEST]


def neighbours(angle, tile):
    return (angle, (tile + TILES - 1) % TILES), (angle, (tile + 1) % TILES)


def start_edges(packs, from_left, from_right, sems, angle, tile):
    def copy(side, landing, peer):
        return pltpu.make_async_remote_copy(
            src_ref=packs.at[side],
            dst_ref=landing,
            send_sem=sems.at[0, side],
            recv_sem=sems.at[1, side],
            device_id=peer,
            device_id_type=MESH,
        )

    left, right = neighbours(angle, tile)
    to_left, to_right = copy(0, from_right, left), copy(1, from_left, right)

    @pl.when(tile > 0)
    def _():
        to_left.start()

    @pl.when(tile < TILES - 1)
    def _():
        to_right.start()

    return to_left, to_right


def finish_edges(copies, tile):
    to_left, to_right = copies

    @pl.when(tile > 0)
    def _():
        to_left.wait_send()
        to_right.wait_recv()

    @pl.when(tile < TILES - 1)
    def _():
        to_right.wait_send()
        to_left.wait_recv()


def clear_edges(from_left, from_right, tile):
    @pl.when(tile == 0)
    def _():
        from_left[...] = jnp.zeros_like(from_left)

    @pl.when(tile == TILES - 1)
    def _():
        from_right[...] = jnp.zeros_like(from_right)


def start_first(parts, landed, sems, angle, tile):
    return [
        send(parts.at[(angle + step) % ANG], landed.at[step], sems, step, ((angle + step) % ANG, tile))
        for step in OPPOSITE
    ]


def finish_first(copies, parts, landed, angle):
    for copy in copies:
        copy.wait()
    total = parts[angle]
    for step in range(1, ANG):
        total = total + landed[step]
    return total


def start_second(source, landed, sems, angle, tile):
    return [
        send(source, landed.at[tile], sems, step, (angle, shifted(tile, step)))
        for step in FARTHEST
    ]


def finish_second(copies, source, landed, tile):
    landed[tile] = source[...]
    for copy in copies:
        copy.wait()
    total = landed[0]
    for index in range(1, TILES):
        total = total + landed[index]
    return total


def start_third(source, gathered, sems, angle, tile):
    return [
        send(source, gathered.at[angle], sems, step, ((angle + step) % ANG, tile))
        for step in OPPOSITE
    ]


def packed_sides(real, imag):
    low = lanes((ROWS, TW)) < HALF
    return (
        jnp.where(low, real, pltpu.roll(imag, HALF, 1)),
        jnp.where(low, pltpu.roll(real, HALF, 1), imag),
    )


def widened(real, imag, before, after):
    low = lanes((ROWS, TW)) < HALF
    real, imag = pltpu.roll(real, HALF, 1), pltpu.roll(imag, HALF, 1)
    return (
        (jnp.where(low, before, real), jnp.where(low, pltpu.roll(before, HALF, 1), imag)),
        (jnp.where(low, real, pltpu.roll(after, HALF, 1)), jnp.where(low, imag, after)),
    )


def halo_kernel(
    counts, shears, psi, target, probe, data, *refs,
):
    tables, refs = refs[:4], refs[4:]
    ext, own_target, packs, info, probe_here, data_here, *refs = refs
    tables_here, refs = refs[:4], refs[4:]
    own, sides, from_left, from_right, edge_sems, local_sems = refs
    angle, tile = place()
    fetches = [
        pltpu.make_async_copy(source, here, local_sems.at[index])
        for index, (source, here) in enumerate(
            zip((psi, target, probe, data) + tables, (own, own_target, probe_here, data_here) + tuple(tables_here))
        )
    ]
    for fetch in fetches:
        fetch.start()
    clear_edges(from_left, from_right, tile)
    met = greet_line(angle, tile)
    row, lane = sublanes((8, TW)), lanes((8, TW))
    count = jnp.where((row == 0) & (lane == 0), counts[0, 0].astype(F32), 0.0)
    info[...] = jnp.where((row == 1) & (lane == angle), shears[0], count)
    fetches[0].wait()
    for side, value in enumerate(packed_sides(own[0], own[1])):
        sides[side] = value
    met()
    edges = start_edges(sides, from_left, from_right, edge_sems, angle, tile)
    fetches[1].wait()
    for side, value in enumerate(packed_sides(own_target[0], own_target[1])):
        packs[side] = value
    for fetch in fetches[2:]:
        fetch.wait()
    finish_edges(edges, tile)
    for side, pair in enumerate(widened(own[0], own[1], from_left[...], from_right[...])):
        for part in range(2):
            ext[side, part] = pair[part]


def exchange_kernel(
    grad, parts, packs, info, ext0, own_target, probe0, ext, probe, info_some, info_all,
    from_left, from_right, goal_left, goal_right, landed_first, first_sum, landed_second, second_sum, gathered, landed_some, landed_info,
    edge_sems, goal_sems, first_sems, second_sems, third_sems, some_sems, info_sems,
):
    angle, tile = place()
    clear_edges(from_left, from_right, tile)
    clear_edges(goal_left, goal_right, tile)
    greet(tile_peers(angle, tile) + angle_peers(angle, tile))()
    first = start_first(parts, landed_first, first_sems, angle, tile)
    edges = start_edges(grad, from_left, from_right, edge_sems, angle, tile)
    some = [
        send(info, landed_some.at[step], some_sems, step, ((angle + step) % ANG, tile)) for step in OPPOSITE
    ]
    first_sum[...] = finish_first(first, parts, landed_first, angle)
    second = start_second(first_sum, landed_second, second_sems, angle, tile)
    for copy in some:
        copy.wait()
    total = info[...]
    for step in range(1, ANG):
        total = total + landed_some[step]
    info_some[...] = total
    infos = start_second(info_some, landed_info, info_sems, angle, tile)
    goals = start_edges(packs, goal_left, goal_right, goal_sems, angle, tile)
    second_sum[...] = finish_second(second, first_sum, landed_second, tile)
    third = start_third(second_sum, gathered, third_sems, angle, tile)
    finish_edges(edges, tile)
    finish_edges(goals, tile)
    low = lanes((ROWS, TW)) < HALF
    inner, outer = tile > 0, tile < TILES - 1
    goal = widened(own_target[0], own_target[1], goal_left[...], goal_right[...])
    for side, landed, inside in ((0, from_left, inner), (1, from_right, outer)):
        for part in range(2):
            total = grad[side, part] + landed[part]
            old = ext0[side, part]
            new = old - ALPHA * (total + RHO * (old - goal[side][part]))
            keep = jnp.logical_or(inside, jnp.logical_not(low) if side == 0 else low)
            ext[side, part] = jnp.where(keep, new, 0.0)
    gathered[angle] = second_sum[...]
    info_all[...] = finish_second(infos, info_some, landed_info, tile)
    number = info_all[pl.ds(0, 1), pl.ds(0, 1)]
    for copy in third:
        copy.wait()
    for chunk in range(ANG):
        part, start = divmod(chunk * CHUNK, PS)
        here = pl.ds(start, CHUNK)
        probe[part, here, :] = probe0[part, here, :] - PROBE_STEP * gathered[chunk] / number


def tail_kernel(
    ext, own_target, grad, rims, parts, info, turns, right_f,
    psi_new, every, gathered, bases, cosines, sines,
    from_left, from_right, landed_first, first_sum, landed_second, second_sum,
    slabs_one, slabs_two, here_one, here_two, work_one, work_two, rows,
    edge_sems, first_sems, second_sems, third_sems, one_sems, two_sems, row_sems,
):
    angle, tile = place()
    clear_edges(from_left, from_right, tile)
    met = greet(tile_peers(angle, tile) + angle_peers(angle, tile))
    low = lanes((ROWS, TW)) < HALF
    for part in range(2):
        old, total = (
            jnp.where(low, pltpu.roll(wide[0, part], HALF, 1), pltpu.roll(wide[1, part], HALF, 1))
            for wide in (ext, grad)
        )
        new = old - ALPHA * (total + RHO * (old - own_target[part]))
        psi_new[part] = new
        for source, place_at in ((own_target[part] - new, part), (rims[part], 2 + part)):
            for slab in range(TILES):
                for slabs, first, count in ((slabs_one, 0, FIRST), (slabs_two, FIRST, ZS - FIRST)):
                    start = slab * ZS + first
                    slabs[slab, pl.ds(place_at * count, count), :] = source[start : start + count]
    work_one[...] = jnp.zeros_like(work_one)
    work_two[...] = jnp.zeros_like(work_two)
    met()
    halves = []
    for slabs, landed, sems in ((slabs_one, here_one, one_sems), (slabs_two, here_two, two_sems)):
        copies = []
        for step in FARTHEST:
            owner = shifted(tile, step)
            copies.append(send(slabs.at[owner], landed.at[tile], sems, step, (angle, owner)))
        halves.append(copies)
    first = start_first(parts, landed_first, first_sems, angle, tile)
    for slabs, landed in ((slabs_one, here_one), (slabs_two, here_two)):
        landed[tile] = slabs[tile]
    first_sum[...] = finish_first(first, parts, landed_first, angle)
    second = start_second(first_sum, landed_second, second_sems, angle, tile)

    def spectrum(copies, landed, work, start, count):
        for copy in copies:
            copy.wait()
        low = lanes((count, TW)) < HALF
        zero = jnp.zeros((count, TW), F32)
        items = []
        for index in range(TILES):
            before = landed[index - 1, pl.ds(3 * count, count), :] if index else zero
            after = landed[index + 1, pl.ds(2 * count, count), :] if index < TILES - 1 else zero
            real = jnp.where(low, before, pltpu.roll(after, HALF, 1))
            imag = jnp.where(low, pltpu.roll(before, HALF, 1), after)
            items.append(
                (
                    landed[index, pl.ds(0, count), :] + ALPHA * real,
                    landed[index, pl.ds(count, count), :] + ALPHA * imag,
                )
            )
        for order, item in enumerate(sixteen(items, -1)):
            turn = (turns[0, pl.ds(order, 1), :], turns[1, pl.ds(order, 1), :])
            real, imag = times(item, turn)
            work[pl.ds(8 * order, count), pl.ds(0, TW)] = real
            work[pl.ds(8 * order, count), pl.ds(TW, TW)] = imag
        result = dot_right(work[...], right_f[...])
        for order in range(TILES):
            rows[pl.ds(start, count), order, :] = result[8 * order : 8 * order + count]

    chip, core = angle // 2, angle % 2
    up, down, over = (chip + 1) % 4, (chip + 3) % 4, (chip + 2) % 4
    upper, lower, across = 2 * up + core, 2 * down + core, 2 * over + core
    above, below, beside = (upper, tile), (lower, tile), (2 * chip + 1 - core, tile)
    one, two = pl.ds(0, FIRST), pl.ds(FIRST, ZS - FIRST)
    spectrum(halves[0], here_one, work_one, 0, FIRST)

    def spread(part, slot):
        peers = ((across, 0), (upper, 1), (lower, 2))
        return [
            send(rows.at[part], every.at[angle, part], row_sems, slot + index, (peer, tile)) for peer, index in peers
        ]

    sent_one = spread(one, 0)
    spectrum(halves[1], here_two, work_two, FIRST, ZS - FIRST)
    sent_two = spread(two, 3)
    side = send(rows, every.at[angle], row_sems, 12, beside)
    edges = start_edges(rims, from_left, from_right, edge_sems, angle, tile)
    every[angle] = rows[...]
    second_sum[...] = finish_second(second, first_sum, landed_second, tile)
    third = [
        send(second_sum, gathered.at[angle], third_sems, slot, (peer, tile))
        for slot, peer in enumerate((across, upper, lower))
    ]
    handed = [side, send(second_sum, gathered.at[angle], third_sems, 3, beside)]
    gathered[angle] = second_sum[...]
    phase_tables(info, bases, cosines, sines, angle)

    def hand(copies, target, sems, slot):
        for index, source in ((1, lower), (2, upper), (0, across)):
            copies[index].wait()
            landed = target(source)
            handed.append(send(landed, landed, sems, slot + index, beside))

    hand(sent_one, lambda source: every.at[source, one], row_sems, 6)
    hand(third, lambda source: gathered.at[source], third_sems, 4)
    finish_edges(edges, tile)
    for part in range(2):
        before, after = from_left[...], from_right[...]
        low = lanes((ROWS, TW)) < HALF
        if part == 0:
            extra = jnp.where(low, before, pltpu.roll(after, HALF, 1))
        else:
            extra = jnp.where(low, pltpu.roll(before, HALF, 1), after)
        psi_new[part] = psi_new[part] - ALPHA * extra
    hand(sent_two, lambda source: every.at[source, two], row_sems, 9)
    for copy in handed:
        copy.wait()


def gradient_kernel(
    counts, pos_z, pos_x, ext, probe, data, right_f, left_f, left_b, right_b, grad, parts, rims, probe_acc,
):
    count = counts[0, 0]
    grad[...] = jnp.zeros_like(grad)
    probe_acc[...] = jnp.zeros_like(probe_acc)
    lane = lanes((PS, TW))

    def sheet(values, axis):
        return jnp.concatenate(values, axis=axis)

    def group(index, carry):
        probe_real, probe_imag = probe[0], probe[1]
        rows, windows, spots = [], [], []
        for offset in range(GROUP):
            slot = GROUP * index + offset
            start_z, start_x = pos_z[0, 0, slot], pos_x[0, 0, slot]
            back = lax.rem(TW - start_x, TW)
            here = pl.ds(start_z, PS)
            real, imag = (
                pltpu.roll(jnp.where(lane >= start_x, ext[0, part, here, :], ext[1, part, here, :]), back, 1)
                for part in range(2)
            )
            windows.append((real, imag))
            spots.append((slot, start_z, start_x))
            rows.append(sheet(times((probe_real, probe_imag), (real, imag)), 1))
        pairs = range(0, GROUP, 2)
        sides = (slice(0, PS), slice(PS, 2 * PS))
        turned = [dot_right(sheet(rows[p : p + 4], 0), right_f[...]) for p in range(0, GROUP, 4)]
        turned = [v[k] for v in turned for k in (slice(0, 2 * PS), slice(2 * PS, 4 * PS))]
        turned = [sheet([sheet([v[k, :PS], v[k, PS:]], 0) for k in sides], 1) for v in turned]
        far = [dot_left(left_f[...], v) for v in turned]
        weighted = []
        for s in range(GROUP):
            slot = spots[s][0]
            far_real, far_imag = (far[s // 2][k, sides[s % 2]] for k in sides)
            live = jnp.where(slot < count, 1.0, 0.0).astype(F32)
            misfit = (far_real * far_real + far_imag * far_imag - data[slot]) * live
            weighted.append(sheet([misfit * far_real, misfit * far_imag], 0))
        turned = [dot_left(left_b[...], sheet(weighted[p : p + 2], 1)) for p in pairs]
        turned = [sheet([sheet([v[:PS, k], v[PS:, k]], 1) for k in sides], 0) for v in turned]
        chi = [dot_right(sheet(turned[p : p + 2], 0), right_b[...]) for p in range(0, GROUP // 2, 2)]
        chi = [v[k] for v in chi for k in (slice(0, 2 * PS), slice(2 * PS, 4 * PS))]
        for s in range(GROUP):
            slot, start_z, start_x = spots[s]
            here = pl.ds(start_z, PS)
            chi_real, chi_imag = (chi[s // 2][sides[s % 2], k] for k in sides)
            real, imag = windows[s]
            probe_acc[pl.ds(0, PS), :] += real * chi_real + imag * chi_imag
            probe_acc[pl.ds(PS, PS), :] += real * chi_imag - imag * chi_real
            grad_real = probe_real * chi_real + probe_imag * chi_imag
            grad_imag = probe_real * chi_imag - probe_imag * chi_real
            for part, value in ((0, grad_real), (1, grad_imag)):
                moved = pltpu.roll(value, start_x, 1)
                grad[0, part, here, :] += jnp.where(lane >= start_x, moved, 0.0)
                grad[1, part, here, :] += jnp.where(lane < start_x, moved, 0.0)
        return carry

    lax.fori_loop(0, (count + GROUP - 1) // GROUP, group, 0)
    for chunk in range(ANG):
        parts[chunk] = probe_acc[pl.ds(chunk * CHUNK, CHUNK), :]
    low = lanes((ROWS, TW)) < HALF
    rims[0] = jnp.where(low, grad[0, 0], pltpu.roll(grad[0, 1], HALF, 1))
    rims[1] = jnp.where(low, pltpu.roll(grad[1, 0], HALF, 1), grad[1, 1])


def phase_tables(info, bases, cosines, sines, here):
    frequency = sublanes((TILES, TW)) + TILES * lanes((TILES, TW))
    signed = jnp.where(frequency < H // 2, frequency, frequency - H).astype(F32)
    centre = (YB * here - ANG * YB // 2).astype(F32) + (YB - 1) / 2.0
    row = sublanes((8, TW))
    for angle in range(ANG):
        turn = signed * (1.0 / H) * info[pl.ds(1, 1), pl.ds(angle, 1)]
        whole = centre * turn
        whole = 2.0 * math.pi * (whole - jnp.round(whole))
        half = math.pi * turn
        bases[angle, 0], bases[angle, 1] = jnp.cos(whole), jnp.sin(whole)
        power = (jnp.cos(half), jnp.sin(half))
        for level in range(5):
            bases[angle, 2 + 2 * level], bases[angle, 3 + 2 * level] = power
            power = times(power, power)

    def fill(angle, carry):
        for order in range(TILES):
            line = [
                tuple(
                    jnp.broadcast_to(bases[angle, 2 + 2 * level + part, pl.ds(order, 1), :], (8, TW))
                    for part in range(2)
                )
                for level in range(5)
            ]
            now = line[0]
            for level in range(3):
                ahead = times(now, line[1 + level])
                chosen = (row & (1 << level)) != 0
                now = tuple(jnp.where(chosen, new, old) for new, old in zip(ahead, now))
            later = times(now, line[4])
            cosines[angle, order, pl.ds(0, 8), :], sines[angle, order, pl.ds(0, 8), :] = now
            cosines[angle, order, pl.ds(8, 8), :], sines[angle, order, pl.ds(8, 8), :] = later
        return carry

    lax.fori_loop(0, ANG, fill, 0)


def flip8(value):
    row = sublanes(value.shape)
    value = pltpu.roll(value, 4, 0)
    value = jnp.where((row & 2) == 0, pltpu.roll(value, 6, 0), pltpu.roll(value, 2, 0))
    return jnp.where((row & 1) == 0, pltpu.roll(value, 7, 0), pltpu.roll(value, 1, 0))


def image_kernel(
    rows, bases, cosines, sines, turns, right_b, probe0, gathered, info, psi,
    image, probe_new, psi_new, turned_a, turned_b, spread_a, spread_b, middle_a, middle_b, ready, sems,
):
    number = info[pl.ds(0, 1), pl.ds(0, 1)]
    for chunk in range(ANG):
        part, start = divmod(chunk * CHUNK, PS)
        here = pl.ds(start, CHUNK)
        probe_new[part, here, :] = probe0[part, here, :] - PROBE_STEP * gathered[chunk] / number
    psi_new[...] = psi[...]

    def shear(z, turned, spread):
        for angle in range(ANG):
            value = (rows[angle, z, :, pl.ds(0, TW)], rows[angle, z, :, pl.ds(TW, TW)])
            turned[angle, 0], turned[angle, 1] = times(value, (bases[angle, 0], bases[angle, 1]))
        for order in range(TILES):
            sums = None
            for angle in range(ANG):
                real = jnp.broadcast_to(turned[angle, 0, pl.ds(order, 1), :], (16, TW))
                imag = jnp.broadcast_to(turned[angle, 1, pl.ds(order, 1), :], (16, TW))
                cosine, sine = cosines[angle, order], sines[angle, order]
                terms = (real * cosine, imag * sine, real * sine, imag * cosine)
                sums = terms if sums is None else tuple(s + t for s, t in zip(sums, terms))
            rc, isn, rs, ic = sums
            above = (rc - isn, rs + ic)
            below = (rc + isn, ic - rs)
            for part in range(2):
                back = jnp.concatenate([flip8(below[part][8:]), flip8(below[part][:8])], axis=0)
                value = jnp.concatenate([back, above[part]], axis=0)
                high, low = split(value)
                here = pl.ds(order * YB, YB)
                spread[here, pl.ds(part * TW, TW)] = high
                spread[here, pl.ds((2 + part) * TW, TW)] = low
                spread[here, pl.ds((4 + part) * TW, TW)] = high

    def finish(slot, spread, middle):
        middle[...] = jnp.dot(spread[...], right_b[...], preferred_element_type=F32)
        for group in range(YB // 16):
            items = []
            for order in range(TILES):
                here = pl.ds(order * YB + 16 * group, 16)
                value = (middle[here, pl.ds(0, TW)], middle[here, pl.ds(TW, TW)])
                turn = (turns[0, pl.ds(order, 1), :], turns[1, pl.ds(order, 1), :])
                items.append(times(value, turn))
            for tile, item in enumerate(sixteen(items, 1)):
                for part in range(2):
                    ready[slot, part, pl.ds(16 * group, 16), pl.ds(tile * TW, TW)] = item[part].astype(BF16)

    def put(slot, z):
        return [
            pltpu.make_async_copy(ready.at[slot, part], image.at[part, z], sems.at[slot, part]) for part in range(2)
        ]

    def step(pair, carry):
        base = 2 * lax.rem(pair, 2)

        @pl.when(pair > 1)
        def _():
            for odd in range(2):
                for copy in put(base + odd, 2 * pair - 4 + odd):
                    copy.wait()

        shear(2 * pair + 1, turned_b, spread_b)
        finish(base, spread_a, middle_a)
        shear(2 * pair + 2, turned_a, spread_a)
        finish(base + 1, spread_b, middle_b)
        for odd in range(2):
            for copy in put(base + odd, 2 * pair + odd):
                copy.start()
        return carry

    shear(0, turned_a, spread_a)
    lax.fori_loop(0, ZS // 2 - 1, step, 0)
    for odd in range(2):
        for copy in put(odd, ZS - 6 + odd):
            copy.wait()
    shear(ZS - 1, turned_b, spread_b)
    finish(0, spread_a, middle_a)
    for copy in put(0, ZS - 2):
        copy.start()
    finish(1, spread_b, middle_b)
    for copy in put(1, ZS - 1):
        copy.start()
    for slot, z in ((2, ZS - 4), (3, ZS - 3), (0, ZS - 2), (1, ZS - 1)):
        for copy in put(slot, z):
            copy.wait()


def arr(*shape):
    return jax.ShapeDtypeStruct(shape, F32)


def dma(*shape):
    return pltpu.SemaphoreType.DMA(shape)


def call(kernel, outs, specs, out_specs, scratch, ident=None):
    extra = {} if ident is None else {"collective_id": ident, "has_side_effects": True}
    return pl.pallas_call(
        kernel,
        out_shape=outs,
        in_specs=specs,
        out_specs=out_specs,
        scratch_shapes=scratch,
        compiler_params=pltpu.CompilerParams(vmem_limit_bytes=VLIMIT, **extra),
    )


def shards(psi, target, probe, data, pos_z, pos_x, counts, shears):
    psi, target = psi.reshape(2, ROWS, TW), target.reshape(2, ROWS, TW)
    data = data.reshape(CAP, PS, PS)
    unit = dft_block(PS, 1.0 / math.sqrt(PS))
    tables = [
        jnp.asarray(t)
        for t in (right_table(unit), left_table(unit.T), left_table(unit), right_table(unit.T))
    ]
    wide, edge, small = arr(2, 2, ROWS, TW), arr(2, ROWS, TW), arr(8, TW)
    chunks, square = arr(ANG, CHUNK, TW), arr(2, PS, PS)
    table_shapes = [jax.ShapeDtypeStruct(t.shape, t.dtype) for t in tables]
    one = lambda *shape: pltpu.VMEM(shape, F32)

    outs = [wide, edge, edge, small, square, arr(CAP, PS, PS)] + table_shapes
    ext, goal, packs, info, probe, data, *tables = call(
        halo_kernel,
        outs,
        [SMEM] * 2 + [HBM] * 8,
        [VMEM] * len(outs),
        [
            one(2, ROWS, TW), one(2, ROWS, TW), one(ROWS, TW), one(ROWS, TW),
            dma(2, 2), dma(8),
        ],
        0,
    )(counts, shears, *(pltpu.with_memory_space_constraint(x, pltpu.HBM) for x in (psi, target, probe, data, *tables)))

    def gradient(ext, probe):
        return call(
            gradient_kernel, [wide, chunks, edge], [SMEM] * 3 + [VMEM] * 7, [VMEM] * 3, [one(2 * PS, PS)]
        )(counts, pos_z, pos_x, ext, probe, data, *tables)

    grad, parts, rims = gradient(ext, probe)
    ext, probe, info, info_all = call(
        exchange_kernel,
        [wide, square, small, small],
        [VMEM] * 7,
        [VMEM] * 4,
        [
            one(2, ROWS, TW), one(2, ROWS, TW), one(ROWS, TW), one(ROWS, TW),
            one(ANG, CHUNK, TW), one(CHUNK, TW), one(TILES, CHUNK, TW), one(CHUNK, TW), one(ANG, CHUNK, TW), one(ANG, 8, TW), one(TILES, 8, TW),
            dma(2, 2), dma(2, 2), dma(2, ANG), dma(2, TILES), dma(2, ANG), dma(2, ANG), dma(2, TILES),
        ],
        1,
    )(grad, parts, packs, info, ext, goal, probe)
    grad, parts, rims = gradient(ext, probe)
    every, phases = arr(ANG, ZS, TILES, WIDE), arr(ANG, TILES, 16, TW)
    psi_new, every, gathered, bases, cosines, sines = call(
        tail_kernel,
        [edge, every, chunks, arr(ANG, 12, TILES, TW), phases, phases],
        [VMEM] * 8,
        [VMEM] * 6,
        [
            one(ROWS, TW), one(ROWS, TW),
            one(ANG, CHUNK, TW), one(CHUNK, TW), one(TILES, CHUNK, TW), one(CHUNK, TW),
            one(TILES, 4 * FIRST, TW), one(TILES, 4 * (ZS - FIRST), TW),
            one(TILES, 4 * FIRST, TW), one(TILES, 4 * (ZS - FIRST), TW),
            one(PS, WIDE), one(PS, WIDE), one(ZS, TILES, WIDE),
            dma(2, 2), dma(2, ANG), dma(2, TILES), dma(2, ANG), dma(2, TILES), dma(2, TILES), dma(2, 13),
        ],
        2,
    )(ext, goal, grad, rims, parts, info, jnp.asarray(turn_table(-1)), jnp.asarray(right_table(dft_block(TW, 1.0))))
    inverse = dft_block(TW, 1.0 / (H * ANG)).T
    image, probe_new, psi_new = call(
        image_kernel,
        [jax.ShapeDtypeStruct((2, ZS, YB, H), BF16), square, edge],
        [VMEM] * 10,
        [HBM, VMEM, VMEM],
        [
            one(ANG, 2, TILES, TW),
            one(ANG, 2, TILES, TW),
            pltpu.VMEM((TILES * YB, 3 * WIDE), BF16),
            pltpu.VMEM((TILES * YB, 3 * WIDE), BF16),
            one(TILES * YB, WIDE),
            one(TILES * YB, WIDE),
            pltpu.VMEM((4, 2, YB, H), BF16),
            dma(4, 2),
        ],
    )(
        every, bases, cosines, sines, jnp.asarray(turn_table(1)), jnp.asarray(right_table(inverse)),
        probe, gathered, info_all, psi_new,
    )
    return psi_new.reshape(2, 1, ROWS, TW), probe_new, image


def solution(mesh):
    in_specs = (
        P(None, "angle", None, "tile"),
        P(None, "angle", None, "tile"),
        P(),
        P("angle", "tile", None, None, None),
        P("angle", "tile", None),
        P("angle", "tile", None),
        P("angle", "tile"),
        P("angle"),
    )
    out_specs = (P(None, "angle", None, "tile"), P(), P(None, "tile", "angle", None))
    return jax.shard_map(shards, mesh=mesh, in_specs=in_specs, out_specs=out_specs, check_vma=False)
```

```python
import functools
import math

import jax
import jax.numpy as jnp
import numpy as np
from jax import lax
from jax.experimental import pallas as pl
from jax.experimental.pallas import tpu as pltpu
from jax.sharding import PartitionSpec as P

ITERS = 2
ALPHA = 0.004
RHO = 5.0
PROBE_STEP = 0.02

ANG = 8
TILES = 16
PS = 128
TW = 128
ROWS = 160
CAP = 16
HALF = 64
WIDE = 256
ZS = ROWS // TILES
YB = 32
H = 2048
CHUNK = 2 * PS // ANG
GROUP = 8
FIRST = 4

F32 = jnp.float32
BF16 = jnp.bfloat16
MESH = pl.DeviceIdType.MESH
VMEM = pl.BlockSpec(memory_space=pltpu.VMEM)
SMEM = pl.BlockSpec(memory_space=pltpu.SMEM)
HBM = pl.BlockSpec(memory_space=pltpu.HBM)
VLIMIT = 20 * 1024 * 1024


def dft_block(length, scale):
    index = np.arange(length)
    turns = (index[:, None] * index[None, :]) % length
    angle = -2.0 * math.pi * turns / length
    real, imag = np.cos(angle) * scale, np.sin(angle) * scale
    return np.block([[real, imag], [-imag, real]])


def split_const(matrix):
    high = matrix.astype(BF16)
    low = (matrix - high.astype(np.float64)).astype(BF16)
    return high, low


def right_table(matrix):
    high, low = split_const(matrix)
    return np.concatenate([high, high, low], axis=0)


def left_table(matrix):
    high, low = split_const(matrix)
    return np.concatenate([high, high, low], axis=1)


def turn_table(orient):
    angle = orient * 2.0 * math.pi * np.arange(TILES)[:, None] * np.arange(TW)[None, :] / H
    return np.stack([np.cos(angle), np.sin(angle)]).astype(np.float32)


def split(value):
    high = value.astype(BF16)
    low = (value - high.astype(F32)).astype(BF16)
    return high, low


def dot_right(value, table):
    high, low = split(value)
    return jnp.dot(jnp.concatenate([high, low, high], axis=1), table, preferred_element_type=F32)


def dot_left(table, value):
    high, low = split(value)
    return jnp.dot(table, jnp.concatenate([high, low, high], axis=0), preferred_element_type=F32)


def times(left, right):
    return left[0] * right[0] - left[1] * right[1], left[0] * right[1] + left[1] * right[0]


def four(items, orient):
    (ar, ai), (br, bi), (cr, ci), (dr, di) = items
    sr, si, ur, ui = ar + cr, ai + ci, ar - cr, ai - ci
    pr, pi, qr, qi = br + dr, bi + di, br - dr, bi - di
    first = (sr + pr, si + pi)
    third = (sr - pr, si - pi)
    plus = (ur - qi, ui + qr)
    minus = (ur + qi, ui - qr)
    return [first, plus, third, minus] if orient > 0 else [first, minus, third, plus]


def turn_by(value, step, orient):
    real, imag = value
    if orient < 0:
        real, imag = imag, real
    if step == 4:
        real, imag = -imag, real
    elif step == 2:
        real, imag = (real - imag) * math.sqrt(0.5), (real + imag) * math.sqrt(0.5)
    elif step == 6:
        real, imag = (real + imag) * -math.sqrt(0.5), (real - imag) * math.sqrt(0.5)
    else:
        angle = 2.0 * math.pi * step / 16
        real, imag = times((real, imag), (math.cos(angle), math.sin(angle)))
    return (imag, real) if orient < 0 else (real, imag)


def sixteen(items, orient):
    columns = []
    for fine in range(4):
        partial = four([items[4 * coarse + fine] for coarse in range(4)], orient)
        for order in range(1, 4):
            step = fine * order
            if step:
                partial[order] = turn_by(partial[order], step, orient)
        columns.append(partial)
    result = [None] * 16
    for low in range(4):
        finished = four([columns[fine][low] for fine in range(4)], orient)
        for high in range(4):
            result[low + 4 * high] = finished[high]
    return result


def lanes(shape):
    return lax.broadcasted_iota(jnp.int32, shape, len(shape) - 1)


def sublanes(shape):
    return lax.broadcasted_iota(jnp.int32, shape, len(shape) - 2)


def place():
    return lax.axis_index("angle"), lax.axis_index("tile")


def greet(peers):
    barrier = pltpu.get_barrier_semaphore()
    for peer in peers:
        pl.semaphore_signal(barrier, inc=1, device_id=peer, device_id_type=MESH)
    return lambda: pl.semaphore_wait(barrier, len(peers))


def send(source, target, sems, slot, peer):
    copy = pltpu.make_async_remote_copy(
        src_ref=source,
        dst_ref=target,
        send_sem=sems.at[0, slot],
        recv_sem=sems.at[1, slot],
        device_id=peer,
        device_id_type=MESH,
    )
    copy.start()
    return copy


def greet_line(angle, tile):
    barrier = pltpu.get_barrier_semaphore()
    sides = ((tile > 0, tile - 1), (tile < TILES - 1, tile + 1))
    for inside, peer in sides:

        @pl.when(inside)
        def _():
            pl.semaphore_signal(barrier, inc=1, device_id=(angle, peer), device_id_type=MESH)

    inner = jnp.logical_and(tile > 0, tile < TILES - 1)

    def wait():
        @pl.when(inner)
        def _():
            pl.semaphore_wait(barrier, 2)

        @pl.when(jnp.logical_not(inner))
        def _():
            pl.semaphore_wait(barrier, 1)

    return wait


def angle_peers(angle, tile):
    return [((angle + step) % ANG, tile) for step in range(1, ANG)]


FARTHEST = sorted(range(1, TILES), key=lambda s: -(min(s // 4, 4 - s // 4) + min(s % 4, 4 - s % 4)))


def shifted(tile, step):
    return (tile // 4 + step // 4) % 4 * 4 + (tile % 4 + step % 4) % 4


def tile_peers(angle, tile):
    return [(angle, shifted(tile, step)) for step in FARTHEST]


def neighbours(angle, tile):
    return (angle, (tile + TILES - 1) % TILES), (angle, (tile + 1) % TILES)


def start_edges(packs, from_left, from_right, sems, angle, tile):
    def copy(side, landing, peer):
        return pltpu.make_async_remote_copy(
            src_ref=packs.at[side],
            dst_ref=landing,
            send_sem=sems.at[0, side],
            recv_sem=sems.at[1, side],
            device_id=peer,
            device_id_type=MESH,
        )

    left, right = neighbours(angle, tile)
    to_left, to_right = copy(0, from_right, left), copy(1, from_left, right)

    @pl.when(tile > 0)
    def _():
        to_left.start()

    @pl.when(tile < TILES - 1)
    def _():
        to_right.start()

    return to_left, to_right


def finish_edges(copies, tile):
    to_left, to_right = copies

    @pl.when(tile > 0)
    def _():
        to_left.wait_send()
        to_right.wait_recv()

    @pl.when(tile < TILES - 1)
    def _():
        to_right.wait_send()
        to_left.wait_recv()


def clear_edges(from_left, from_right, tile):
    @pl.when(tile == 0)
    def _():
        from_left[...] = jnp.zeros_like(from_left)

    @pl.when(tile == TILES - 1)
    def _():
        from_right[...] = jnp.zeros_like(from_right)


def start_first(parts, landed, sems, angle, tile):
    return [
        send(parts.at[(angle + step) % ANG], landed.at[step], sems, step, ((angle + step) % ANG, tile))
        for step in range(1, ANG)
    ]


def finish_first(copies, parts, landed, angle):
    for copy in copies:
        copy.wait()
    total = parts[angle]
    for step in range(1, ANG):
        total = total + landed[step]
    return total


def start_second(source, landed, sems, angle, tile):
    return [
        send(source, landed.at[tile], sems, step, (angle, shifted(tile, step)))
        for step in FARTHEST
    ]


def finish_second(copies, source, landed, tile):
    landed[tile] = source[...]
    for copy in copies:
        copy.wait()
    total = landed[0]
    for index in range(1, TILES):
        total = total + landed[index]
    return total


def start_third(source, gathered, sems, angle, tile):
    return [
        send(source, gathered.at[angle], sems, step, ((angle + step) % ANG, tile))
        for step in range(1, ANG)
    ]


def packed_sides(real, imag):
    low = lanes((ROWS, TW)) < HALF
    return (
        jnp.where(low, real, pltpu.roll(imag, HALF, 1)),
        jnp.where(low, pltpu.roll(real, HALF, 1), imag),
    )


def widened(real, imag, before, after):
    low = lanes((ROWS, TW)) < HALF
    real, imag = pltpu.roll(real, HALF, 1), pltpu.roll(imag, HALF, 1)
    return (
        (jnp.where(low, before, real), jnp.where(low, pltpu.roll(before, HALF, 1), imag)),
        (jnp.where(low, real, pltpu.roll(after, HALF, 1)), jnp.where(low, imag, after)),
    )


def halo_kernel(
    counts, shears, psi, target, probe, data, *refs,
):
    tables, refs = refs[:4], refs[4:]
    ext, own_target, packs, info, probe_here, data_here, *refs = refs
    tables_here, refs = refs[:4], refs[4:]
    own, sides, from_left, from_right, edge_sems, local_sems = refs
    angle, tile = place()
    fetches = [
        pltpu.make_async_copy(source, here, local_sems.at[index])
        for index, (source, here) in enumerate(
            zip((psi, target, probe, data) + tables, (own, own_target, probe_here, data_here) + tuple(tables_here))
        )
    ]
    for fetch in fetches:
        fetch.start()
    clear_edges(from_left, from_right, tile)
    met = greet_line(angle, tile)
    row, lane = sublanes((8, TW)), lanes((8, TW))
    count = jnp.where((row == 0) & (lane == 0), counts[0, 0].astype(F32), 0.0)
    info[...] = jnp.where((row == 1) & (lane == angle), shears[0], count)
    fetches[0].wait()
    for side, value in enumerate(packed_sides(own[0], own[1])):
        sides[side] = value
    met()
    edges = start_edges(sides, from_left, from_right, edge_sems, angle, tile)
    fetches[1].wait()
    for side, value in enumerate(packed_sides(own_target[0], own_target[1])):
        packs[side] = value
    for fetch in fetches[2:]:
        fetch.wait()
    finish_edges(edges, tile)
    for side, pair in enumerate(widened(own[0], own[1], from_left[...], from_right[...])):
        for part in range(2):
            ext[side, part] = pair[part]


def exchange_kernel(
    grad, parts, packs, info, ext0, own_target, probe0, ext, probe, info_some, info_all,
    from_left, from_right, goal_left, goal_right, landed_first, first_sum, landed_second, second_sum, gathered, landed_some, landed_info,
    edge_sems, goal_sems, first_sems, second_sems, third_sems, some_sems, info_sems,
):
    angle, tile = place()
    clear_edges(from_left, from_right, tile)
    clear_edges(goal_left, goal_right, tile)
    greet(tile_peers(angle, tile) + angle_peers(angle, tile))()
    first = start_first(parts, landed_first, first_sems, angle, tile)
    edges = start_edges(grad, from_left, from_right, edge_sems, angle, tile)
    some = [
        send(info, landed_some.at[step], some_sems, step, ((angle + step) % ANG, tile)) for step in range(1, ANG)
    ]
    first_sum[...] = finish_first(first, parts, landed_first, angle)
    second = start_second(first_sum, landed_second, second_sems, angle, tile)
    for copy in some:
        copy.wait()
    total = info[...]
    for step in range(1, ANG):
        total = total + landed_some[step]
    info_some[...] = total
    infos = start_second(info_some, landed_info, info_sems, angle, tile)
    goals = start_edges(packs, goal_left, goal_right, goal_sems, angle, tile)
    second_sum[...] = finish_second(second, first_sum, landed_second, tile)
    third = start_third(second_sum, gathered, third_sems, angle, tile)
    finish_edges(edges, tile)
    finish_edges(goals, tile)
    low = lanes((ROWS, TW)) < HALF
    inner, outer = tile > 0, tile < TILES - 1
    goal = widened(own_target[0], own_target[1], goal_left[...], goal_right[...])
    for side, landed, inside in ((0, from_left, inner), (1, from_right, outer)):
        for part in range(2):
            total = grad[side, part] + landed[part]
            old = ext0[side, part]
            new = old - ALPHA * (total + RHO * (old - goal[side][part]))
            keep = jnp.logical_or(inside, jnp.logical_not(low) if side == 0 else low)
            ext[side, part] = jnp.where(keep, new, 0.0)
    gathered[angle] = second_sum[...]
    info_all[...] = finish_second(infos, info_some, landed_info, tile)
    number = info_all[pl.ds(0, 1), pl.ds(0, 1)]
    for copy in third:
        copy.wait()
    for chunk in range(ANG):
        part, start = divmod(chunk * CHUNK, PS)
        here = pl.ds(start, CHUNK)
        probe[part, here, :] = probe0[part, here, :] - PROBE_STEP * gathered[chunk] / number


def tail_kernel(
    ext, own_target, grad, rims, parts, info, turns, right_f,
    psi_new, every, gathered, bases, cosines, sines,
    from_left, from_right, landed_first, first_sum, landed_second, second_sum,
    slabs_one, slabs_two, here_one, here_two, work_one, work_two, rows,
    edge_sems, first_sems, second_sems, third_sems, one_sems, two_sems, row_sems,
):
    angle, tile = place()
    clear_edges(from_left, from_right, tile)
    met = greet(tile_peers(angle, tile) + angle_peers(angle, tile))
    low = lanes((ROWS, TW)) < HALF
    for part in range(2):
        old, total = (
            jnp.where(low, pltpu.roll(wide[0, part], HALF, 1), pltpu.roll(wide[1, part], HALF, 1))
            for wide in (ext, grad)
        )
        new = old - ALPHA * (total + RHO * (old - own_target[part]))
        psi_new[part] = new
        for source, place_at in ((own_target[part] - new, part), (rims[part], 2 + part)):
            for slab in range(TILES):
                for slabs, first, count in ((slabs_one, 0, FIRST), (slabs_two, FIRST, ZS - FIRST)):
                    start = slab * ZS + first
                    slabs[slab, pl.ds(place_at * count, count), :] = source[start : start + count]
    work_one[...] = jnp.zeros_like(work_one)
    work_two[...] = jnp.zeros_like(work_two)
    met()
    halves = []
    for slabs, landed, sems in ((slabs_one, here_one, one_sems), (slabs_two, here_two, two_sems)):
        copies = []
        for step in FARTHEST:
            owner = shifted(tile, step)
            copies.append(send(slabs.at[owner], landed.at[tile], sems, step, (angle, owner)))
        halves.append(copies)
    first = start_first(parts, landed_first, first_sems, angle, tile)
    for slabs, landed in ((slabs_one, here_one), (slabs_two, here_two)):
        landed[tile] = slabs[tile]
    first_sum[...] = finish_first(first, parts, landed_first, angle)
    second = start_second(first_sum, landed_second, second_sems, angle, tile)

    def spectrum(copies, landed, work, start, count):
        for copy in copies:
            copy.wait()
        low = lanes((count, TW)) < HALF
        zero = jnp.zeros((count, TW), F32)
        items = []
        for index in range(TILES):
            before = landed[index - 1, pl.ds(3 * count, count), :] if index else zero
            after = landed[index + 1, pl.ds(2 * count, count), :] if index < TILES - 1 else zero
            real = jnp.where(low, before, pltpu.roll(after, HALF, 1))
            imag = jnp.where(low, pltpu.roll(before, HALF, 1), after)
            items.append(
                (
                    landed[index, pl.ds(0, count), :] + ALPHA * real,
                    landed[index, pl.ds(count, count), :] + ALPHA * imag,
                )
            )
        for order, item in enumerate(sixteen(items, -1)):
            turn = (turns[0, pl.ds(order, 1), :], turns[1, pl.ds(order, 1), :])
            real, imag = times(item, turn)
            work[pl.ds(8 * order, count), pl.ds(0, TW)] = real
            work[pl.ds(8 * order, count), pl.ds(TW, TW)] = imag
        result = dot_right(work[...], right_f[...])
        for order in range(TILES):
            rows[pl.ds(start, count), order, :] = result[8 * order : 8 * order + count]

    chip, core = angle // 2, angle % 2
    up, down, over = (chip + 1) % 4, (chip + 3) % 4, (chip + 2) % 4
    upper, lower, across = 2 * up + core, 2 * down + core, 2 * over + core
    above, below, beside = (upper, tile), (lower, tile), (2 * chip + 1 - core, tile)
    one, two = pl.ds(0, FIRST), pl.ds(FIRST, ZS - FIRST)
    spectrum(halves[0], here_one, work_one, 0, FIRST)

    def spread(part, slot):
        peers = ((across, 0), (upper, 1), (lower, 2))
        return [
            send(rows.at[part], every.at[angle, part], row_sems, slot + index, (peer, tile)) for peer, index in peers
        ]

    sent_one = spread(one, 0)
    spectrum(halves[1], here_two, work_two, FIRST, ZS - FIRST)
    sent_two = spread(two, 3)
    side = send(rows, every.at[angle], row_sems, 12, beside)
    edges = start_edges(rims, from_left, from_right, edge_sems, angle, tile)
    every[angle] = rows[...]
    second_sum[...] = finish_second(second, first_sum, landed_second, tile)
    third = [
        send(second_sum, gathered.at[angle], third_sems, slot, (peer, tile))
        for slot, peer in enumerate((across, upper, lower))
    ]
    handed = [side, send(second_sum, gathered.at[angle], third_sems, 3, beside)]
    gathered[angle] = second_sum[...]
    phase_tables(info, bases, cosines, sines, angle)

    def hand(copies, target, sems, slot):
        for index, source in ((1, lower), (2, upper), (0, across)):
            copies[index].wait()
            landed = target(source)
            handed.append(send(landed, landed, sems, slot + index, beside))

    hand(sent_one, lambda source: every.at[source, one], row_sems, 6)
    hand(third, lambda source: gathered.at[source], third_sems, 4)
    finish_edges(edges, tile)
    for part in range(2):
        before, after = from_left[...], from_right[...]
        low = lanes((ROWS, TW)) < HALF
        if part == 0:
            extra = jnp.where(low, before, pltpu.roll(after, HALF, 1))
        else:
            extra = jnp.where(low, pltpu.roll(before, HALF, 1), after)
        psi_new[part] = psi_new[part] - ALPHA * extra
    hand(sent_two, lambda source: every.at[source, two], row_sems, 9)
    for copy in handed:
        copy.wait()


def gradient_kernel(
    counts, pos_z, pos_x, ext, probe, data, right_f, left_f, left_b, right_b, grad, parts, *refs,
):
    *rims, probe_acc = refs
    count = counts[0, 0]
    grad[...] = jnp.zeros_like(grad)
    probe_acc[...] = jnp.zeros_like(probe_acc)
    lane = lanes((PS, TW))

    def sheet(values, axis):
        return jnp.concatenate(values, axis=axis)

    def group(index, carry):
        probe_real, probe_imag = probe[0], probe[1]
        rows, windows, spots = [], [], []
        for offset in range(GROUP):
            slot = GROUP * index + offset
            start_z, start_x = pos_z[0, 0, slot], pos_x[0, 0, slot]
            back = lax.rem(TW - start_x, TW)
            here = pl.ds(start_z, PS)
            real, imag = (
                pltpu.roll(jnp.where(lane >= start_x, ext[0, part, here, :], ext[1, part, here, :]), back, 1)
                for part in range(2)
            )
            windows.append((real, imag))
            spots.append((slot, start_z, start_x))
            rows.append(sheet(times((probe_real, probe_imag), (real, imag)), 1))
        pairs = range(0, GROUP, 2)
        sides = (slice(0, PS), slice(PS, 2 * PS))
        turned = [dot_right(sheet(rows[p : p + 4], 0), right_f[...]) for p in range(0, GROUP, 4)]
        turned = [v[k] for v in turned for k in (slice(0, 2 * PS), slice(2 * PS, 4 * PS))]
        turned = [sheet([sheet([v[k, :PS], v[k, PS:]], 0) for k in sides], 1) for v in turned]
        far = [dot_left(left_f[...], v) for v in turned]
        weighted = []
        for s in range(GROUP):
            slot = spots[s][0]
            far_real, far_imag = (far[s // 2][k, sides[s % 2]] for k in sides)
            live = jnp.where(slot < count, 1.0, 0.0).astype(F32)
            misfit = (far_real * far_real + far_imag * far_imag - data[slot]) * live
            weighted.append(sheet([misfit * far_real, misfit * far_imag], 0))
        turned = [dot_left(left_b[...], sheet(weighted[p : p + 2], 1)) for p in pairs]
        turned = [sheet([sheet([v[:PS, k], v[PS:, k]], 1) for k in sides], 0) for v in turned]
        chi = [dot_right(sheet(turned[p : p + 2], 0), right_b[...]) for p in range(0, GROUP // 2, 2)]
        chi = [v[k] for v in chi for k in (slice(0, 2 * PS), slice(2 * PS, 4 * PS))]
        for s in range(GROUP):
            slot, start_z, start_x = spots[s]
            here = pl.ds(start_z, PS)
            chi_real, chi_imag = (chi[s // 2][sides[s % 2], k] for k in sides)
            real, imag = windows[s]
            probe_acc[pl.ds(0, PS), :] += real * chi_real + imag * chi_imag
            probe_acc[pl.ds(PS, PS), :] += real * chi_imag - imag * chi_real
            grad_real = probe_real * chi_real + probe_imag * chi_imag
            grad_imag = probe_real * chi_imag - probe_imag * chi_real
            for part, value in ((0, grad_real), (1, grad_imag)):
                moved = pltpu.roll(value, start_x, 1)
                grad[0, part, here, :] += jnp.where(lane >= start_x, moved, 0.0)
                grad[1, part, here, :] += jnp.where(lane < start_x, moved, 0.0)
        return carry

    lax.fori_loop(0, (count + GROUP - 1) // GROUP, group, 0)
    for chunk in range(ANG):
        parts[chunk] = probe_acc[pl.ds(chunk * CHUNK, CHUNK), :]
    for rim in rims:
        low = lanes((ROWS, TW)) < HALF
        rim[0] = jnp.where(low, grad[0, 0], pltpu.roll(grad[0, 1], HALF, 1))
        rim[1] = jnp.where(low, pltpu.roll(grad[1, 0], HALF, 1), grad[1, 1])


def phase_tables(info, bases, cosines, sines, here):
    frequency = sublanes((TILES, TW)) + TILES * lanes((TILES, TW))
    signed = jnp.where(frequency < H // 2, frequency, frequency - H).astype(F32)
    centre = (YB * here - ANG * YB // 2).astype(F32) + (YB - 1) / 2.0
    row = sublanes((8, TW))
    for angle in range(ANG):
        turn = signed * (1.0 / H) * info[pl.ds(1, 1), pl.ds(angle, 1)]
        whole = centre * turn
        whole = 2.0 * math.pi * (whole - jnp.round(whole))
        half = math.pi * turn
        bases[angle, 0], bases[angle, 1] = jnp.cos(whole), jnp.sin(whole)
        power = (jnp.cos(half), jnp.sin(half))
        for level in range(5):
            bases[angle, 2 + 2 * level], bases[angle, 3 + 2 * level] = power
            power = times(power, power)

    def fill(angle, carry):
        for order in range(TILES):
            line = [
                tuple(
                    jnp.broadcast_to(bases[angle, 2 + 2 * level + part, pl.ds(order, 1), :], (8, TW))
                    for part in range(2)
                )
                for level in range(5)
            ]
            now = line[0]
            for level in range(3):
                ahead = times(now, line[1 + level])
                chosen = (row & (1 << level)) != 0
                now = tuple(jnp.where(chosen, new, old) for new, old in zip(ahead, now))
            later = times(now, line[4])
            cosines[angle, order, pl.ds(0, 8), :], sines[angle, order, pl.ds(0, 8), :] = now
            cosines[angle, order, pl.ds(8, 8), :], sines[angle, order, pl.ds(8, 8), :] = later
        return carry

    lax.fori_loop(0, ANG, fill, 0)


def flip8(value):
    row = sublanes(value.shape)
    value = pltpu.roll(value, 4, 0)
    value = jnp.where((row & 2) == 0, pltpu.roll(value, 6, 0), pltpu.roll(value, 2, 0))
    return jnp.where((row & 1) == 0, pltpu.roll(value, 7, 0), pltpu.roll(value, 1, 0))


def image_kernel(
    rows, bases, cosines, sines, turns, right_b, probe0, gathered, info, psi,
    image, probe_new, psi_new, turned_a, turned_b, spread_a, spread_b, middle_a, middle_b, ready, sems,
):
    number = info[pl.ds(0, 1), pl.ds(0, 1)]
    for chunk in range(ANG):
        part, start = divmod(chunk * CHUNK, PS)
        here = pl.ds(start, CHUNK)
        probe_new[part, here, :] = probe0[part, here, :] - PROBE_STEP * gathered[chunk] / number
    psi_new[...] = psi[...]

    def shear(z, turned, spread):
        for angle in range(ANG):
            value = (rows[angle, z, :, pl.ds(0, TW)], rows[angle, z, :, pl.ds(TW, TW)])
            turned[angle, 0], turned[angle, 1] = times(value, (bases[angle, 0], bases[angle, 1]))
        for order in range(TILES):
            sums = None
            for angle in range(ANG):
                real = jnp.broadcast_to(turned[angle, 0, pl.ds(order, 1), :], (16, TW))
                imag = jnp.broadcast_to(turned[angle, 1, pl.ds(order, 1), :], (16, TW))
                cosine, sine = cosines[angle, order], sines[angle, order]
                terms = (real * cosine, imag * sine, real * sine, imag * cosine)
                sums = terms if sums is None else tuple(s + t for s, t in zip(sums, terms))
            rc, isn, rs, ic = sums
            above = (rc - isn, rs + ic)
            below = (rc + isn, ic - rs)
            for part in range(2):
                back = jnp.concatenate([flip8(below[part][8:]), flip8(below[part][:8])], axis=0)
                value = jnp.concatenate([back, above[part]], axis=0)
                high, low = split(value)
                here = pl.ds(order * YB, YB)
                spread[here, pl.ds(part * TW, TW)] = high
                spread[here, pl.ds((2 + part) * TW, TW)] = low
                spread[here, pl.ds((4 + part) * TW, TW)] = high

    def finish(slot, spread, middle):
        middle[...] = jnp.dot(spread[...], right_b[...], preferred_element_type=F32)
        for group in range(YB // 16):
            items = []
            for order in range(TILES):
                here = pl.ds(order * YB + 16 * group, 16)
                value = (middle[here, pl.ds(0, TW)], middle[here, pl.ds(TW, TW)])
                turn = (turns[0, pl.ds(order, 1), :], turns[1, pl.ds(order, 1), :])
                items.append(times(value, turn))
            for tile, item in enumerate(sixteen(items, 1)):
                for part in range(2):
                    ready[slot, part, pl.ds(16 * group, 16), pl.ds(tile * TW, TW)] = item[part].astype(BF16)

    def put(slot, z):
        return [
            pltpu.make_async_copy(ready.at[slot, part], image.at[part, z], sems.at[slot, part]) for part in range(2)
        ]

    def step(pair, carry):
        base = 2 * lax.rem(pair, 2)

        @pl.when(pair > 1)
        def _():
            for odd in range(2):
                for copy in put(base + odd, 2 * pair - 4 + odd):
                    copy.wait()

        shear(2 * pair + 1, turned_b, spread_b)
        finish(base, spread_a, middle_a)
        shear(2 * pair + 2, turned_a, spread_a)
        finish(base + 1, spread_b, middle_b)
        for odd in range(2):
            for copy in put(base + odd, 2 * pair + odd):
                copy.start()
        return carry

    shear(0, turned_a, spread_a)
    lax.fori_loop(0, ZS // 2 - 1, step, 0)
    for odd in range(2):
        for copy in put(odd, ZS - 6 + odd):
            copy.wait()
    shear(ZS - 1, turned_b, spread_b)
    finish(0, spread_a, middle_a)
    for copy in put(0, ZS - 2):
        copy.start()
    finish(1, spread_b, middle_b)
    for copy in put(1, ZS - 1):
        copy.start()
    for slot, z in ((2, ZS - 4), (3, ZS - 3), (0, ZS - 2), (1, ZS - 1)):
        for copy in put(slot, z):
            copy.wait()


def arr(*shape):
    return jax.ShapeDtypeStruct(shape, F32)


def dma(*shape):
    return pltpu.SemaphoreType.DMA(shape)


def call(kernel, outs, specs, out_specs, scratch, ident=None):
    extra = {} if ident is None else {"collective_id": ident, "has_side_effects": True}
    return pl.pallas_call(
        kernel,
        out_shape=outs,
        in_specs=specs,
        out_specs=out_specs,
        scratch_shapes=scratch,
        compiler_params=pltpu.CompilerParams(vmem_limit_bytes=VLIMIT, **extra),
    )


def shards(psi, target, probe, data, pos_z, pos_x, counts, shears):
    psi, target = psi.reshape(2, ROWS, TW), target.reshape(2, ROWS, TW)
    data = data.reshape(CAP, PS, PS)
    unit = dft_block(PS, 1.0 / math.sqrt(PS))
    tables = [
        jnp.asarray(t)
        for t in (right_table(unit), left_table(unit.T), left_table(unit), right_table(unit.T))
    ]
    wide, edge, small = arr(2, 2, ROWS, TW), arr(2, ROWS, TW), arr(8, TW)
    chunks, square = arr(ANG, CHUNK, TW), arr(2, PS, PS)
    table_shapes = [jax.ShapeDtypeStruct(t.shape, t.dtype) for t in tables]
    one = lambda *shape: pltpu.VMEM(shape, F32)

    outs = [wide, edge, edge, small, square, arr(CAP, PS, PS)] + table_shapes
    ext, goal, packs, info, probe, data, *tables = call(
        halo_kernel,
        outs,
        [SMEM] * 2 + [HBM] * 8,
        [VMEM] * len(outs),
        [
            one(2, ROWS, TW), one(2, ROWS, TW), one(ROWS, TW), one(ROWS, TW),
            dma(2, 2), dma(8),
        ],
        0,
    )(counts, shears, *(pltpu.with_memory_space_constraint(x, pltpu.HBM) for x in (psi, target, probe, data, *tables)))

    def gradient(ext, probe, rims):
        return call(
            gradient_kernel, [wide, chunks] + rims, [SMEM] * 3 + [VMEM] * 7, [VMEM] * (2 + len(rims)), [one(2 * PS, PS)]
        )(counts, pos_z, pos_x, ext, probe, data, *tables)

    grad, parts = gradient(ext, probe, [])
    ext, probe, info, info_all = call(
        exchange_kernel,
        [wide, square, small, small],
        [VMEM] * 7,
        [VMEM] * 4,
        [
            one(2, ROWS, TW), one(2, ROWS, TW), one(ROWS, TW), one(ROWS, TW),
            one(ANG, CHUNK, TW), one(CHUNK, TW), one(TILES, CHUNK, TW), one(CHUNK, TW), one(ANG, CHUNK, TW), one(ANG, 8, TW), one(TILES, 8, TW),
            dma(2, 2), dma(2, 2), dma(2, ANG), dma(2, TILES), dma(2, ANG), dma(2, ANG), dma(2, TILES),
        ],
        1,
    )(grad, parts, packs, info, ext, goal, probe)
    grad, parts, rims = gradient(ext, probe, [edge])
    every, phases = arr(ANG, ZS, TILES, WIDE), arr(ANG, TILES, 16, TW)
    psi_new, every, gathered, bases, cosines, sines = call(
        tail_kernel,
        [edge, every, chunks, arr(ANG, 12, TILES, TW), phases, phases],
        [VMEM] * 8,
        [VMEM] * 6,
        [
            one(ROWS, TW), one(ROWS, TW),
            one(ANG, CHUNK, TW), one(CHUNK, TW), one(TILES, CHUNK, TW), one(CHUNK, TW),
            one(TILES, 4 * FIRST, TW), one(TILES, 4 * (ZS - FIRST), TW),
            one(TILES, 4 * FIRST, TW), one(TILES, 4 * (ZS - FIRST), TW),
            one(PS, WIDE), one(PS, WIDE), one(ZS, TILES, WIDE),
            dma(2, 2), dma(2, ANG), dma(2, TILES), dma(2, ANG), dma(2, TILES), dma(2, TILES), dma(2, 13),
        ],
        2,
    )(ext, goal, grad, rims, parts, info, jnp.asarray(turn_table(-1)), jnp.asarray(right_table(dft_block(TW, 1.0))))
    inverse = dft_block(TW, 1.0 / (H * ANG)).T
    image, probe_new, psi_new = call(
        image_kernel,
        [jax.ShapeDtypeStruct((2, ZS, YB, H), BF16), square, edge],
        [VMEM] * 10,
        [HBM, VMEM, VMEM],
        [
            one(ANG, 2, TILES, TW),
            one(ANG, 2, TILES, TW),
            pltpu.VMEM((TILES * YB, 3 * WIDE), BF16),
            pltpu.VMEM((TILES * YB, 3 * WIDE), BF16),
            one(TILES * YB, WIDE),
            one(TILES * YB, WIDE),
            pltpu.VMEM((4, 2, YB, H), BF16),
            dma(4, 2),
        ],
    )(
        every, bases, cosines, sines, jnp.asarray(turn_table(1)), jnp.asarray(right_table(inverse)),
        probe, gathered, info_all, psi_new,
    )
    return psi_new.reshape(2, 1, ROWS, TW), probe_new, image


def solution(mesh):
    in_specs = (
        P(None, "angle", None, "tile"),
        P(None, "angle", None, "tile"),
        P(),
        P("angle", "tile", None, None, None),
        P("angle", "tile", None),
        P("angle", "tile", None),
        P("angle", "tile"),
        P("angle"),
    )
    out_specs = (P(None, "angle", None, "tile"), P(), P(None, "tile", "angle", None))
    return jax.shard_map(shards, mesh=mesh, in_specs=in_specs, out_specs=out_specs, check_vma=False)
```

```python
import functools
import math

import jax
import jax.numpy as jnp
import numpy as np
from jax import lax
from jax.experimental import pallas as pl
from jax.experimental.pallas import tpu as pltpu
from jax.sharding import PartitionSpec as P

ITERS = 2
ALPHA = 0.004
RHO = 5.0
PROBE_STEP = 0.02

ANG = 8
TILES = 16
PS = 128
TW = 128
ROWS = 160
CAP = 16
HALF = 64
WIDE = 256
ZS = ROWS // TILES
YB = 32
H = 2048
CHUNK = 2 * PS // ANG
GROUP = 8
FIRST = 4

F32 = jnp.float32
BF16 = jnp.bfloat16
MESH = pl.DeviceIdType.MESH
VMEM = pl.BlockSpec(memory_space=pltpu.VMEM)
SMEM = pl.BlockSpec(memory_space=pltpu.SMEM)
HBM = pl.BlockSpec(memory_space=pltpu.HBM)
VLIMIT = 20 * 1024 * 1024


def dft_block(length, scale):
    index = np.arange(length)
    turns = (index[:, None] * index[None, :]) % length
    angle = -2.0 * math.pi * turns / length
    real, imag = np.cos(angle) * scale, np.sin(angle) * scale
    return np.block([[real, imag], [-imag, real]])


def split_const(matrix):
    high = matrix.astype(BF16)
    low = (matrix - high.astype(np.float64)).astype(BF16)
    return high, low


def right_table(matrix):
    high, low = split_const(matrix)
    return np.concatenate([high, high, low], axis=0)


def left_table(matrix):
    high, low = split_const(matrix)
    return np.concatenate([high, high, low], axis=1)


def turn_table(orient):
    angle = orient * 2.0 * math.pi * np.arange(TILES)[:, None] * np.arange(TW)[None, :] / H
    return np.stack([np.cos(angle), np.sin(angle)]).astype(np.float32)


def split(value):
    high = value.astype(BF16)
    low = (value - high.astype(F32)).astype(BF16)
    return high, low


def dot_right(value, table):
    high, low = split(value)
    return jnp.dot(jnp.concatenate([high, low, high], axis=1), table, preferred_element_type=F32)


def dot_left(table, value):
    high, low = split(value)
    return jnp.dot(table, jnp.concatenate([high, low, high], axis=0), preferred_element_type=F32)


def times(left, right):
    return left[0] * right[0] - left[1] * right[1], left[0] * right[1] + left[1] * right[0]


def four(items, orient):
    (ar, ai), (br, bi), (cr, ci), (dr, di) = items
    sr, si, ur, ui = ar + cr, ai + ci, ar - cr, ai - ci
    pr, pi, qr, qi = br + dr, bi + di, br - dr, bi - di
    first = (sr + pr, si + pi)
    third = (sr - pr, si - pi)
    plus = (ur - qi, ui + qr)
    minus = (ur + qi, ui - qr)
    return [first, plus, third, minus] if orient > 0 else [first, minus, third, plus]


def turn_by(value, step, orient):
    real, imag = value
    if orient < 0:
        real, imag = imag, real
    if step == 4:
        real, imag = -imag, real
    elif step == 2:
        real, imag = (real - imag) * math.sqrt(0.5), (real + imag) * math.sqrt(0.5)
    elif step == 6:
        real, imag = (real + imag) * -math.sqrt(0.5), (real - imag) * math.sqrt(0.5)
    else:
        angle = 2.0 * math.pi * step / 16
        real, imag = times((real, imag), (math.cos(angle), math.sin(angle)))
    return (imag, real) if orient < 0 else (real, imag)


def sixteen(items, orient):
    columns = []
    for fine in range(4):
        partial = four([items[4 * coarse + fine] for coarse in range(4)], orient)
        for order in range(1, 4):
            step = fine * order
            if step:
                partial[order] = turn_by(partial[order], step, orient)
        columns.append(partial)
    result = [None] * 16
    for low in range(4):
        finished = four([columns[fine][low] for fine in range(4)], orient)
        for high in range(4):
            result[low + 4 * high] = finished[high]
    return result


def lanes(shape):
    return lax.broadcasted_iota(jnp.int32, shape, len(shape) - 1)


def sublanes(shape):
    return lax.broadcasted_iota(jnp.int32, shape, len(shape) - 2)


def place():
    return lax.axis_index("angle"), lax.axis_index("tile")


def greet(peers):
    barrier = pltpu.get_barrier_semaphore()
    for peer in peers:
        pl.semaphore_signal(barrier, inc=1, device_id=peer, device_id_type=MESH)
    return lambda: pl.semaphore_wait(barrier, len(peers))


def send(source, target, sems, slot, peer):
    copy = pltpu.make_async_remote_copy(
        src_ref=source,
        dst_ref=target,
        send_sem=sems.at[0, slot],
        recv_sem=sems.at[1, slot],
        device_id=peer,
        device_id_type=MESH,
    )
    copy.start()
    return copy


def greet_line(angle, tile):
    barrier = pltpu.get_barrier_semaphore()
    sides = ((tile > 0, tile - 1), (tile < TILES - 1, tile + 1))
    for inside, peer in sides:

        @pl.when(inside)
        def _():
            pl.semaphore_signal(barrier, inc=1, device_id=(angle, peer), device_id_type=MESH)

    inner = jnp.logical_and(tile > 0, tile < TILES - 1)

    def wait():
        @pl.when(inner)
        def _():
            pl.semaphore_wait(barrier, 2)

        @pl.when(jnp.logical_not(inner))
        def _():
            pl.semaphore_wait(barrier, 1)

    return wait


def angle_peers(angle, tile):
    return [((angle + step) % ANG, tile) for step in range(1, ANG)]


FARTHEST = sorted(range(1, TILES), key=lambda s: -(min(s // 4, 4 - s // 4) + min(s % 4, 4 - s % 4)))


def shifted(tile, step):
    return (tile // 4 + step // 4) % 4 * 4 + (tile % 4 + step % 4) % 4


def tile_peers(angle, tile):
    return [(angle, shifted(tile, step)) for step in FARTHEST]


def neighbours(angle, tile):
    return (angle, (tile + TILES - 1) % TILES), (angle, (tile + 1) % TILES)


def start_edges(packs, from_left, from_right, sems, angle, tile):
    def copy(side, landing, peer):
        return pltpu.make_async_remote_copy(
            src_ref=packs.at[side],
            dst_ref=landing,
            send_sem=sems.at[0, side],
            recv_sem=sems.at[1, side],
            device_id=peer,
            device_id_type=MESH,
        )

    left, right = neighbours(angle, tile)
    to_left, to_right = copy(0, from_right, left), copy(1, from_left, right)

    @pl.when(tile > 0)
    def _():
        to_left.start()

    @pl.when(tile < TILES - 1)
    def _():
        to_right.start()

    return to_left, to_right


def finish_edges(copies, tile):
    to_left, to_right = copies

    @pl.when(tile > 0)
    def _():
        to_left.wait_send()
        to_right.wait_recv()

    @pl.when(tile < TILES - 1)
    def _():
        to_right.wait_send()
        to_left.wait_recv()


def clear_edges(from_left, from_right, tile):
    @pl.when(tile == 0)
    def _():
        from_left[...] = jnp.zeros_like(from_left)

    @pl.when(tile == TILES - 1)
    def _():
        from_right[...] = jnp.zeros_like(from_right)


def start_first(parts, landed, sems, angle, tile):
    return [
        send(parts.at[(angle + step) % ANG], landed.at[step], sems, step, ((angle + step) % ANG, tile))
        for step in range(1, ANG)
    ]


def finish_first(copies, parts, landed, angle):
    for copy in copies:
        copy.wait()
    total = parts[angle]
    for step in range(1, ANG):
        total = total + landed[step]
    return total


def start_second(source, landed, sems, angle, tile):
    return [
        send(source, landed.at[tile], sems, step, (angle, shifted(tile, step)))
        for step in FARTHEST
    ]


def finish_second(copies, source, landed, tile):
    landed[tile] = source[...]
    for copy in copies:
        copy.wait()
    total = landed[0]
    for index in range(1, TILES):
        total = total + landed[index]
    return total


def start_third(source, gathered, sems, angle, tile):
    return [
        send(source, gathered.at[angle], sems, step, ((angle + step) % ANG, tile))
        for step in range(1, ANG)
    ]


def packed_sides(real, imag):
    low = lanes((ROWS, TW)) < HALF
    return (
        jnp.where(low, real, pltpu.roll(imag, HALF, 1)),
        jnp.where(low, pltpu.roll(real, HALF, 1), imag),
    )


def widened(real, imag, before, after):
    low = lanes((ROWS, TW)) < HALF
    real, imag = pltpu.roll(real, HALF, 1), pltpu.roll(imag, HALF, 1)
    return (
        (jnp.where(low, before, real), jnp.where(low, pltpu.roll(before, HALF, 1), imag)),
        (jnp.where(low, real, pltpu.roll(after, HALF, 1)), jnp.where(low, imag, after)),
    )


def halo_kernel(
    counts, shears, psi, target, probe, data, *refs,
):
    tables, refs = refs[:4], refs[4:]
    ext, own_target, packs, info, probe_here, data_here, *refs = refs
    tables_here, refs = refs[:4], refs[4:]
    own, sides, from_left, from_right, edge_sems, local_sems = refs
    angle, tile = place()
    fetches = [
        pltpu.make_async_copy(source, here, local_sems.at[index])
        for index, (source, here) in enumerate(
            zip((psi, target, probe, data) + tables, (own, own_target, probe_here, data_here) + tuple(tables_here))
        )
    ]
    for fetch in fetches:
        fetch.start()
    clear_edges(from_left, from_right, tile)
    met = greet_line(angle, tile)
    row, lane = sublanes((8, TW)), lanes((8, TW))
    count = jnp.where((row == 0) & (lane == 0), counts[0, 0].astype(F32), 0.0)
    info[...] = jnp.where((row == 1) & (lane == angle), shears[0], count)
    fetches[0].wait()
    for side, value in enumerate(packed_sides(own[0], own[1])):
        sides[side] = value
    met()
    edges = start_edges(sides, from_left, from_right, edge_sems, angle, tile)
    fetches[1].wait()
    for side, value in enumerate(packed_sides(own_target[0], own_target[1])):
        packs[side] = value
    for fetch in fetches[2:]:
        fetch.wait()
    finish_edges(edges, tile)
    for side, pair in enumerate(widened(own[0], own[1], from_left[...], from_right[...])):
        for part in range(2):
            ext[side, part] = pair[part]


def exchange_kernel(
    grad, parts, packs, info, ext0, own_target, probe0, ext, probe, info_some, info_all,
    from_left, from_right, goal_left, goal_right, landed_first, first_sum, landed_second, second_sum, gathered, landed_some, landed_info,
    edge_sems, goal_sems, first_sems, second_sems, third_sems, some_sems, info_sems,
):
    angle, tile = place()
    clear_edges(from_left, from_right, tile)
    clear_edges(goal_left, goal_right, tile)
    greet(tile_peers(angle, tile) + angle_peers(angle, tile))()
    first = start_first(parts, landed_first, first_sems, angle, tile)
    edges = start_edges(grad, from_left, from_right, edge_sems, angle, tile)
    some = [
        send(info, landed_some.at[step], some_sems, step, ((angle + step) % ANG, tile)) for step in range(1, ANG)
    ]
    first_sum[...] = finish_first(first, parts, landed_first, angle)
    second = start_second(first_sum, landed_second, second_sems, angle, tile)
    for copy in some:
        copy.wait()
    total = info[...]
    for step in range(1, ANG):
        total = total + landed_some[step]
    info_some[...] = total
    infos = start_second(info_some, landed_info, info_sems, angle, tile)
    goals = start_edges(packs, goal_left, goal_right, goal_sems, angle, tile)
    second_sum[...] = finish_second(second, first_sum, landed_second, tile)
    third = start_third(second_sum, gathered, third_sems, angle, tile)
    finish_edges(edges, tile)
    finish_edges(goals, tile)
    low = lanes((ROWS, TW)) < HALF
    inner, outer = tile > 0, tile < TILES - 1
    goal = widened(own_target[0], own_target[1], goal_left[...], goal_right[...])
    for side, landed, inside in ((0, from_left, inner), (1, from_right, outer)):
        for part in range(2):
            total = grad[side, part] + landed[part]
            old = ext0[side, part]
            new = old - ALPHA * (total + RHO * (old - goal[side][part]))
            keep = jnp.logical_or(inside, jnp.logical_not(low) if side == 0 else low)
            ext[side, part] = jnp.where(keep, new, 0.0)
    gathered[angle] = second_sum[...]
    info_all[...] = finish_second(infos, info_some, landed_info, tile)
    number = info_all[pl.ds(0, 1), pl.ds(0, 1)]
    for copy in third:
        copy.wait()
    for chunk in range(ANG):
        part, start = divmod(chunk * CHUNK, PS)
        here = pl.ds(start, CHUNK)
        probe[part, here, :] = probe0[part, here, :] - PROBE_STEP * gathered[chunk] / number


def tail_kernel(
    ext, own_target, grad, rims, parts, info, turns, right_f,
    psi_new, every, gathered, bases, cosines, sines,
    from_left, from_right, landed_first, first_sum, landed_second, second_sum,
    slabs_one, slabs_two, here_one, here_two, work_one, work_two, rows,
    edge_sems, first_sems, second_sems, third_sems, one_sems, two_sems, row_sems,
):
    angle, tile = place()
    clear_edges(from_left, from_right, tile)
    met = greet(tile_peers(angle, tile) + angle_peers(angle, tile))
    low = lanes((ROWS, TW)) < HALF
    for part in range(2):
        old, total = (
            jnp.where(low, pltpu.roll(wide[0, part], HALF, 1), pltpu.roll(wide[1, part], HALF, 1))
            for wide in (ext, grad)
        )
        new = old - ALPHA * (total + RHO * (old - own_target[part]))
        psi_new[part] = new
        for source, place_at in ((own_target[part] - new, part), (rims[part], 2 + part)):
            for slab in range(TILES):
                for slabs, first, count in ((slabs_one, 0, FIRST), (slabs_two, FIRST, ZS - FIRST)):
                    start = slab * ZS + first
                    slabs[slab, pl.ds(place_at * count, count), :] = source[start : start + count]
    work_one[...] = jnp.zeros_like(work_one)
    work_two[...] = jnp.zeros_like(work_two)
    met()
    halves = []
    for slabs, landed, sems in ((slabs_one, here_one, one_sems), (slabs_two, here_two, two_sems)):
        copies = []
        for step in FARTHEST:
            owner = shifted(tile, step)
            copies.append(send(slabs.at[owner], landed.at[tile], sems, step, (angle, owner)))
        halves.append(copies)
    first = start_first(parts, landed_first, first_sems, angle, tile)
    for slabs, landed in ((slabs_one, here_one), (slabs_two, here_two)):
        landed[tile] = slabs[tile]
    first_sum[...] = finish_first(first, parts, landed_first, angle)
    second = start_second(first_sum, landed_second, second_sems, angle, tile)

    def spectrum(copies, landed, work, start, count):
        for copy in copies:
            copy.wait()
        low = lanes((count, TW)) < HALF
        zero = jnp.zeros((count, TW), F32)
        items = []
        for index in range(TILES):
            before = landed[index - 1, pl.ds(3 * count, count), :] if index else zero
            after = landed[index + 1, pl.ds(2 * count, count), :] if index < TILES - 1 else zero
            real = jnp.where(low, before, pltpu.roll(after, HALF, 1))
            imag = jnp.where(low, pltpu.roll(before, HALF, 1), after)
            items.append(
                (
                    landed[index, pl.ds(0, count), :] + ALPHA * real,
                    landed[index, pl.ds(count, count), :] + ALPHA * imag,
                )
            )
        for order, item in enumerate(sixteen(items, -1)):
            turn = (turns[0, pl.ds(order, 1), :], turns[1, pl.ds(order, 1), :])
            real, imag = times(item, turn)
            work[pl.ds(8 * order, count), pl.ds(0, TW)] = real
            work[pl.ds(8 * order, count), pl.ds(TW, TW)] = imag
        result = dot_right(work[...], right_f[...])
        for order in range(TILES):
            rows[pl.ds(start, count), order, :] = result[8 * order : 8 * order + count]

    chip, core = angle // 2, angle % 2
    up, down, over = (chip + 1) % 4, (chip + 3) % 4, (chip + 2) % 4
    upper, lower, across = 2 * up + core, 2 * down + core, 2 * over + core
    above, below, beside = (upper, tile), (lower, tile), (2 * chip + 1 - core, tile)
    one, two = pl.ds(0, FIRST), pl.ds(FIRST, ZS - FIRST)
    spectrum(halves[0], here_one, work_one, 0, FIRST)

    def spread(part, slot):
        peers = ((across, 0), (upper, 1), (lower, 2))
        return [
            send(rows.at[part], every.at[angle, part], row_sems, slot + index, (peer, tile)) for peer, index in peers
        ]

    sent_one = spread(one, 0)
    spectrum(halves[1], here_two, work_two, FIRST, ZS - FIRST)
    sent_two = spread(two, 3)
    side = send(rows, every.at[angle], row_sems, 12, beside)
    edges = start_edges(rims, from_left, from_right, edge_sems, angle, tile)
    every[angle] = rows[...]
    second_sum[...] = finish_second(second, first_sum, landed_second, tile)
    third = [
        send(second_sum, gathered.at[angle], third_sems, slot, (peer, tile))
        for slot, peer in enumerate((across, upper, lower))
    ]
    handed = [side, send(second_sum, gathered.at[angle], third_sems, 3, beside)]
    gathered[angle] = second_sum[...]
    phase_tables(info, bases, cosines, sines, angle)

    def hand(copies, target, sems, slot):
        for index, source in ((1, lower), (2, upper), (0, across)):
            copies[index].wait()
            landed = target(source)
            handed.append(send(landed, landed, sems, slot + index, beside))

    hand(sent_one, lambda source: every.at[source, one], row_sems, 6)
    hand(third, lambda source: gathered.at[source], third_sems, 4)
    finish_edges(edges, tile)
    for part in range(2):
        before, after = from_left[...], from_right[...]
        low = lanes((ROWS, TW)) < HALF
        if part == 0:
            extra = jnp.where(low, before, pltpu.roll(after, HALF, 1))
        else:
            extra = jnp.where(low, pltpu.roll(before, HALF, 1), after)
        psi_new[part] = psi_new[part] - ALPHA * extra
    hand(sent_two, lambda source: every.at[source, two], row_sems, 9)
    for copy in handed:
        copy.wait()


def gradient_kernel(
    counts, pos_z, pos_x, ext, probe, data, right_f, left_f, left_b, right_b, grad, parts, *refs,
):
    *rims, probe_acc = refs
    count = counts[0, 0]
    grad[...] = jnp.zeros_like(grad)
    probe_acc[...] = jnp.zeros_like(probe_acc)
    lane = lanes((PS, TW))

    def sheet(values, axis):
        return jnp.concatenate(values, axis=axis)

    def group(index, carry):
        probe_real, probe_imag = probe[0], probe[1]
        rows, windows, spots = [], [], []
        for offset in range(GROUP):
            slot = GROUP * index + offset
            start_z, start_x = pos_z[0, 0, slot], pos_x[0, 0, slot]
            back = lax.rem(TW - start_x, TW)
            here = pl.ds(start_z, PS)
            real, imag = (
                pltpu.roll(jnp.where(lane >= start_x, ext[0, part, here, :], ext[1, part, here, :]), back, 1)
                for part in range(2)
            )
            windows.append((real, imag))
            spots.append((slot, start_z, start_x))
            rows.append(sheet(times((probe_real, probe_imag), (real, imag)), 1))
        pairs = range(0, GROUP, 2)
        sides = (slice(0, PS), slice(PS, 2 * PS))
        turned = [dot_right(sheet(rows[p : p + 4], 0), right_f[...]) for p in range(0, GROUP, 4)]
        turned = [v[k] for v in turned for k in (slice(0, 2 * PS), slice(2 * PS, 4 * PS))]
        turned = [sheet([sheet([v[k, :PS], v[k, PS:]], 0) for k in sides], 1) for v in turned]
        far = [dot_left(left_f[...], v) for v in turned]
        weighted = []
        for s in range(GROUP):
            slot = spots[s][0]
            far_real, far_imag = (far[s // 2][k, sides[s % 2]] for k in sides)
            live = jnp.where(slot < count, 1.0, 0.0).astype(F32)
            misfit = (far_real * far_real + far_imag * far_imag - data[slot]) * live
            weighted.append(sheet([misfit * far_real, misfit * far_imag], 0))
        turned = [dot_left(left_b[...], sheet(weighted[p : p + 2], 1)) for p in pairs]
        turned = [sheet([sheet([v[:PS, k], v[PS:, k]], 1) for k in sides], 0) for v in turned]
        chi = [dot_right(sheet(turned[p : p + 2], 0), right_b[...]) for p in range(0, GROUP // 2, 2)]
        chi = [v[k] for v in chi for k in (slice(0, 2 * PS), slice(2 * PS, 4 * PS))]
        for s in range(GROUP):
            slot, start_z, start_x = spots[s]
            here = pl.ds(start_z, PS)
            chi_real, chi_imag = (chi[s // 2][sides[s % 2], k] for k in sides)
            real, imag = windows[s]
            probe_acc[pl.ds(0, PS), :] += real * chi_real + imag * chi_imag
            probe_acc[pl.ds(PS, PS), :] += real * chi_imag - imag * chi_real
            grad_real = probe_real * chi_real + probe_imag * chi_imag
            grad_imag = probe_real * chi_imag - probe_imag * chi_real
            for part, value in ((0, grad_real), (1, grad_imag)):
                moved = pltpu.roll(value, start_x, 1)
                grad[0, part, here, :] += jnp.where(lane >= start_x, moved, 0.0)
                grad[1, part, here, :] += jnp.where(lane < start_x, moved, 0.0)
        return carry

    lax.fori_loop(0, (count + GROUP - 1) // GROUP, group, 0)
    for chunk in range(ANG):
        parts[chunk] = probe_acc[pl.ds(chunk * CHUNK, CHUNK), :]
    for rim in rims:
        low = lanes((ROWS, TW)) < HALF
        rim[0] = jnp.where(low, grad[0, 0], pltpu.roll(grad[0, 1], HALF, 1))
        rim[1] = jnp.where(low, pltpu.roll(grad[1, 0], HALF, 1), grad[1, 1])


def phase_tables(info, bases, cosines, sines, here):
    frequency = sublanes((TILES, TW)) + TILES * lanes((TILES, TW))
    signed = jnp.where(frequency < H // 2, frequency, frequency - H).astype(F32)
    centre = (YB * here - ANG * YB // 2).astype(F32) + (YB - 1) / 2.0
    row = sublanes((8, TW))
    for angle in range(ANG):
        turn = signed * (1.0 / H) * info[pl.ds(1, 1), pl.ds(angle, 1)]
        whole = centre * turn
        whole = 2.0 * math.pi * (whole - jnp.round(whole))
        half = math.pi * turn
        bases[angle, 0], bases[angle, 1] = jnp.cos(whole), jnp.sin(whole)
        power = (jnp.cos(half), jnp.sin(half))
        for level in range(5):
            bases[angle, 2 + 2 * level], bases[angle, 3 + 2 * level] = power
            power = times(power, power)

    def fill(angle, carry):
        for order in range(TILES):
            line = [
                tuple(
                    jnp.broadcast_to(bases[angle, 2 + 2 * level + part, pl.ds(order, 1), :], (8, TW))
                    for part in range(2)
                )
                for level in range(5)
            ]
            now = line[0]
            for level in range(3):
                ahead = times(now, line[1 + level])
                chosen = (row & (1 << level)) != 0
                now = tuple(jnp.where(chosen, new, old) for new, old in zip(ahead, now))
            later = times(now, line[4])
            cosines[angle, order, pl.ds(0, 8), :], sines[angle, order, pl.ds(0, 8), :] = now
            cosines[angle, order, pl.ds(8, 8), :], sines[angle, order, pl.ds(8, 8), :] = later
        return carry

    lax.fori_loop(0, ANG, fill, 0)


def flip8(value):
    row = sublanes(value.shape)
    value = pltpu.roll(value, 4, 0)
    value = jnp.where((row & 2) == 0, pltpu.roll(value, 6, 0), pltpu.roll(value, 2, 0))
    return jnp.where((row & 1) == 0, pltpu.roll(value, 7, 0), pltpu.roll(value, 1, 0))


def image_kernel(
    rows, bases, cosines, sines, turns, right_b, probe0, gathered, info, psi,
    image, probe_new, psi_new, turned_a, turned_b, spread_a, spread_b, middle_a, middle_b, ready, sems,
):
    number = info[pl.ds(0, 1), pl.ds(0, 1)]
    for chunk in range(ANG):
        part, start = divmod(chunk * CHUNK, PS)
        here = pl.ds(start, CHUNK)
        probe_new[part, here, :] = probe0[part, here, :] - PROBE_STEP * gathered[chunk] / number
    psi_new[...] = psi[...]

    def shear(z, turned, spread):
        for angle in range(ANG):
            value = (rows[angle, z, :, pl.ds(0, TW)], rows[angle, z, :, pl.ds(TW, TW)])
            turned[angle, 0], turned[angle, 1] = times(value, (bases[angle, 0], bases[angle, 1]))
        for order in range(TILES):
            sums = None
            for angle in range(ANG):
                real = jnp.broadcast_to(turned[angle, 0, pl.ds(order, 1), :], (16, TW))
                imag = jnp.broadcast_to(turned[angle, 1, pl.ds(order, 1), :], (16, TW))
                cosine, sine = cosines[angle, order], sines[angle, order]
                terms = (real * cosine, imag * sine, real * sine, imag * cosine)
                sums = terms if sums is None else tuple(s + t for s, t in zip(sums, terms))
            rc, isn, rs, ic = sums
            above = (rc - isn, rs + ic)
            below = (rc + isn, ic - rs)
            for part in range(2):
                back = jnp.concatenate([flip8(below[part][8:]), flip8(below[part][:8])], axis=0)
                value = jnp.concatenate([back, above[part]], axis=0)
                high, low = split(value)
                here = pl.ds(order * YB, YB)
                spread[here, pl.ds(part * TW, TW)] = high
                spread[here, pl.ds((2 + part) * TW, TW)] = low
                spread[here, pl.ds((4 + part) * TW, TW)] = high

    def finish(slot, spread, middle):
        middle[...] = jnp.dot(spread[...], right_b[...], preferred_element_type=F32)
        for group in range(YB // 16):
            items = []
            for order in range(TILES):
                here = pl.ds(order * YB + 16 * group, 16)
                value = (middle[here, pl.ds(0, TW)], middle[here, pl.ds(TW, TW)])
                turn = (turns[0, pl.ds(order, 1), :], turns[1, pl.ds(order, 1), :])
                items.append(times(value, turn) if order else value)
            for tile, item in enumerate(sixteen(items, 1)):
                for part in range(2):
                    ready[slot, part, pl.ds(16 * group, 16), pl.ds(tile * TW, TW)] = item[part].astype(BF16)

    def put(slot, z):
        return [
            pltpu.make_async_copy(ready.at[slot, part], image.at[part, z], sems.at[slot, part]) for part in range(2)
        ]

    def step(pair, carry):
        base = 2 * lax.rem(pair, 2)

        @pl.when(pair > 1)
        def _():
            for odd in range(2):
                for copy in put(base + odd, 2 * pair - 4 + odd):
                    copy.wait()

        shear(2 * pair + 1, turned_b, spread_b)
        finish(base, spread_a, middle_a)
        shear(2 * pair + 2, turned_a, spread_a)
        finish(base + 1, spread_b, middle_b)
        for odd in range(2):
            for copy in put(base + odd, 2 * pair + odd):
                copy.start()
        return carry

    shear(0, turned_a, spread_a)
    lax.fori_loop(0, ZS // 2 - 1, step, 0)
    for odd in range(2):
        for copy in put(odd, ZS - 6 + odd):
            copy.wait()
    shear(ZS - 1, turned_b, spread_b)
    finish(0, spread_a, middle_a)
    for copy in put(0, ZS - 2):
        copy.start()
    finish(1, spread_b, middle_b)
    for copy in put(1, ZS - 1):
        copy.start()
    for slot, z in ((2, ZS - 4), (3, ZS - 3), (0, ZS - 2), (1, ZS - 1)):
        for copy in put(slot, z):
            copy.wait()


def arr(*shape):
    return jax.ShapeDtypeStruct(shape, F32)


def dma(*shape):
    return pltpu.SemaphoreType.DMA(shape)


def call(kernel, outs, specs, out_specs, scratch, ident=None):
    extra = {} if ident is None else {"collective_id": ident, "has_side_effects": True}
    return pl.pallas_call(
        kernel,
        out_shape=outs,
        in_specs=specs,
        out_specs=out_specs,
        scratch_shapes=scratch,
        compiler_params=pltpu.CompilerParams(vmem_limit_bytes=VLIMIT, **extra),
    )


def shards(psi, target, probe, data, pos_z, pos_x, counts, shears):
    psi, target = psi.reshape(2, ROWS, TW), target.reshape(2, ROWS, TW)
    data = data.reshape(CAP, PS, PS)
    unit = dft_block(PS, 1.0 / math.sqrt(PS))
    tables = [
        jnp.asarray(t)
        for t in (right_table(unit), left_table(unit.T), left_table(unit), right_table(unit.T))
    ]
    wide, edge, small = arr(2, 2, ROWS, TW), arr(2, ROWS, TW), arr(8, TW)
    chunks, square = arr(ANG, CHUNK, TW), arr(2, PS, PS)
    table_shapes = [jax.ShapeDtypeStruct(t.shape, t.dtype) for t in tables]
    one = lambda *shape: pltpu.VMEM(shape, F32)

    outs = [wide, edge, edge, small, square, arr(CAP, PS, PS)] + table_shapes
    ext, goal, packs, info, probe, data, *tables = call(
        halo_kernel,
        outs,
        [SMEM] * 2 + [HBM] * 8,
        [VMEM] * len(outs),
        [
            one(2, ROWS, TW), one(2, ROWS, TW), one(ROWS, TW), one(ROWS, TW),
            dma(2, 2), dma(8),
        ],
        0,
    )(counts, shears, *(pltpu.with_memory_space_constraint(x, pltpu.HBM) for x in (psi, target, probe, data, *tables)))

    def gradient(ext, probe, rims):
        return call(
            gradient_kernel, [wide, chunks] + rims, [SMEM] * 3 + [VMEM] * 7, [VMEM] * (2 + len(rims)), [one(2 * PS, PS)]
        )(counts, pos_z, pos_x, ext, probe, data, *tables)

    grad, parts = gradient(ext, probe, [])
    ext, probe, info, info_all = call(
        exchange_kernel,
        [wide, square, small, small],
        [VMEM] * 7,
        [VMEM] * 4,
        [
            one(2, ROWS, TW), one(2, ROWS, TW), one(ROWS, TW), one(ROWS, TW),
            one(ANG, CHUNK, TW), one(CHUNK, TW), one(TILES, CHUNK, TW), one(CHUNK, TW), one(ANG, CHUNK, TW), one(ANG, 8, TW), one(TILES, 8, TW),
            dma(2, 2), dma(2, 2), dma(2, ANG), dma(2, TILES), dma(2, ANG), dma(2, ANG), dma(2, TILES),
        ],
        1,
    )(grad, parts, packs, info, ext, goal, probe)
    grad, parts, rims = gradient(ext, probe, [edge])
    every, phases = arr(ANG, ZS, TILES, WIDE), arr(ANG, TILES, 16, TW)
    psi_new, every, gathered, bases, cosines, sines = call(
        tail_kernel,
        [edge, every, chunks, arr(ANG, 12, TILES, TW), phases, phases],
        [VMEM] * 8,
        [VMEM] * 6,
        [
            one(ROWS, TW), one(ROWS, TW),
            one(ANG, CHUNK, TW), one(CHUNK, TW), one(TILES, CHUNK, TW), one(CHUNK, TW),
            one(TILES, 4 * FIRST, TW), one(TILES, 4 * (ZS - FIRST), TW),
            one(TILES, 4 * FIRST, TW), one(TILES, 4 * (ZS - FIRST), TW),
            one(PS, WIDE), one(PS, WIDE), one(ZS, TILES, WIDE),
            dma(2, 2), dma(2, ANG), dma(2, TILES), dma(2, ANG), dma(2, TILES), dma(2, TILES), dma(2, 13),
        ],
        2,
    )(ext, goal, grad, rims, parts, info, jnp.asarray(turn_table(-1)), jnp.asarray(right_table(dft_block(TW, 1.0))))
    inverse = dft_block(TW, 1.0 / (H * ANG)).T
    image, probe_new, psi_new = call(
        image_kernel,
        [jax.ShapeDtypeStruct((2, ZS, YB, H), BF16), square, edge],
        [VMEM] * 10,
        [HBM, VMEM, VMEM],
        [
            one(ANG, 2, TILES, TW),
            one(ANG, 2, TILES, TW),
            pltpu.VMEM((TILES * YB, 3 * WIDE), BF16),
            pltpu.VMEM((TILES * YB, 3 * WIDE), BF16),
            one(TILES * YB, WIDE),
            one(TILES * YB, WIDE),
            pltpu.VMEM((4, 2, YB, H), BF16),
            dma(4, 2),
        ],
    )(
        every, bases, cosines, sines, jnp.asarray(turn_table(1)), jnp.asarray(right_table(inverse)),
        probe, gathered, info_all, psi_new,
    )
    return psi_new.reshape(2, 1, ROWS, TW), probe_new, image


def solution(mesh):
    in_specs = (
        P(None, "angle", None, "tile"),
        P(None, "angle", None, "tile"),
        P(),
        P("angle", "tile", None, None, None),
        P("angle", "tile", None),
        P("angle", "tile", None),
        P("angle", "tile"),
        P("angle"),
    )
    out_specs = (P(None, "angle", None, "tile"), P(), P(None, "tile", "angle", None))
    return jax.shard_map(shards, mesh=mesh, in_specs=in_specs, out_specs=out_specs, check_vma=False)
```
